128 devices in a mesh: frame: 32 (over x, y, core), head: 4 (over z).
Axes of the slice: x: 4, y: 4, z: 4, core: 2. Of those that a mesh axis runs over, the one named last changes fastest.
Arguments:
- query_raw: bfloat16 [4096, 2560], P('frame', 'head'), may hold values from -20 to 20
- key_raw: bfloat16 [4096, 2560], P('frame', 'head'), may hold values from -20 to 20
- values: bfloat16 [4096, 2560], P('frame', 'head'), may hold values from -6 to 6
- query_gain: float32 [2560], P('head'), may hold values from 0.5 to 2
- key_gain: float32 [2560], P('head'), may hold values from 0.5 to 2
- out_grad: bfloat16 [4096, 2560], P('frame', 'head'), may hold values from -128 to 128
- window_offset: int32 [7], replicated, may hold values from 0 to 3
Outputs:
- query_raw_grad: bfloat16 [4096, 2560], P('frame', 'head')
- key_raw_grad: bfloat16 [4096, 2560], P('frame', 'head')
- value_grad: bfloat16 [4096, 2560], P('frame', 'head')
The draws below stay inside these ranges and needn't reach their ends.
All inputs are finite; a program needn't handle non-finite values.
Results may differ from the reference program's by a relative error of at most 0.0065.
The reference program's roundings to bfloat16 on the way (of `queries`, `keys`, `probs_half` and `grad_half`) count: a program that leaves them out, or rounds other values in their place, can miss the bound.
Values may be sent and summed in bfloat16 or wider, within the bound.
A program may use at most 64 MiB of HBM per device.

```python
import math
import jax
import jax.numpy as jnp
from jax import lax

HEADS = 20
HD = 128
NB = 4
BANDS = 7
TOK_FRAME = 128
FRAMES = 32
BLK = 32
TOKENS = 4096
FEAT = 2560


def head_factor(stream):
    factor = jnp.exp(jax.random.uniform(stream, (TOKENS, HEADS), minval=math.log(0.5), maxval=math.log(2.0)))
    return jnp.repeat(factor, HD, axis=1)


def raw_pair(key):
    base = jax.random.fold_in(key, 17)
    streams = jax.random.split(base, 11)
    row_query = jnp.exp(jax.random.uniform(streams[0], (TOKENS, 1), minval=math.log(0.3), maxval=math.log(3.0)))
    row_key = jnp.exp(jax.random.uniform(streams[1], (TOKENS, 1), minval=math.log(0.3), maxval=math.log(3.0)))
    col_query = jnp.exp(jax.random.uniform(streams[2], (FEAT,), minval=math.log(0.1), maxval=math.log(0.8)))
    col_key = jnp.exp(jax.random.uniform(streams[3], (FEAT,), minval=math.log(0.1), maxval=math.log(0.8)))
    key_heads = head_factor(streams[10])
    query_all = row_query * col_query * jax.random.truncated_normal(streams[5], -4.0, 4.0, (TOKENS, FEAT))
    key_all = row_key * col_key * key_heads * jax.random.truncated_normal(streams[6], -4.0, 4.0, (TOKENS, FEAT))
    return (query_all, key_all)


def draw_query_raw(key, part):
    return raw_pair(key)[0].astype(jnp.bfloat16)


def draw_key_raw(key, part):
    return raw_pair(key)[1].astype(jnp.bfloat16)


def draw_query_gain(key, part):
    base = jax.random.fold_in(key, 31)
    gain = jax.random.uniform(base, (FEAT,), minval=1.5, maxval=2.0)
    return gain


def draw_key_gain(key, part):
    base = jax.random.fold_in(key, 37)
    gain = jax.random.uniform(base, (FEAT,), minval=1.5, maxval=2.0)
    return gain


def draw_out_grad(key, part):
    base = jax.random.fold_in(key, 29)
    gradient = jax.random.truncated_normal(base, -4.0, 4.0, (TOKENS, FEAT)) * 32.0
    return gradient.astype(jnp.bfloat16)


def touch_ends(entries, key, least, high):
    longest = entries.shape.index(max(entries.shape))
    spots = []
    for shift in (0, 1):
        where = [jax.random.randint(jax.random.fold_in(key, axis), (), 0, length) for axis, length in enumerate(entries.shape)]
        where[longest] = (where[longest] + shift) % entries.shape[longest]
        spots.append(tuple(where))
    return entries.at[spots[0]].set(least).at[spots[1]].set(high)


def steps_of(rng, shape, pieces, smallest, largest):
    def one(axis_at, blocks):
        heights = jax.random.uniform(jax.random.fold_in(jax.random.fold_in(rng, 6), axis_at), (blocks,), jnp.float32, smallest / len(pieces), largest / len(pieces))
        return jnp.repeat(jnp.exp(heights), shape[axis_at] // blocks).reshape((-1,) + (1,) * (len(shape) - axis_at - 1))

    level = one(*pieces[0])
    for cut in pieces[1:]:
        level = level * one(*cut)
    return level


def noise(rng, shape, spread, reach, cuts=(), held_as=jnp.bfloat16):
    drawn = spread * jax.random.normal(rng, shape, jnp.float32)
    if cuts:
        drawn = drawn * steps_of(rng, shape, cuts, -0.22, 0.18)
    return jnp.clip(drawn, -reach, reach).astype(held_as)


def setup_inputs(seed: int = 0) -> dict:
    key_of = jax.random.split(jax.random.key(seed), 8)
    query_raw = draw_query_raw(jax.random.fold_in(key_of[7], 71), 0)
    key_raw = draw_key_raw(jax.random.fold_in(key_of[7], 71), 0)
    values = noise(key_of[2], (TOKENS, FEAT), 1.0, 6.0, ((0, 32), (1, 4)))
    query_gain = draw_query_gain(jax.random.fold_in(key_of[7], 71), 0)
    key_gain = draw_key_gain(jax.random.fold_in(key_of[7], 71), 0)
    out_grad = draw_out_grad(jax.random.fold_in(key_of[7], 71), 0)
    window_offset = touch_ends(jax.random.randint(key_of[6], (BANDS,), 0, NB), jax.random.fold_in(key_of[6], 1), 0, NB - 1).astype(jnp.int32)
    return dict(query_raw=query_raw, key_raw=key_raw, values=values, query_gain=query_gain, key_gain=key_gain, out_grad=out_grad, window_offset=window_offset)


EPSILON = 1e-06
MASKED_SCORE = -1e+30

def window_mask(query_rows, key_rows, window_offset):
    query_frame = query_rows // TOK_FRAME
    key_frame = key_rows // TOK_FRAME
    query_block = query_rows % TOK_FRAME // BLK
    key_block = key_rows % TOK_FRAME // BLK
    distance = jnp.abs(query_frame[:, None] - key_frame[None, :])
    band_level = jnp.zeros(distance.shape, jnp.int32)
    for exponent in range(1, BANDS + 1):
        band_level = band_level + (distance >= 2 ** exponent).astype(jnp.int32)
    offset = jnp.zeros(distance.shape, jnp.int32)
    for band_index in range(BANDS):
        offset = offset + jnp.where(band_level == band_index + 1, window_offset[band_index], 0).astype(jnp.int32)
    window_width = jnp.maximum(1, jnp.right_shift(jnp.int32(NB), band_level))
    relative = (key_block[None, :] - query_block[:, None] - offset) % NB
    return (band_level == 0) | (relative < window_width)

def normalize(raw_rows, gain):
    raw_float = raw_rows.astype(jnp.float32)
    square_sum = lax.optimization_barrier(jnp.sum(raw_float * raw_float, axis=-1, keepdims=True))
    inverse_rms = lax.rsqrt(square_sum / (HEADS * HD) + EPSILON)
    return ((raw_float * inverse_rms * gain).astype(jnp.bfloat16), inverse_rms)

def norm_backward(raw_rows, gain, inverse_rms, gradient):
    raw_float = raw_rows.astype(jnp.float32)
    gained = gain * gradient
    inner_sum = lax.optimization_barrier(jnp.sum(gained * raw_float, axis=-1, keepdims=True))
    cubed = inverse_rms * inverse_rms * inverse_rms
    return (inverse_rms * gained - cubed / (HEADS * HD) * raw_float * inner_sum).astype(jnp.bfloat16)

def reference(query_raw, key_raw, values, query_gain, key_gain, out_grad, window_offset):
    score_scale = HD ** (-0.5)
    queries, query_rms = normalize(query_raw, query_gain)
    keys, key_rms = normalize(key_raw, key_gain)
    key_heads = keys.reshape(TOKENS, HEADS, HD).astype(jnp.float32)
    value_heads = values.reshape(TOKENS, HEADS, HD).astype(jnp.float32)
    query_heads = queries.reshape(FRAMES, TOK_FRAME, HEADS, HD)
    grad_heads = out_grad.reshape(FRAMES, TOK_FRAME, HEADS, HD)
    key_rows = jnp.arange(TOKENS, dtype=jnp.int32)

    def frame_step(running, frame_index):
        key_acc, value_acc = running
        query_block = query_heads[frame_index].astype(jnp.float32)
        grad_block = grad_heads[frame_index].astype(jnp.float32)
        query_rows = frame_index * TOK_FRAME + jnp.arange(TOK_FRAME, dtype=jnp.int32)
        allowed = window_mask(query_rows, key_rows, window_offset)[None]
        scores = jnp.einsum('qhd,khd->hqk', query_block, key_heads) * score_scale
        row_peak = lax.optimization_barrier(jnp.max(jnp.where(allowed, scores, MASKED_SCORE), axis=-1, keepdims=True))
        row_total = lax.optimization_barrier(jnp.sum(jnp.where(allowed, jnp.exp(scores - row_peak), 0.0), axis=-1, keepdims=True))
        log_total = row_peak + jnp.log(row_total)
        probs = jnp.where(allowed, jnp.exp(scores - log_total), 0.0)
        grad_probs = jnp.einsum('qhd,khd->hqk', grad_block, value_heads)
        delta = lax.optimization_barrier(jnp.sum(probs * grad_probs, axis=-1, keepdims=True))
        grad_scores = probs * (grad_probs - delta)
        query_grad = jnp.einsum('hqk,khd->qhd', grad_scores, key_heads, precision=lax.Precision.HIGHEST) * score_scale
        probs_half = lax.optimization_barrier(probs.astype(jnp.bfloat16)).astype(jnp.float32)
        grad_half = lax.optimization_barrier(grad_scores.astype(jnp.bfloat16)).astype(jnp.float32)
        value_acc = value_acc + jnp.einsum('hqk,qhd->khd', probs_half, grad_block)
        key_acc = key_acc + jnp.einsum('hqk,qhd->khd', grad_half, query_block)
        return ((key_acc, value_acc), query_grad)
    zero_heads = jnp.zeros((TOKENS, HEADS, HD), jnp.float32)
    (key_acc, value_acc), query_grads = lax.scan(frame_step, (zero_heads, zero_heads), jnp.arange(FRAMES, dtype=jnp.int32))
    query_grad = query_grads.reshape(TOKENS, FEAT)
    key_grad = key_acc.reshape(TOKENS, FEAT) * score_scale
    value_grad = value_acc.reshape(TOKENS, FEAT).astype(jnp.bfloat16)
    query_raw_grad = norm_backward(query_raw, query_gain, query_rms, query_grad)
    key_raw_grad = norm_backward(key_raw, key_gain, key_rms, key_grad)
    return (query_raw_grad, key_raw_grad, value_grad)
```

```python
import functools
import math

import jax
import jax.numpy as jnp
import numpy as np
from jax import lax
from jax.experimental import pallas as pl
from jax.experimental.pallas import tpu as pltpu
from jax.sharding import PartitionSpec as P

HEADS = 20
HD = 128
NB = 4
TOK = 128
BLK = 32
FRAMES = 32
FEAT = HEADS * HD
LOCAL_HEADS = 5
LOCAL = LOCAL_HEADS * HD
TILES = 8
EPSILON = 1e-06
NEG = -1e30
SCALE = HD ** (-0.5)
SCALE2 = SCALE * math.log2(math.e)
MESH = pl.DeviceIdType.MESH
VMEM_LIMIT = 60 * 1024 * 1024

UNITS = LOCAL_HEADS * NB


def unit_device(head, block):
    return 2 * ((3 * (2 * head + block // 2)) % 16) + block % 2


def my_unit():
    me = lax.axis_index("frame")
    slot = lax.rem(11 * (me // 2), 16)
    return me, slot < 2 * LOCAL_HEADS, slot // 2, 2 * lax.rem(slot, 2) + lax.rem(me, 2)


def block_table():
    rows, starts = [], [0]
    for tile in range(TILES):
        for frame in range(max(0, 4 * tile - 4), min(FRAMES, 4 * tile + 8)):
            rows.append((frame, frame - 4 * tile + 4))
        for other in range(TILES):
            apart = other - tile
            if abs(apart) < 2:
                continue
            near = {2: (2, 3), 3: (3,), 4: (3, 4)}.get(abs(apart), (4,))
            for level in near:
                if len(near) == 1:
                    kind = 12
                else:
                    kind = 13 + {-4: 0, -2: 1, 2: 2, 4: 3}[apart] * 2 + (level - near[0])
                rows.append((32 + (level - 2) * 8 + other, kind))
        starts.append(len(rows))
    return np.array(rows, np.int32), np.array(starts, np.int32)


KIND_FAR = [(-4, 3), (-4, 4), (-2, 2), (-2, 3), (2, 2), (2, 3), (4, 3), (4, 4)]
KINDS = 13 + len(KIND_FAR)
MOST_BLOCKS = 20


def enter(barrier_head=True):
    barrier = pltpu.get_barrier_semaphore()
    me = lax.axis_index("frame")
    row = lax.axis_index("head")
    for step in range(1, FRAMES):
        pl.semaphore_signal(
            barrier, inc=1, device_id={"frame": lax.rem(me + step, FRAMES)}, device_id_type=MESH
        )
    for step in range(1, 4):
        pl.semaphore_signal(
            barrier, inc=1, device_id={"head": lax.rem(row + step, 4)}, device_id_type=MESH
        )
    pl.semaphore_wait(barrier, FRAMES - 1 + 3)


def pair_rows(first, second):
    lane = lax.broadcasted_iota(jnp.int32, (TOK, TOK), 1)
    both = jnp.where(lane == 0, first, jnp.where(lane == 1, second, 0.0))
    return both.T[:8]


def pair_columns(rows):
    full = jnp.concatenate([rows, jnp.zeros((TOK - 8, TOK), jnp.float32)], axis=0).T
    return full[:, 0:1], full[:, 1:2]


def head_sum(stat, slots, send_sem, recv_sem):
    row = lax.axis_index("head")
    copies = []
    for step in range(1, 4):
        copy = pltpu.make_async_remote_copy(
            src_ref=stat,
            dst_ref=slots.at[step - 1],
            send_sem=send_sem.at[step - 1],
            recv_sem=recv_sem.at[step - 1],
            device_id={"head": lax.rem(row + step, 4)},
            device_id_type=MESH,
        )
        copy.start()
        copies.append(copy)
    return copies


def head_slice(head):
    return pl.ds(head * HD, HD)


def send_kernel(
    q_ref, k_ref, v_ref, g_ref, qgain_ref, kgain_ref,
    k_all, v_all, q_all, g_all, total_ref,
    keys, queries, stat, slots,
    zsend, zrecv, vsend, gsend, ksend, qsend, vrecv, grecv, krecv, qrecv,
):
    me, is_unit, _, _ = my_unit()
    enter()

    def send(src, dst_all, target, send_sem, recv_sem):
        @pl.when(me != target)
        def _():
            pltpu.make_async_remote_copy(
                src_ref=src, dst_ref=dst_all.at[me], send_sem=send_sem, recv_sem=recv_sem.at[me],
                device_id={"frame": target}, device_id_type=MESH,
            ).start()

        @pl.when(me == target)
        def _():
            pltpu.make_async_copy(src, dst_all.at[me], recv_sem.at[me]).start()

    for head in range(LOCAL_HEADS):
        for block in range(NB):
            unit = head * NB + block
            target = unit_device(head, block)
            send(v_ref.at[:, head_slice(head)], v_all, target, vsend.at[unit], vrecv)
            send(g_ref.at[pl.ds(block * BLK, BLK), head_slice(head)], g_all, target, gsend.at[unit], grecv)

    def squares(ref):
        acc = jnp.zeros((TOK, HD), jnp.float32)
        for head in range(LOCAL_HEADS):
            part = ref[:, head_slice(head)].astype(jnp.float32)
            acc = acc + part * part
        return jnp.sum(acc, axis=1, keepdims=True)

    stat[...] = pair_rows(squares(q_ref), squares(k_ref))
    for copy in head_sum(stat, slots, zsend, zrecv):
        copy.wait()
    total = stat[...] + slots[0] + slots[1] + slots[2]
    total_ref[...] = total
    qsum, ksum = pair_columns(total)
    qrms = lax.rsqrt(qsum / FEAT + EPSILON)
    krms = lax.rsqrt(ksum / FEAT + EPSILON)
    for head in range(LOCAL_HEADS):
        part = k_ref[:, head_slice(head)].astype(jnp.float32)
        keys[head] = (part * krms * kgain_ref[:, head_slice(head)]).astype(jnp.bfloat16)
        part = q_ref[:, head_slice(head)].astype(jnp.float32)
        queries[head] = (part * qrms * qgain_ref[:, head_slice(head)]).astype(jnp.bfloat16)
        for block in range(NB):
            unit = head * NB + block
            target = unit_device(head, block)
            send(keys.at[head], k_all, target, ksend.at[unit], krecv)
            send(queries.at[head, pl.ds(block * BLK, BLK)], q_all, target, qsend.at[unit], qrecv)

    @pl.when(is_unit)
    def _():
        @pl.loop(0, FRAMES)
        def _(frame):
            for ref, sem in ((v_all, vrecv), (g_all, grecv), (k_all, krecv), (q_all, qrecv)):
                pltpu.make_async_copy(ref.at[frame], ref.at[frame], sem.at[frame]).wait()

    for head in range(LOCAL_HEADS):
        for block in range(NB):
            unit = head * NB + block
            target = unit_device(head, block)

            @pl.when(me != target)
            def _():
                rows = pl.ds(block * BLK, BLK)
                for src, dst, ssem, rsem in (
                    (v_ref.at[:, head_slice(head)], v_all, vsend, vrecv),
                    (g_ref.at[rows, head_slice(head)], g_all, gsend, grecv),
                    (keys.at[head], k_all, ksend, krecv),
                    (queries.at[head, rows], q_all, qsend, qrecv),
                ):
                    pltpu.make_async_remote_copy(
                        src_ref=src, dst_ref=dst.at[me], send_sem=ssem.at[unit], recv_sem=rsem.at[me],
                        device_id={"frame": target}, device_id_type=MESH,
                    ).wait_send()


def dot(a, b, contract):
    return lax.dot_general(a, b, (contract, ((), ())), preferred_element_type=jnp.float32)


def unit_kernel(
    offset_ref, table_ref, start_ref,
    k_all, v_all, q_all, g_all,
    dkv_all, dq_all,
    kv, kt, w, acc, bias, tbuf, gbuf, dqt,
):
    _, is_unit, _, block = my_unit()

    @pl.when(is_unit)
    def _():
        row_frame = lax.broadcasted_iota(jnp.int32, (TOK, TOK), 0) // BLK
        lane_frame = lax.broadcasted_iota(jnp.int32, (TOK, TOK), 1) // BLK
        zero = jnp.zeros((TOK, TOK), jnp.float32)
        hit1 = jnp.where(((row_frame - block - offset_ref[0]) & 3) < 2, 0.0, NEG)
        hit2 = jnp.where(((row_frame - block - offset_ref[1]) & 3) < 1, 0.0, NEG)

        @pl.loop(0, 12)
        def _(kind):
            d = jnp.abs(kind - 4 - lane_frame)
            bias[kind] = jnp.where(d < 2, 0.0, jnp.where(d < 4, hit1, hit2))

        bias[12] = zero
        for index, (apart, level) in enumerate(KIND_FAR):
            d = jnp.abs(4 * apart + row_frame - lane_frame)
            bias[13 + index] = jnp.where((d >= 2**level) & (d < 2 ** (level + 1)), 0.0, NEG)

        picks = [
            pl.multiple_of(((block + offset_ref[level - 1]) & 3) * BLK, BLK) for level in (2, 3, 4)
        ]

        @pl.loop(0, FRAMES)
        def _(frame):
            kv[pl.ds(pl.multiple_of(frame * TOK, TOK), TOK), 0:HD] = k_all[frame]
            kv[pl.ds(pl.multiple_of(frame * TOK, TOK), TOK), HD : 2 * HD] = v_all[frame]
            for index, pick in enumerate(picks):
                where = pl.multiple_of((FRAMES * NB + index * FRAMES + frame) * BLK, BLK)
                kv[pl.ds(where, BLK), 0:HD] = k_all[frame, pl.ds(pick, BLK)]
                kv[pl.ds(where, BLK), HD : 2 * HD] = v_all[frame, pl.ds(pick, BLK)]

        @pl.loop(0, 56)
        def _(blk):
            at = pl.ds(pl.multiple_of(blk * TOK, TOK), TOK)
            kt[blk] = kv[at, 0:HD].T
            acc[at, :] = jnp.zeros((TOK, 2 * HD), jnp.float32)

        @pl.loop(0, TILES)
        def _(tile):
            w[tile, 0:TOK, HD:] = jnp.zeros((TOK, HD), jnp.bfloat16)
            w[tile, TOK:, 0:HD] = jnp.zeros((TOK, HD), jnp.bfloat16)
            for part in range(4):
                w[tile, part * BLK : (part + 1) * BLK, 0:HD] = q_all[4 * tile + part]
                w[tile, TOK + part * BLK : TOK + (part + 1) * BLK, HD:] = g_all[4 * tile + part]

        @pl.loop(0, TILES)
        def _(tile):
            first = start_ref[tile]
            count = start_ref[tile + 1] - first

            def scores(slot, peak):
                blk, kind = table_ref[first + slot, 0], table_ref[first + slot, 1]
                at = pl.ds(pl.multiple_of(blk * TOK, TOK), TOK)
                both = dot(kv[at, :], w[tile], ((1,), (1,)))
                t = both[:, 0:TOK] * SCALE2 + bias[kind]
                tbuf[slot] = t
                gbuf[slot] = both[:, TOK:]
                return jnp.maximum(peak, jnp.max(t.reshape(16, 8, TOK), axis=0))

            peak = lax.fori_loop(0, count, scores, jnp.full((8, TOK), NEG, jnp.float32))
            peak = jnp.max(peak, axis=0, keepdims=True)

            def weigh(slot, sums):
                weight = jnp.exp2(tbuf[slot] - peak)
                tbuf[slot] = weight
                return (
                    sums[0] + jnp.sum(weight.reshape(16, 8, TOK), axis=0),
                    sums[1] + jnp.sum((weight * gbuf[slot]).reshape(16, 8, TOK), axis=0),
                )

            blank = jnp.zeros((8, TOK), jnp.float32)
            total, weighted = lax.fori_loop(0, count, weigh, (blank, blank))
            total = jnp.sum(total, axis=0, keepdims=True)
            inverse = 1.0 / total
            delta = jnp.sum(weighted, axis=0, keepdims=True) * inverse
            dqt[...] = jnp.zeros((HD, 2 * TOK), jnp.float32)

            @pl.loop(0, count)
            def _(slot):
                blk = table_ref[first + slot, 0]
                at = pl.ds(pl.multiple_of(blk * TOK, TOK), TOK)
                probs = tbuf[slot] * inverse
                grad = probs * (gbuf[slot] - delta)
                high = grad.astype(jnp.bfloat16)
                low = (grad - high.astype(jnp.float32)).astype(jnp.bfloat16)
                left = jnp.concatenate([high, probs.astype(jnp.bfloat16)], axis=1)
                acc[at, :] += dot(left, w[tile], ((1,), (0,)))
                dqt[...] += dot(kt[blk], jnp.concatenate([high, low], axis=1), ((1,), (0,)))

            dq = (dqt[:, 0:TOK] + dqt[:, TOK:]).T
            for part in range(4):
                dq_all[4 * tile + part] = dq[part * BLK : (part + 1) * BLK]

        @pl.loop(0, FRAMES)
        def _(frame):
            for index, pick in enumerate(picks):
                home = pl.ds(pl.multiple_of(frame * TOK + pick, BLK), BLK)
                where = pl.multiple_of((FRAMES * NB + index * FRAMES + frame) * BLK, BLK)
                acc[home, :] += acc[pl.ds(where, BLK), :]
            dkv_all[frame] = acc[pl.ds(pl.multiple_of(frame * TOK, TOK), TOK), :].astype(jnp.bfloat16)


def home_kernel(
    q_ref, k_ref, qgain_ref, kgain_ref, total_ref, dkv_all, dq_all,
    dq_out, dk_out, dv_out,
    dkv_in, dq_in, kgrad, stat, slots,
    zsend, zrecv, kvsend, qsend, kvrecv, qrecv,
):
    me, is_unit, head, block = my_unit()
    enter()
    unit = head * NB + block

    def copies(frame):
        return (
            pltpu.make_async_remote_copy(
                src_ref=dq_all.at[frame], dst_ref=dq_in.at[unit], send_sem=qsend.at[frame],
                recv_sem=qrecv.at[unit], device_id={"frame": frame}, device_id_type=MESH,
            ),
            pltpu.make_async_remote_copy(
                src_ref=dkv_all.at[frame], dst_ref=dkv_in.at[unit], send_sem=kvsend.at[frame],
                recv_sem=kvrecv.at[unit], device_id={"frame": frame}, device_id_type=MESH,
            ),
        )

    @pl.when(is_unit)
    def _():
        pltpu.make_async_copy(dq_all.at[me], dq_in.at[unit], qrecv.at[unit]).start()
        pltpu.make_async_copy(dkv_all.at[me], dkv_in.at[unit], kvrecv.at[unit]).start()

        @pl.loop(1, FRAMES)
        def _(step):
            for copy in copies(lax.rem(me + step, FRAMES)):
                copy.start()

    qsum, ksum = pair_columns(total_ref[...])
    qrms = lax.rsqrt(qsum / FEAT + EPSILON)
    krms = lax.rsqrt(ksum / FEAT + EPSILON)
    qinner = jnp.zeros((TOK, HD), jnp.float32)
    kinner = jnp.zeros((TOK, HD), jnp.float32)
    for h in range(LOCAL_HEADS):
        for b in range(NB):
            u = h * NB + b
            pltpu.make_async_copy(dq_in.at[u], dq_in.at[u], qrecv.at[u]).wait()
            pltpu.make_async_copy(dkv_in.at[u], dkv_in.at[u], kvrecv.at[u]).wait()
        gained = qgain_ref[:, head_slice(h)] * (dq_in[pl.ds(h * NB, NB)].reshape(TOK, HD) * SCALE)
        qinner = qinner + gained * q_ref[:, head_slice(h)].astype(jnp.float32)
        both = dkv_in[h * NB].astype(jnp.float32)
        for b in range(1, NB):
            both = both + dkv_in[h * NB + b].astype(jnp.float32)
        dv_out[:, head_slice(h)] = both[:, HD:].astype(jnp.bfloat16)
        gained = kgain_ref[:, head_slice(h)] * (both[:, 0:HD] * SCALE)
        kgrad[:, head_slice(h)] = gained
        kinner = kinner + gained * k_ref[:, head_slice(h)].astype(jnp.float32)
    stat[...] = pair_rows(
        jnp.sum(qinner, axis=1, keepdims=True), jnp.sum(kinner, axis=1, keepdims=True)
    )
    for copy in head_sum(stat, slots, zsend, zrecv):
        copy.wait()
    qdot, kdot = pair_columns(stat[...] + slots[0] + slots[1] + slots[2])
    qfactor = qrms * qrms * qrms / FEAT * qdot
    kfactor = krms * krms * krms / FEAT * kdot
    for h in range(LOCAL_HEADS):
        gained = qgain_ref[:, head_slice(h)] * (dq_in[pl.ds(h * NB, NB)].reshape(TOK, HD) * SCALE)
        raw = q_ref[:, head_slice(h)].astype(jnp.float32)
        dq_out[:, head_slice(h)] = (qrms * gained - qfactor * raw).astype(jnp.bfloat16)
        raw = k_ref[:, head_slice(h)].astype(jnp.float32)
        dk_out[:, head_slice(h)] = (krms * kgrad[:, head_slice(h)] - kfactor * raw).astype(jnp.bfloat16)

    @pl.when(is_unit)
    def _():
        @pl.loop(1, FRAMES)
        def _(step):
            for copy in copies(lax.rem(me + step, FRAMES)):
                copy.wait_send()


def local(query_raw, key_raw, values, query_gain, key_gain, out_grad, window_offset):
    bf16, f32 = jnp.bfloat16, jnp.float32
    vmem = pl.BlockSpec(memory_space=pltpu.VMEM)
    hbm = pl.BlockSpec(memory_space=pl.ANY)
    smem = pl.BlockSpec(memory_space=pltpu.SMEM)
    dma = pltpu.SemaphoreType.DMA
    qgain = query_gain.reshape(1, LOCAL)
    kgain = key_gain.reshape(1, LOCAL)
    shape = jax.ShapeDtypeStruct
    k_all, v_all, q_all, g_all, total = pl.pallas_call(
        send_kernel,
        name="to_units",
        out_shape=(
            shape((FRAMES, TOK, HD), bf16),
            shape((FRAMES, TOK, HD), bf16),
            shape((FRAMES, BLK, HD), bf16),
            shape((FRAMES, BLK, HD), bf16),
            shape((8, TOK), f32),
        ),
        in_specs=[vmem] * 6,
        out_specs=[hbm] * 4 + [vmem],
        scratch_shapes=[
            pltpu.VMEM((LOCAL_HEADS, TOK, HD), bf16),
            pltpu.VMEM((LOCAL_HEADS, TOK, HD), bf16),
            pltpu.VMEM((8, TOK), f32),
            pltpu.VMEM((3, 8, TOK), f32),
            dma((3,)), dma((3,)),
            dma((UNITS,)), dma((UNITS,)), dma((UNITS,)), dma((UNITS,)),
            dma((FRAMES,)), dma((FRAMES,)), dma((FRAMES,)), dma((FRAMES,)),
        ],
        compiler_params=pltpu.CompilerParams(
            collective_id=0, has_side_effects=True, vmem_limit_bytes=VMEM_LIMIT
        ),
    )(query_raw, key_raw, values, out_grad, qgain, kgain)
    table, starts = block_table()
    dkv_all, dq_all = pl.pallas_call(
        unit_kernel,
        name="unit_grads",
        out_shape=(shape((FRAMES, TOK, 2 * HD), bf16), shape((FRAMES, BLK, HD), f32)),
        in_specs=[smem] * 3 + [vmem] * 4,
        out_specs=[vmem] * 2,
        scratch_shapes=[
            pltpu.VMEM((56 * TOK, 2 * HD), bf16),
            pltpu.VMEM((56, HD, TOK), bf16),
            pltpu.VMEM((TILES, 2 * TOK, 2 * HD), bf16),
            pltpu.VMEM((56 * TOK, 2 * HD), f32),
            pltpu.VMEM((KINDS, TOK, TOK), f32),
            pltpu.VMEM((MOST_BLOCKS, TOK, TOK), f32),
            pltpu.VMEM((MOST_BLOCKS, TOK, TOK), f32),
            pltpu.VMEM((HD, 2 * TOK), f32),
        ],
        compiler_params=pltpu.CompilerParams(vmem_limit_bytes=VMEM_LIMIT),
    )(window_offset, jnp.asarray(table), jnp.asarray(starts), k_all, v_all, q_all, g_all)
    return pl.pallas_call(
        home_kernel,
        name="to_homes",
        out_shape=(shape((TOK, LOCAL), bf16),) * 3,
        in_specs=[vmem] * 5 + [hbm] * 2,
        out_specs=[vmem] * 3,
        scratch_shapes=[
            pltpu.VMEM((UNITS, TOK, 2 * HD), bf16),
            pltpu.VMEM((UNITS, BLK, HD), f32),
            pltpu.VMEM((TOK, LOCAL), f32),
            pltpu.VMEM((8, TOK), f32),
            pltpu.VMEM((3, 8, TOK), f32),
            dma((3,)), dma((3,)),
            dma((FRAMES,)), dma((FRAMES,)), dma((UNITS,)), dma((UNITS,)),
        ],
        compiler_params=pltpu.CompilerParams(
            collective_id=1, has_side_effects=True, vmem_limit_bytes=VMEM_LIMIT
        ),
    )(query_raw, key_raw, qgain, kgain, total, dkv_all, dq_all)


def solution(mesh):
    placed = (
        P("frame", "head"),
        P("frame", "head"),
        P("frame", "head"),
        P("head"),
        P("head"),
        P("frame", "head"),
        P(),
    )
    return jax.shard_map(
        local,
        mesh=mesh,
        in_specs=placed,
        out_specs=(P("frame", "head"), P("frame", "head"), P("frame", "head")),
        check_vma=False,
    )
```

```python
import functools
import math

import jax
import jax.numpy as jnp
import numpy as np
from jax import lax
from jax.experimental import pallas as pl
from jax.experimental.pallas import tpu as pltpu
from jax.sharding import PartitionSpec as P

HEADS = 20
HD = 128
NB = 4
TOK = 128
BLK = 32
FRAMES = 32
FEAT = HEADS * HD
LOCAL_HEADS = 5
LOCAL = LOCAL_HEADS * HD
TILES = 8
EPSILON = 1e-06
NEG = -1e30
SCALE = HD ** (-0.5)
SCALE2 = SCALE * math.log2(math.e)
MESH = pl.DeviceIdType.MESH
VMEM_LIMIT = 60 * 1024 * 1024

UNITS = LOCAL_HEADS * NB


def my_unit():
    me = lax.axis_index("frame")
    slot = lax.rem(11 * (me // 2), 16)
    return me, slot < 2 * LOCAL_HEADS, slot // 2, 2 * lax.rem(slot, 2) + lax.rem(me, 2)


def block_table():
    rows = []
    for tile in range(TILES):
        for frame in range(max(0, 4 * tile - 4), min(FRAMES, 4 * tile + 8)):
            rows.append((frame, frame - 4 * tile + 4))
        for other in range(TILES):
            apart = other - tile
            if abs(apart) < 2:
                continue
            near = {2: (2, 3), 3: (3,), 4: (3, 4)}.get(abs(apart), (4,))
            for level in near:
                if len(near) == 1:
                    kind = 12
                else:
                    kind = 13 + {-4: 0, -2: 1, 2: 2, 4: 3}[apart] * 2 + (level - near[0])
                rows.append((32 + (level - 2) * 8 + other, kind))
        while len(rows) < (tile + 1) * MOST_BLOCKS:
            rows.append((4 * tile, KINDS - 1))
    return np.array(rows, np.int32)


KIND_FAR = [(-4, 3), (-4, 4), (-2, 2), (-2, 3), (2, 2), (2, 3), (4, 3), (4, 4)]
KINDS = 14 + len(KIND_FAR)
MOST_BLOCKS = 20
GROUP = 4


def enter(barrier_head=True):
    barrier = pltpu.get_barrier_semaphore()
    me = lax.axis_index("frame")
    row = lax.axis_index("head")
    for step in range(1, FRAMES):
        pl.semaphore_signal(
            barrier, inc=1, device_id={"frame": lax.rem(me + step, FRAMES)}, device_id_type=MESH
        )
    for step in range(1, 4):
        pl.semaphore_signal(
            barrier, inc=1, device_id={"head": lax.rem(row + step, 4)}, device_id_type=MESH
        )
    pl.semaphore_wait(barrier, FRAMES - 1 + 3)


def pair_rows(first, second):
    lane = lax.broadcasted_iota(jnp.int32, (TOK, TOK), 1)
    both = jnp.where(lane == 0, first, jnp.where(lane == 1, second, 0.0))
    return both.T[:8]


def pair_columns(rows):
    full = jnp.concatenate([rows, jnp.zeros((TOK - 8, TOK), jnp.float32)], axis=0).T
    return full[:, 0:1], full[:, 1:2]


def head_sum(stat, slots, send_sem, recv_sem):
    row = lax.axis_index("head")
    copies = []
    for step in range(1, 4):
        copy = pltpu.make_async_remote_copy(
            src_ref=stat,
            dst_ref=slots.at[step - 1],
            send_sem=send_sem.at[step - 1],
            recv_sem=recv_sem.at[step - 1],
            device_id={"head": lax.rem(row + step, 4)},
            device_id_type=MESH,
        )
        copy.start()
        copies.append(copy)
    return copies


def head_slice(head):
    return pl.ds(head * HD, HD)


def lanes(head):
    return pl.ds(pl.multiple_of(head * HD, HD), HD)


def send_kernel(
    q_ref, k_ref, v_ref, g_ref, qgain_ref, kgain_ref,
    k_all, v_all, q_all, g_all, total_ref,
    keys, queries, stat, slots,
    zsend, zrecv, vsend, gsend, ksend, qsend, vrecv, grecv, krecv, qrecv, vpass, kpass,
):
    me, is_unit, _, _ = my_unit()
    core = lax.rem(me, 2)
    chip = me // 2
    enter()

    def remote(src, dst_all, target, send_sem, recv_sem):
        return pltpu.make_async_remote_copy(
            src_ref=src, dst_ref=dst_all.at[me], send_sem=send_sem, recv_sem=recv_sem.at[me],
            device_id={"frame": target}, device_id_type=MESH,
        )

    def send(src, dst_all, target, send_sem, recv_sem):
        @pl.when(me != target)
        def _():
            remote(src, dst_all, target, send_sem, recv_sem).start()

        @pl.when(me == target)
        def _():
            pltpu.make_async_copy(src, dst_all.at[me], recv_sem.at[me]).start()

    def raw_parts(slot):
        head, half = slot // 2, lax.rem(slot, 2)
        base = 2 * lax.rem(3 * slot, 16)
        yield v_ref.at[:, lanes(head)], v_all, base + core, vsend.at[slot], vrecv
        for side in range(2):
            rows = pl.ds(pl.multiple_of((2 * half + side) * BLK, BLK), BLK)
            yield g_ref.at[rows, lanes(head)], g_all, base + side, gsend.at[2 * slot + side], grecv

    def normal_parts(slot):
        head, half = slot // 2, lax.rem(slot, 2)
        base = 2 * lax.rem(3 * slot, 16)
        yield keys.at[head], k_all, base + core, ksend.at[slot], krecv
        for side in range(2):
            rows = pl.ds(pl.multiple_of((2 * half + side) * BLK, BLK), BLK)
            yield queries.at[head, rows], q_all, base + side, qsend.at[2 * slot + side], qrecv

    @pl.loop(0, 2 * LOCAL_HEADS)
    def _(step):
        for part in raw_parts(lax.rem(step + chip, 2 * LOCAL_HEADS)):
            send(*part)

    def squares(ref):
        acc = jnp.zeros((TOK, HD), jnp.float32)
        for head in range(LOCAL_HEADS):
            part = ref[:, head_slice(head)].astype(jnp.float32)
            acc = acc + part * part
        return jnp.sum(acc, axis=1, keepdims=True)

    stat[...] = pair_rows(squares(q_ref), squares(k_ref))
    for copy in head_sum(stat, slots, zsend, zrecv):
        copy.wait()
    total = stat[...] + slots[0] + slots[1] + slots[2]
    total_ref[...] = total
    qsum, ksum = pair_columns(total)
    qrms = lax.rsqrt(qsum / FEAT + EPSILON)
    krms = lax.rsqrt(ksum / FEAT + EPSILON)
    for head in range(LOCAL_HEADS):
        part = k_ref[:, head_slice(head)].astype(jnp.float32)
        keys[head] = (part * krms * kgain_ref[head_slice(head)].reshape(1, HD)).astype(jnp.bfloat16)
        part = q_ref[:, head_slice(head)].astype(jnp.float32)
        queries[head] = (part * qrms * qgain_ref[head_slice(head)].reshape(1, HD)).astype(jnp.bfloat16)

    @pl.loop(0, 2 * LOCAL_HEADS)
    def _(step):
        for part in normal_parts(lax.rem(step + chip, 2 * LOCAL_HEADS)):
            send(*part)

    def forward(ref, step, send_sem, recv_sem):
        frame = lax.rem(me + 2 * step, FRAMES)
        return pltpu.make_async_remote_copy(
            src_ref=ref.at[frame], dst_ref=ref.at[frame], send_sem=send_sem.at[step],
            recv_sem=recv_sem.at[frame], device_id={"frame": me + 1 - 2 * core}, device_id_type=MESH,
        )

    def arrived(ref, frame, sem):
        pltpu.make_async_copy(ref.at[frame], ref.at[frame], sem.at[frame]).wait()

    @pl.when(is_unit)
    def _():
        for ref, ssem, rsem in ((v_all, vpass, vrecv), (k_all, kpass, krecv)):
            @pl.loop(0, FRAMES // 2)
            def _(step):
                arrived(ref, lax.rem(me + 2 * step, FRAMES), rsem)
                forward(ref, step, ssem, rsem).start()

        @pl.loop(0, FRAMES)
        def _(frame):
            arrived(g_all, frame, grecv)
            arrived(q_all, frame, qrecv)

        @pl.loop(0, FRAMES // 2)
        def _(step):
            frame = 2 * step + 1 - core
            arrived(v_all, frame, vrecv)
            arrived(k_all, frame, krecv)
            forward(v_all, step, vpass, vrecv).wait_send()
            forward(k_all, step, kpass, krecv).wait_send()

    @pl.loop(0, 2 * LOCAL_HEADS)
    def _(slot):
        for parts in (raw_parts(slot), normal_parts(slot)):
            for src, dst, target, ssem, rsem in parts:
                @pl.when(me != target)
                def _():
                    remote(src, dst, target, ssem, rsem).wait_send()


def dot(a, b, contract):
    return lax.dot_general(a, b, (contract, ((), ())), preferred_element_type=jnp.float32)


def unit_kernel(
    offset_ref, table_ref,
    k_all, v_all, q_all, g_all,
    dkv_keep, dkv_give, dq_all,
    kv, kt, w, acc, bias, tbuf, gbuf, dqt,
):
    me, is_unit, _, block = my_unit()
    core = lax.rem(me, 2)

    @pl.when(is_unit)
    def _():
        row_frame = lax.broadcasted_iota(jnp.int32, (TOK, TOK), 0) // BLK
        lane_frame = lax.broadcasted_iota(jnp.int32, (TOK, TOK), 1) // BLK
        zero = jnp.zeros((TOK, TOK), jnp.float32)
        hit1 = jnp.where(((row_frame - block - offset_ref[0]) & 3) < 2, 0.0, NEG)
        hit2 = jnp.where(((row_frame - block - offset_ref[1]) & 3) < 1, 0.0, NEG)

        @pl.loop(0, 12)
        def _(kind):
            d = jnp.abs(kind - 4 - lane_frame)
            bias[kind] = jnp.where(d < 2, 0.0, jnp.where(d < 4, hit1, hit2))

        bias[12] = zero
        bias[KINDS - 1] = zero + NEG
        for index, (apart, level) in enumerate(KIND_FAR):
            d = jnp.abs(4 * apart + row_frame - lane_frame)
            bias[13 + index] = jnp.where((d >= 2**level) & (d < 2 ** (level + 1)), 0.0, NEG)

        picks = [
            pl.multiple_of(((block + offset_ref[level - 1]) & 3) * BLK, BLK) for level in (2, 3, 4)
        ]

        @pl.loop(0, FRAMES)
        def _(frame):
            kv[pl.ds(pl.multiple_of(frame * TOK, TOK), TOK), 0:HD] = k_all[frame]
            kv[pl.ds(pl.multiple_of(frame * TOK, TOK), TOK), HD : 2 * HD] = v_all[frame]
            for index, pick in enumerate(picks):
                where = pl.multiple_of((FRAMES * NB + index * FRAMES + frame) * BLK, BLK)
                kv[pl.ds(where, BLK), 0:HD] = k_all[frame, pl.ds(pick, BLK)]
                kv[pl.ds(where, BLK), HD : 2 * HD] = v_all[frame, pl.ds(pick, BLK)]

        @pl.loop(0, 56)
        def _(blk):
            at = pl.ds(pl.multiple_of(blk * TOK, TOK), TOK)
            kt[blk] = kv[at, 0:HD].T
            acc[at, :] = jnp.zeros((TOK, 2 * HD), jnp.float32)

        @pl.loop(0, TILES)
        def _(tile):
            w[tile, 0:TOK, HD:] = jnp.zeros((TOK, HD), jnp.bfloat16)
            w[tile, TOK:, 0:HD] = jnp.zeros((TOK, HD), jnp.bfloat16)
            for part in range(4):
                w[tile, part * BLK : (part + 1) * BLK, 0:HD] = q_all[4 * tile + part]
                w[tile, TOK + part * BLK : TOK + (part + 1) * BLK, HD:] = g_all[4 * tile + part]

        @pl.loop(0, TILES)
        def _(tile):
            first = tile * MOST_BLOCKS
            blks = [table_ref[first + slot, 0] for slot in range(MOST_BLOCKS)]
            at = [pl.ds(pl.multiple_of(blk * TOK, TOK), TOK) for blk in blks]
            groups = [range(i, i + GROUP) for i in range(0, MOST_BLOCKS, GROUP)]
            peak = jnp.full((8, TOK), NEG, jnp.float32)
            for group in groups:
                rows = jnp.concatenate([kv[at[slot], :] for slot in group], axis=0)
                both = dot(rows, w[tile], ((1,), (1,)))
                for index, slot in enumerate(group):
                    part = both[index * TOK : (index + 1) * TOK]
                    t = part[:, 0:TOK] * SCALE2 + bias[table_ref[first + slot, 1]]
                    tbuf[slot] = t
                    gbuf[slot] = part[:, TOK:]
                    peak = jnp.maximum(peak, jnp.max(t.reshape(16, 8, TOK), axis=0))
            peak = jnp.max(peak, axis=0, keepdims=True)
            total = jnp.zeros((8, TOK), jnp.float32)
            weighted = jnp.zeros((8, TOK), jnp.float32)
            for slot in range(MOST_BLOCKS):
                weight = jnp.exp2(tbuf[slot] - peak)
                tbuf[slot] = weight
                total = total + jnp.sum(weight.reshape(16, 8, TOK), axis=0)
                weighted = weighted + jnp.sum((weight * gbuf[slot]).reshape(16, 8, TOK), axis=0)
            total = jnp.sum(total, axis=0, keepdims=True)
            inverse = 1.0 / total
            delta = jnp.sum(weighted, axis=0, keepdims=True) * inverse
            dqt[...] = jnp.zeros((HD, 2 * TOK), jnp.float32)
            for group in groups:
                lefts, lows, highs = [], [], []
                for slot in group:
                    probs = tbuf[slot] * inverse
                    grad = probs * (gbuf[slot] - delta)
                    high = grad.astype(jnp.bfloat16)
                    low = (grad - high.astype(jnp.float32)).astype(jnp.bfloat16)
                    lefts.append(jnp.concatenate([high, probs.astype(jnp.bfloat16)], axis=1))
                    lows.append(jnp.concatenate([high, low], axis=1))
                both = dot(jnp.concatenate(lefts, axis=0), w[tile], ((1,), (0,)))
                for index, slot in enumerate(group):
                    acc[at[slot], :] += both[index * TOK : (index + 1) * TOK]
                keyt = jnp.concatenate([kt[blks[slot]] for slot in group], axis=1)
                dqt[...] += dot(keyt, jnp.concatenate(lows, axis=0), ((1,), (0,)))

            dq = (dqt[:, 0:TOK] + dqt[:, TOK:]).T
            for part in range(4):
                dq_all[4 * tile + part] = dq[part * BLK : (part + 1) * BLK]

        def gathered(frame):
            for index, pick in enumerate(picks):
                home = pl.ds(pl.multiple_of(frame * TOK + pick, BLK), BLK)
                where = pl.multiple_of((FRAMES * NB + index * FRAMES + frame) * BLK, BLK)
                acc[home, :] += acc[pl.ds(where, BLK), :]
            return acc[pl.ds(pl.multiple_of(frame * TOK, TOK), TOK), :]

        @pl.loop(0, FRAMES // 2)
        def _(step):
            dkv_keep[step] = gathered(2 * step + core)
            dkv_give[step] = gathered(2 * step + 1 - core).astype(jnp.bfloat16)


def home_kernel(
    q_ref, k_ref, qgain_ref, kgain_ref, total_ref, dkv_keep, dkv_give, dq_all,
    dq_out, dk_out, dv_out,
    other, mixed, dkv_in, dq_in, kgrad, stat, slots,
    zsend, zrecv, give_send, give_recv, kvsend, qsend, kvrecv, qrecv,
):
    me, is_unit, head, block = my_unit()
    core = lax.rem(me, 2)
    slot = 2 * head + block // 2
    unit = head * NB + block
    enter()

    def order(step):
        x = lax.rem(me // 8 + step + 1, 4)
        y = lax.rem(me // 2 + step // 4 + step, 4)
        return x * 4 + y

    def give(step):
        return pltpu.make_async_remote_copy(
            src_ref=dkv_give.at[step], dst_ref=other.at[step], send_sem=give_send.at[step],
            recv_sem=give_recv.at[step], device_id={"frame": me + 1 - 2 * core}, device_id_type=MESH,
        )

    def send_dq(frame):
        return pltpu.make_async_remote_copy(
            src_ref=dq_all.at[frame], dst_ref=dq_in.at[unit], send_sem=qsend.at[frame],
            recv_sem=qrecv.at[unit], device_id={"frame": frame}, device_id_type=MESH,
        )

    def send_dkv(pair):
        return pltpu.make_async_remote_copy(
            src_ref=mixed.at[pair], dst_ref=dkv_in.at[slot], send_sem=kvsend.at[pair],
            recv_sem=kvrecv.at[slot], device_id={"frame": 2 * pair + core}, device_id_type=MESH,
        )

    @pl.when(is_unit)
    def _():
        @pl.loop(0, FRAMES // 2)
        def _(step):
            give(order(step)).start()

        @pl.loop(0, FRAMES)
        def _(step):
            frame = 2 * order(lax.rem(step, 16)) + lax.rem(core + step // 16, 2)

            @pl.when(frame != me)
            def _():
                send_dq(frame).start()

            @pl.when(frame == me)
            def _():
                pltpu.make_async_copy(dq_all.at[frame], dq_in.at[unit], qrecv.at[unit]).start()

        @pl.loop(0, FRAMES // 2)
        def _(step):
            pair = order(step)
            give(pair).wait_recv()
            mixed[pair] = (dkv_keep[pair] + other[pair].astype(jnp.float32)).astype(jnp.bfloat16)

            @pl.when(2 * pair + core != me)
            def _():
                send_dkv(pair).start()

            @pl.when(2 * pair + core == me)
            def _():
                pltpu.make_async_copy(mixed.at[pair], dkv_in.at[slot], kvrecv.at[slot]).start()

    qsum, ksum = pair_columns(total_ref[...])
    qrms = lax.rsqrt(qsum / FEAT + EPSILON)
    krms = lax.rsqrt(ksum / FEAT + EPSILON)
    qinner = jnp.zeros((TOK, HD), jnp.float32)
    kinner = jnp.zeros((TOK, HD), jnp.float32)
    for h in range(LOCAL_HEADS):
        for b in range(NB):
            u = h * NB + b
            pltpu.make_async_copy(dq_in.at[u], dq_in.at[u], qrecv.at[u]).wait()
        gained = qgain_ref[head_slice(h)].reshape(1, HD) * (dq_in[pl.ds(h * NB, NB)].reshape(TOK, HD) * SCALE)
        qinner = qinner + gained * q_ref[:, head_slice(h)].astype(jnp.float32)
        for u in (2 * h, 2 * h + 1):
            pltpu.make_async_copy(dkv_in.at[u], dkv_in.at[u], kvrecv.at[u]).wait()
        both = dkv_in[2 * h].astype(jnp.float32) + dkv_in[2 * h + 1].astype(jnp.float32)
        dv_out[:, head_slice(h)] = both[:, HD:].astype(jnp.bfloat16)
        gained = kgain_ref[head_slice(h)].reshape(1, HD) * (both[:, 0:HD] * SCALE)
        kgrad[:, head_slice(h)] = gained
        kinner = kinner + gained * k_ref[:, head_slice(h)].astype(jnp.float32)
    stat[...] = pair_rows(
        jnp.sum(qinner, axis=1, keepdims=True), jnp.sum(kinner, axis=1, keepdims=True)
    )
    for copy in head_sum(stat, slots, zsend, zrecv):
        copy.wait()
    qdot, kdot = pair_columns(stat[...] + slots[0] + slots[1] + slots[2])
    qfactor = qrms * qrms * qrms / FEAT * qdot
    kfactor = krms * krms * krms / FEAT * kdot
    for h in range(LOCAL_HEADS):
        gained = qgain_ref[head_slice(h)].reshape(1, HD) * (dq_in[pl.ds(h * NB, NB)].reshape(TOK, HD) * SCALE)
        raw = q_ref[:, head_slice(h)].astype(jnp.float32)
        dq_out[:, head_slice(h)] = (qrms * gained - qfactor * raw).astype(jnp.bfloat16)
        raw = k_ref[:, head_slice(h)].astype(jnp.float32)
        dk_out[:, head_slice(h)] = (krms * kgrad[:, head_slice(h)] - kfactor * raw).astype(jnp.bfloat16)

    @pl.when(is_unit)
    def _():
        @pl.loop(0, FRAMES)
        def _(frame):
            @pl.when(frame != me)
            def _():
                send_dq(frame).wait_send()

        @pl.loop(0, FRAMES // 2)
        def _(pair):
            give(pair).wait_send()

            @pl.when(2 * pair + core != me)
            def _():
                send_dkv(pair).wait_send()


def unit_call(window_offset, k_all, v_all, q_all, g_all):
    bf16, f32 = jnp.bfloat16, jnp.float32
    vmem = pl.BlockSpec(memory_space=pltpu.VMEM)
    smem = pl.BlockSpec(memory_space=pltpu.SMEM)
    shape = jax.ShapeDtypeStruct
    return pl.pallas_call(
        unit_kernel,
        name="unit_grads",
        out_shape=(
            shape((FRAMES // 2, TOK, 2 * HD), f32),
            shape((FRAMES // 2, TOK, 2 * HD), bf16),
            shape((FRAMES, BLK, HD), f32),
        ),
        in_specs=[smem] * 2 + [vmem] * 4,
        out_specs=[vmem] * 3,
        scratch_shapes=[
            pltpu.VMEM((56 * TOK, 2 * HD), bf16),
            pltpu.VMEM((56, HD, TOK), bf16),
            pltpu.VMEM((TILES, 2 * TOK, 2 * HD), bf16),
            pltpu.VMEM((56 * TOK, 2 * HD), f32),
            pltpu.VMEM((KINDS, TOK, TOK), f32),
            pltpu.VMEM((MOST_BLOCKS, TOK, TOK), f32),
            pltpu.VMEM((MOST_BLOCKS, TOK, TOK), f32),
            pltpu.VMEM((HD, 2 * TOK), f32),
        ],
        compiler_params=pltpu.CompilerParams(vmem_limit_bytes=VMEM_LIMIT),
    )(window_offset, jnp.asarray(block_table()), k_all, v_all, q_all, g_all)


def local(query_raw, key_raw, values, query_gain, key_gain, out_grad, window_offset):
    bf16, f32 = jnp.bfloat16, jnp.float32
    vmem = pl.BlockSpec(memory_space=pltpu.VMEM)
    hbm = pl.BlockSpec(memory_space=pl.ANY)
    dma = pltpu.SemaphoreType.DMA
    shape = jax.ShapeDtypeStruct
    k_all, v_all, q_all, g_all, total = pl.pallas_call(
        send_kernel,
        name="to_units",
        out_shape=(
            shape((FRAMES, TOK, HD), bf16),
            shape((FRAMES, TOK, HD), bf16),
            shape((FRAMES, BLK, HD), bf16),
            shape((FRAMES, BLK, HD), bf16),
            shape((8, TOK), f32),
        ),
        in_specs=[vmem] * 6,
        out_specs=[hbm] * 4 + [vmem],
        scratch_shapes=[
            pltpu.VMEM((LOCAL_HEADS, TOK, HD), bf16),
            pltpu.VMEM((LOCAL_HEADS, TOK, HD), bf16),
            pltpu.VMEM((8, TOK), f32),
            pltpu.VMEM((3, 8, TOK), f32),
            dma((3,)), dma((3,)),
            dma((UNITS // 2,)), dma((UNITS,)), dma((UNITS // 2,)), dma((UNITS,)),
            dma((FRAMES,)), dma((FRAMES,)), dma((FRAMES,)), dma((FRAMES,)),
            dma((FRAMES // 2,)), dma((FRAMES // 2,)),
        ],
        compiler_params=pltpu.CompilerParams(
            collective_id=0, has_side_effects=True, vmem_limit_bytes=VMEM_LIMIT
        ),
    )(query_raw, key_raw, values, out_grad, query_gain, key_gain)
    dkv_keep, dkv_give, dq_all = unit_call(window_offset, k_all, v_all, q_all, g_all)
    return pl.pallas_call(
        home_kernel,
        name="to_homes",
        out_shape=(shape((TOK, LOCAL), bf16),) * 3,
        in_specs=[vmem] * 6 + [hbm] * 2,
        out_specs=[vmem] * 3,
        scratch_shapes=[
            pltpu.VMEM((FRAMES // 2, TOK, 2 * HD), bf16),
            pltpu.VMEM((FRAMES // 2, TOK, 2 * HD), bf16),
            pltpu.VMEM((UNITS // 2, TOK, 2 * HD), bf16),
            pltpu.VMEM((UNITS, BLK, HD), f32),
            pltpu.VMEM((TOK, LOCAL), f32),
            pltpu.VMEM((8, TOK), f32),
            pltpu.VMEM((3, 8, TOK), f32),
            dma((3,)), dma((3,)),
            dma((FRAMES // 2,)), dma((FRAMES // 2,)),
            dma((FRAMES // 2,)), dma((FRAMES,)), dma((UNITS // 2,)), dma((UNITS,)),
        ],
        compiler_params=pltpu.CompilerParams(
            collective_id=1, has_side_effects=True, vmem_limit_bytes=VMEM_LIMIT
        ),
    )(query_raw, key_raw, query_gain, key_gain, total, dkv_keep, dkv_give, dq_all)


def solution(mesh):
    placed = (
        P("frame", "head"),
        P("frame", "head"),
        P("frame", "head"),
        P("head"),
        P("head"),
        P("frame", "head"),
        P(),
    )
    return jax.shard_map(
        local,
        mesh=mesh,
        in_specs=placed,
        out_specs=(P("frame", "head"), P("frame", "head"), P("frame", "head")),
        check_vma=False,
    )
```

```python
import functools
import math

import jax
import jax.numpy as jnp
from jax import lax
from jax.experimental import pallas as pl
from jax.experimental.pallas import tpu as pltpu
from jax.sharding import PartitionSpec as P

HEADS = 20
HD = 128
NB = 4
TOK = 128
BLK = 32
FRAMES = 32
FEAT = HEADS * HD
LOCAL_HEADS = 5
LOCAL = LOCAL_HEADS * HD
TILES = 8
EPSILON = 1e-06
NEG = -1e30
SCALE = HD ** (-0.5)
SCALE2 = SCALE * math.log2(math.e)
MESH = pl.DeviceIdType.MESH
VMEM_LIMIT = 60 * 1024 * 1024

UNITS = LOCAL_HEADS * NB


def my_unit():
    me = lax.axis_index("frame")
    slot = lax.rem(11 * (me // 2), 16)
    return me, slot < 2 * LOCAL_HEADS, slot // 2, 2 * lax.rem(slot, 2) + lax.rem(me, 2)


KIND_FAR = [(-4, 3), (-4, 4), (-2, 2), (-2, 3), (2, 2), (2, 3), (4, 3), (4, 4)]
OPEN = 12
SHUT = 13 + len(KIND_FAR)
KINDS = SHUT + 1
MOST_BLOCKS = 20
GROUP = 4


def far_kind(apart, level):
    return 13 + KIND_FAR.index((apart, level))


def far_block(level, other):
    return FRAMES + 8 * (level - 2) + other


def tile_blocks(tile):
    def pick(over, plain, wrapped):
        return plain + over * (wrapped - plain)

    found = [(4 * tile + part, 4 + part) for part in range(4)]
    for apart, first in ((1, 8), (7, 0)):
        other = (tile + apart) % TILES
        over = (tile + apart) // TILES
        over = over if apart == 1 else 1 - over
        for part in range(4):
            block = 4 * other + part
            if part == 0:
                block = pick(over, block, far_block(4, other))
            found.append((block, pick(over, first + part, OPEN if part == 0 else SHUT)))
    for apart in (2, 3, 4, 5, 6):
        other = (tile + apart) % TILES
        over = (tile + apart) // TILES
        if apart == 2:
            found.append((far_block(2 + 2 * over, other), pick(over, far_kind(2, 2), OPEN)))
            found.append((far_block(3, other), pick(over, far_kind(2, 3), SHUT)))
        elif apart == 3:
            found.append((far_block(3 + over, other), OPEN + 0 * over))
        elif apart == 4:
            for level in (3, 4):
                found.append((far_block(level, other), pick(over, far_kind(4, level), far_kind(-4, level))))
        elif apart == 5:
            found.append((far_block(4 - over, other), OPEN + 0 * over))
        else:
            found.append((far_block(4 - 2 * over, other), pick(over, OPEN, far_kind(-2, 2))))
            found.append((far_block(3, other), pick(over, SHUT, far_kind(-2, 3))))
    return found


def greet():
    barrier = pltpu.get_barrier_semaphore()
    me = lax.axis_index("frame")
    row = lax.axis_index("head")
    for step in range(1, FRAMES):
        pl.semaphore_signal(
            barrier, inc=1, device_id={"frame": lax.rem(me + step, FRAMES)}, device_id_type=MESH
        )
    for step in range(1, 4):
        pl.semaphore_signal(
            barrier, inc=1, device_id={"head": lax.rem(row + step, 4)}, device_id_type=MESH
        )


def all_here():
    pl.semaphore_wait(pltpu.get_barrier_semaphore(), FRAMES - 1 + 3)


def pair_rows(first, second):
    lane = lax.broadcasted_iota(jnp.int32, (TOK, TOK), 1)
    both = jnp.where(lane == 0, first, jnp.where(lane == 1, second, 0.0))
    return both.T[:8]


def pair_columns(rows):
    full = jnp.concatenate([rows, jnp.zeros((TOK - 8, TOK), jnp.float32)], axis=0).T
    return full[:, 0:1], full[:, 1:2]


def head_sum(stat, slots, send_sem, recv_sem):
    row = lax.axis_index("head")
    copies = []
    for step in range(1, 4):
        copy = pltpu.make_async_remote_copy(
            src_ref=stat,
            dst_ref=slots.at[step - 1],
            send_sem=send_sem.at[step - 1],
            recv_sem=recv_sem.at[step - 1],
            device_id={"head": lax.rem(row + step, 4)},
            device_id_type=MESH,
        )
        copy.start()
        copies.append(copy)
    return copies


def head_slice(head):
    return pl.ds(head * HD, HD)


def lanes(head):
    return pl.ds(pl.multiple_of(head * HD, HD), HD)


def dot(a, b, contract):
    return lax.dot_general(a, b, (contract, ((), ())), preferred_element_type=jnp.float32)


def frame_rows(frame, width=TOK):
    return pl.ds(pl.multiple_of(frame * width, width), width)


def main_kernel(
    offset_ref, q_ref, k_ref, v_ref, g_ref, qgain_ref, kgain_ref,
    qgrad, kgrad, vgrad, total_ref, inner_ref,
    keys, queries, stat, slots, stat2, slots2,
    kv, kt, w, acc, bias, tbuf, gbuf, dqt,
    dq_done, given, other, mixed, dkv_in, dq_in,
    zsend, zrecv, zsend2, zrecv2, vsend, gsend, ksend, qsend, vrecv, grecv, krecv, qrecv, vpass, kpass,
    give_send, give_recv, kvsend, dqsend, kvrecv, dqrecv,
):
    me, is_unit, my_head, block = my_unit()
    core = lax.rem(me, 2)
    chip = me // 2
    partner = me + 1 - 2 * core
    slot_id = 2 * my_head + block // 2
    unit = my_head * NB + block

    def squares(ref):
        sums = jnp.zeros((TOK, HD), jnp.float32)
        for head in range(LOCAL_HEADS):
            part = ref[:, head_slice(head)].astype(jnp.float32)
            sums = sums + part * part
        return jnp.sum(sums, axis=1, keepdims=True)

    greet()
    stat[...] = pair_rows(squares(q_ref), squares(k_ref))
    all_here()
    sums = head_sum(stat, slots, zsend, zrecv)

    def k_at(frame):
        return kv.at[frame_rows(frame), pl.ds(0, HD)]

    def v_at(frame):
        return kv.at[frame_rows(frame), pl.ds(HD, HD)]

    def q_at(frame):
        return w.at[frame // 4, frame_rows(lax.rem(frame, 4), BLK), pl.ds(0, HD)]

    def g_at(frame):
        return w.at[frame // 4, frame_rows(4 + lax.rem(frame, 4), BLK), pl.ds(HD, HD)]

    def remote(src, place, target, send_sem, recv_sem):
        return pltpu.make_async_remote_copy(
            src_ref=src, dst_ref=place(me), send_sem=send_sem, recv_sem=recv_sem.at[me],
            device_id={"frame": target}, device_id_type=MESH,
        )

    def send(src, place, target, send_sem, recv_sem):
        @pl.when(me != target)
        def _():
            remote(src, place, target, send_sem, recv_sem).start()

        @pl.when(me == target)
        def _():
            pltpu.make_async_copy(src, place(me), recv_sem.at[me]).start()

    def parts_of(slot, key_like, query_like, ksem, qsem, krec, qrec, k_place, q_place):
        head, half = slot // 2, lax.rem(slot, 2)
        base = 2 * lax.rem(3 * slot, 16)
        yield key_like(head), k_place, base + core, ksem.at[slot], krec
        for side in range(2):
            rows = frame_rows(2 * half + side, BLK)
            yield query_like(head, rows), q_place, base + side, qsem.at[2 * slot + side], qrec

    def raw_parts(slot):
        return parts_of(
            slot, lambda head: v_ref.at[:, lanes(head)], lambda head, rows: g_ref.at[rows, lanes(head)],
            vsend, gsend, vrecv, grecv, v_at, g_at,
        )

    def normal_parts(slot):
        return parts_of(
            slot, lambda head: keys.at[head], lambda head, rows: queries.at[head, rows],
            ksend, qsend, krecv, qrecv, k_at, q_at,
        )

    @pl.loop(0, 2 * LOCAL_HEADS)
    def _(step):
        for part in raw_parts(lax.rem(step + chip, 2 * LOCAL_HEADS)):
            send(*part)

    for copy in sums:
        copy.wait()
    total = stat[...] + slots[0] + slots[1] + slots[2]
    total_ref[...] = total
    qsum, ksum = pair_columns(total)
    qrms = lax.rsqrt(qsum / FEAT + EPSILON)
    krms = lax.rsqrt(ksum / FEAT + EPSILON)
    for head in range(LOCAL_HEADS):
        part = k_ref[:, head_slice(head)].astype(jnp.float32)
        keys[head] = (part * krms * kgain_ref[head_slice(head)].reshape(1, HD)).astype(jnp.bfloat16)
        part = q_ref[:, head_slice(head)].astype(jnp.float32)
        queries[head] = (part * qrms * qgain_ref[head_slice(head)].reshape(1, HD)).astype(jnp.bfloat16)

    @pl.loop(0, 2 * LOCAL_HEADS)
    def _(step):
        for part in normal_parts(lax.rem(step + chip, 2 * LOCAL_HEADS)):
            send(*part)

    def order(step):
        x = lax.rem(me // 8 + step + 1, 4)
        y = lax.rem(me // 2 + step // 4 + step, 4)
        return x * 4 + y

    def forward(place, step, send_sem, recv_sem):
        frame = lax.rem(me + 2 * step, FRAMES)
        return pltpu.make_async_remote_copy(
            src_ref=place(frame), dst_ref=place(frame), send_sem=send_sem.at[step],
            recv_sem=recv_sem.at[frame], device_id={"frame": partner}, device_id_type=MESH,
        )

    def arrived(place, frame, sem):
        pltpu.make_async_copy(place(frame), place(frame), sem.at[frame]).wait()

    def give(pair):
        return pltpu.make_async_remote_copy(
            src_ref=given.at[pair], dst_ref=other.at[pair], send_sem=give_send.at[pair],
            recv_sem=give_recv.at[pair], device_id={"frame": partner}, device_id_type=MESH,
        )

    def send_dq(frame):
        return pltpu.make_async_remote_copy(
            src_ref=dq_done.at[frame], dst_ref=dq_in.at[unit], send_sem=dqsend.at[frame],
            recv_sem=dqrecv.at[unit], device_id={"frame": frame}, device_id_type=MESH,
        )

    def send_dkv(pair):
        return pltpu.make_async_remote_copy(
            src_ref=mixed.at[pair], dst_ref=dkv_in.at[slot_id], send_sem=kvsend.at[pair],
            recv_sem=kvrecv.at[slot_id], device_id={"frame": 2 * pair + core}, device_id_type=MESH,
        )

    @pl.when(is_unit)
    def _():
        @pl.loop(0, FRAMES // 2)
        def _(step):
            arrived(v_at, lax.rem(me + 2 * step, FRAMES), vrecv)
            forward(v_at, step, vpass, vrecv).start()

        row_frame = lax.broadcasted_iota(jnp.int32, (TOK, TOK), 0) // BLK
        lane_frame = lax.broadcasted_iota(jnp.int32, (TOK, TOK), 1) // BLK
        zero = jnp.zeros((TOK, TOK), jnp.float32)
        hit1 = jnp.where(((row_frame - block - offset_ref[0]) & 3) < 2, 0.0, NEG)
        hit2 = jnp.where(((row_frame - block - offset_ref[1]) & 3) < 1, 0.0, NEG)

        @pl.loop(0, 12)
        def _(kind):
            d = jnp.abs(kind - 4 - lane_frame)
            bias[kind] = jnp.where(d < 2, 0.0, jnp.where(d < 4, hit1, hit2))

        bias[OPEN] = zero
        bias[SHUT] = zero + NEG
        for apart, level in KIND_FAR:
            d = jnp.abs(4 * apart + row_frame - lane_frame)
            bias[far_kind(apart, level)] = jnp.where((d >= 2**level) & (d < 2 ** (level + 1)), 0.0, NEG)

        @pl.loop(0, 56)
        def _(blk):
            acc[frame_rows(blk), :] = jnp.zeros((TOK, 2 * HD), jnp.float32)

        @pl.loop(0, TILES)
        def _(tile):
            w[tile, 0:TOK, HD:] = jnp.zeros((TOK, HD), jnp.bfloat16)
            w[tile, TOK:, 0:HD] = jnp.zeros((TOK, HD), jnp.bfloat16)

        @pl.loop(0, FRAMES // 2)
        def _(step):
            frame = lax.rem(me + 2 * step, FRAMES)
            arrived(k_at, frame, krecv)
            forward(k_at, step, kpass, krecv).start()
            kt[frame] = kv[frame_rows(frame), 0:HD].T

        @pl.loop(0, FRAMES)
        def _(frame):
            arrived(g_at, frame, grecv)
            arrived(q_at, frame, qrecv)

        @pl.loop(0, FRAMES // 2)
        def _(step):
            frame = lax.rem(me + 2 * step, FRAMES) + 1 - 2 * core
            arrived(v_at, frame, vrecv)
            arrived(k_at, frame, krecv)
            kt[frame] = kv[frame_rows(frame), 0:HD].T

        chosen = [(block + offset_ref[level - 1]) & 3 for level in (2, 3, 4)]
        is_chosen = [
            [(1 - jnp.minimum((pick - which) & 3, 1)).astype(jnp.float32) for which in range(NB)]
            for pick in chosen
        ]

        @pl.loop(0, FRAMES)
        def _(frame):
            blocks = [kv[frame_rows(NB * frame + which, BLK), :] for which in range(NB)]
            for index, weights in enumerate(is_chosen):
                picked = blocks[0] * weights[0].astype(jnp.bfloat16)
                for which in range(1, NB):
                    picked = picked + blocks[which] * weights[which].astype(jnp.bfloat16)
                kv[frame_rows(FRAMES * NB + index * FRAMES + frame, BLK), :] = picked

        @pl.loop(FRAMES, 56)
        def _(blk):
            kt[blk] = kv[frame_rows(blk), 0:HD].T

        @pl.loop(0, TILES)
        def _(tile):
            found = tile_blocks(tile)
            at = [frame_rows(blk) for blk, _ in found]
            groups = [range(i, i + GROUP) for i in range(0, MOST_BLOCKS, GROUP)]
            peak = jnp.full((8, TOK), NEG, jnp.float32)
            for group in groups:
                rows = jnp.concatenate([kv[at[slot], :] for slot in group], axis=0)
                both = dot(rows, w[tile], ((1,), (1,)))
                for index, slot in enumerate(group):
                    part = both[index * TOK : (index + 1) * TOK]
                    t = part[:, 0:TOK] * SCALE2 + bias[found[slot][1]]
                    tbuf[slot] = t
                    gbuf[slot] = part[:, TOK:]
                    peak = jnp.maximum(peak, jnp.max(t.reshape(16, 8, TOK), axis=0))
            peak = jnp.max(peak, axis=0, keepdims=True)
            total = jnp.zeros((8, TOK), jnp.float32)
            weighted = jnp.zeros((8, TOK), jnp.float32)
            for slot in range(MOST_BLOCKS):
                weight = jnp.exp2(tbuf[slot] - peak)
                tbuf[slot] = weight
                total = total + jnp.sum(weight.reshape(16, 8, TOK), axis=0)
                weighted = weighted + jnp.sum((weight * gbuf[slot]).reshape(16, 8, TOK), axis=0)
            total = jnp.sum(total, axis=0, keepdims=True)
            inverse = 1.0 / total
            delta = jnp.sum(weighted, axis=0, keepdims=True) * inverse
            dqt[...] = jnp.zeros((HD, 2 * TOK), jnp.float32)
            for group in groups:
                lefts, lows = [], []
                for slot in group:
                    probs = tbuf[slot] * inverse
                    grad = probs * (gbuf[slot] - delta)
                    high = grad.astype(jnp.bfloat16)
                    low = (grad - high.astype(jnp.float32)).astype(jnp.bfloat16)
                    lefts.append(jnp.concatenate([high, probs.astype(jnp.bfloat16)], axis=1))
                    lows.append(jnp.concatenate([high, low], axis=1))
                both = dot(jnp.concatenate(lefts, axis=0), w[tile], ((1,), (0,)))
                for index, slot in enumerate(group):
                    acc[at[slot], :] += both[index * TOK : (index + 1) * TOK]
                keyt = jnp.concatenate([kt[found[slot][0]] for slot in group], axis=1)
                dqt[...] += dot(keyt, jnp.concatenate(lows, axis=0), ((1,), (0,)))

            dq = (dqt[:, 0:TOK] + dqt[:, TOK:]).T.astype(jnp.bfloat16)
            for part in range(4):
                frame = 4 * tile + part
                dq_done[frame] = dq[part * BLK : (part + 1) * BLK]

                @pl.when(frame != me)
                def _():
                    send_dq(frame).start()

                @pl.when(frame == me)
                def _():
                    pltpu.make_async_copy(dq_done.at[frame], dq_in.at[unit], dqrecv.at[unit]).start()

        def gathered(frame):
            pieces = []
            for which in range(NB):
                piece = acc[frame_rows(NB * frame + which, BLK), :]
                for index, weights in enumerate(is_chosen):
                    far = acc[frame_rows(FRAMES * NB + index * FRAMES + frame, BLK), :]
                    piece = piece + far * weights[which]
                pieces.append(piece)
            return jnp.concatenate(pieces, axis=0)

        @pl.loop(0, FRAMES // 2)
        def _(step):
            pair = order(step)
            given[pair] = gathered(2 * pair + 1 - core).astype(jnp.bfloat16)
            give(pair).start()

        @pl.loop(0, FRAMES // 2)
        def _(step):
            pair = order(step)
            mine = gathered(2 * pair + core)
            give(pair).wait_recv()
            mixed[pair] = (mine + other[pair].astype(jnp.float32)).astype(jnp.bfloat16)

            @pl.when(2 * pair + core != me)
            def _():
                send_dkv(pair).start()

            @pl.when(2 * pair + core == me)
            def _():
                pltpu.make_async_copy(mixed.at[pair], dkv_in.at[slot_id], kvrecv.at[slot_id]).start()

    qinner = jnp.zeros((TOK, HD), jnp.float32)
    kinner = jnp.zeros((TOK, HD), jnp.float32)
    for h in range(LOCAL_HEADS):
        for b in range(NB):
            u = h * NB + b
            pltpu.make_async_copy(dq_in.at[u], dq_in.at[u], dqrecv.at[u]).wait()
        dq = dq_in[pl.ds(h * NB, NB)].astype(jnp.float32).reshape(TOK, HD)
        gained = qgain_ref[head_slice(h)].reshape(1, HD) * (dq * SCALE)
        qgrad[:, head_slice(h)] = gained
        qinner = qinner + gained * q_ref[:, head_slice(h)].astype(jnp.float32)
    for h in range(LOCAL_HEADS):
        for u in (2 * h, 2 * h + 1):
            pltpu.make_async_copy(dkv_in.at[u], dkv_in.at[u], kvrecv.at[u]).wait()
        both = dkv_in[2 * h].astype(jnp.float32) + dkv_in[2 * h + 1].astype(jnp.float32)
        vgrad[:, head_slice(h)] = both[:, HD:].astype(jnp.bfloat16)
        gained = kgain_ref[head_slice(h)].reshape(1, HD) * (both[:, 0:HD] * SCALE)
        kgrad[:, head_slice(h)] = gained
        kinner = kinner + gained * k_ref[:, head_slice(h)].astype(jnp.float32)
    stat2[...] = pair_rows(
        jnp.sum(qinner, axis=1, keepdims=True), jnp.sum(kinner, axis=1, keepdims=True)
    )
    for copy in head_sum(stat2, slots2, zsend2, zrecv2):
        copy.wait()
    inner_ref[...] = stat2[...] + slots2[0] + slots2[1] + slots2[2]

    @pl.loop(0, 2 * LOCAL_HEADS)
    def _(slot):
        for parts in (raw_parts(slot), normal_parts(slot)):
            for src, place, target, ssem, rsem in parts:
                @pl.when(me != target)
                def _():
                    remote(src, place, target, ssem, rsem).wait_send()

    @pl.when(is_unit)
    def _():
        @pl.loop(0, FRAMES)
        def _(frame):
            @pl.when(frame != me)
            def _():
                send_dq(frame).wait_send()

        @pl.loop(0, FRAMES // 2)
        def _(pair):
            forward(v_at, pair, vpass, vrecv).wait_send()
            forward(k_at, pair, kpass, krecv).wait_send()
            give(pair).wait_send()

            @pl.when(2 * pair + core != me)
            def _():
                send_dkv(pair).wait_send()


def finish_kernel(q_ref, k_ref, qgrad, kgrad, vgrad, total_ref, inner_ref, dq_out, dk_out, dv_out):
    qsum, ksum = pair_columns(total_ref[...])
    qdot, kdot = pair_columns(inner_ref[...])
    for raw, grad, square, inner, out in (
        (q_ref, qgrad, qsum, qdot, dq_out),
        (k_ref, kgrad, ksum, kdot, dk_out),
    ):
        rms = lax.rsqrt(square / FEAT + EPSILON)
        factor = rms * rms * rms / FEAT * inner
        for head in range(LOCAL_HEADS):
            at = head_slice(head)
            out[:, at] = (rms * grad[:, at] - factor * raw[:, at].astype(jnp.float32)).astype(jnp.bfloat16)
    dv_out[...] = vgrad[...]


def local(query_raw, key_raw, values, query_gain, key_gain, out_grad, window_offset):
    bf16, f32 = jnp.bfloat16, jnp.float32
    vmem = pl.BlockSpec(memory_space=pltpu.VMEM)
    smem = pl.BlockSpec(memory_space=pltpu.SMEM)
    dma = pltpu.SemaphoreType.DMA
    shape = jax.ShapeDtypeStruct
    half = FRAMES // 2
    qgrad, kgrad, vgrad, total, inner = pl.pallas_call(
        main_kernel,
        name="band_grads",
        out_shape=(
            shape((TOK, LOCAL), f32),
            shape((TOK, LOCAL), f32),
            shape((TOK, LOCAL), bf16),
            shape((8, TOK), f32),
            shape((8, TOK), f32),
        ),
        in_specs=[smem] + [vmem] * 6,
        out_specs=[vmem] * 5,
        scratch_shapes=[
            pltpu.VMEM((LOCAL_HEADS, TOK, HD), bf16),
            pltpu.VMEM((LOCAL_HEADS, TOK, HD), bf16),
            pltpu.VMEM((8, TOK), f32),
            pltpu.VMEM((3, 8, TOK), f32),
            pltpu.VMEM((8, TOK), f32),
            pltpu.VMEM((3, 8, TOK), f32),
            pltpu.VMEM((56 * TOK, 2 * HD), bf16),
            pltpu.VMEM((56, HD, TOK), bf16),
            pltpu.VMEM((TILES, 2 * TOK, 2 * HD), bf16),
            pltpu.VMEM((56 * TOK, 2 * HD), f32),
            pltpu.VMEM((KINDS, TOK, TOK), f32),
            pltpu.VMEM((MOST_BLOCKS, TOK, TOK), f32),
            pltpu.VMEM((MOST_BLOCKS, TOK, TOK), f32),
            pltpu.VMEM((HD, 2 * TOK), f32),
            pltpu.VMEM((FRAMES, BLK, HD), bf16),
            pltpu.VMEM((half, TOK, 2 * HD), bf16),
            pltpu.VMEM((half, TOK, 2 * HD), bf16),
            pltpu.VMEM((half, TOK, 2 * HD), bf16),
            pltpu.VMEM((UNITS // 2, TOK, 2 * HD), bf16),
            pltpu.VMEM((UNITS, BLK, HD), bf16),
            dma((3,)), dma((3,)), dma((3,)), dma((3,)),
            dma((UNITS // 2,)), dma((UNITS,)), dma((UNITS // 2,)), dma((UNITS,)),
            dma((FRAMES,)), dma((FRAMES,)), dma((FRAMES,)), dma((FRAMES,)),
            dma((half,)), dma((half,)), dma((half,)), dma((half,)),
            dma((half,)), dma((FRAMES,)), dma((UNITS // 2,)), dma((UNITS,)),
        ],
        compiler_params=pltpu.CompilerParams(
            collective_id=0, has_side_effects=True, vmem_limit_bytes=VMEM_LIMIT
        ),
    )(window_offset, query_raw, key_raw, values, out_grad, query_gain, key_gain)
    return pl.pallas_call(
        finish_kernel,
        name="norm_grads",
        out_shape=(shape((TOK, LOCAL), bf16),) * 3,
        in_specs=[vmem] * 7,
        out_specs=[vmem] * 3,
    )(query_raw, key_raw, qgrad, kgrad, vgrad, total, inner)


def solution(mesh):
    placed = (
        P("frame", "head"),
        P("frame", "head"),
        P("frame", "head"),
        P("head"),
        P("head"),
        P("frame", "head"),
        P(),
    )
    return jax.shard_map(
        local,
        mesh=mesh,
        in_specs=placed,
        out_specs=(P("frame", "head"), P("frame", "head"), P("frame", "head")),
        check_vma=False,
    )
```

```python
import functools
import math

import jax
import jax.numpy as jnp
from jax import lax
from jax.experimental import pallas as pl
from jax.experimental.pallas import tpu as pltpu
from jax.sharding import PartitionSpec as P

HEADS = 20
HD = 128
NB = 4
TOK = 128
BLK = 32
FRAMES = 32
FEAT = HEADS * HD
LOCAL_HEADS = 5
LOCAL = LOCAL_HEADS * HD
TILES = 8
EPSILON = 1e-06
NEG = -1e30
SCALE = HD ** (-0.5)
SCALE2 = SCALE * math.log2(math.e)
MESH = pl.DeviceIdType.MESH
VMEM_LIMIT = 60 * 1024 * 1024

UNITS = LOCAL_HEADS * NB


def my_unit():
    me = lax.axis_index("frame")
    slot = lax.rem(11 * (me // 2), 16)
    return me, slot < 2 * LOCAL_HEADS, slot // 2, 2 * lax.rem(slot, 2) + lax.rem(me, 2)


KIND_FAR = [(-4, 3), (-4, 4), (-2, 2), (-2, 3), (2, 2), (2, 3), (4, 3), (4, 4)]
OPEN = 12
SHUT = 13 + len(KIND_FAR)
KINDS = SHUT + 1
MOST_BLOCKS = 20
TILE_BLOCKS = 7


def far_kind(apart, level):
    return 13 + KIND_FAR.index((apart, level))


def blocks_between(apart, over):
    def pick(plain, wrapped):
        return plain + over * (wrapped - plain)

    if apart == 0:
        return [(part, part, 4 + part) for part in range(4)]
    if apart in (1, 7):
        first, slot = (8, 4) if apart == 1 else (0, 8)
        return [(slot, pick(0, 6), pick(first, OPEN))] + [
            (slot + part, part, pick(first + part, SHUT)) for part in range(1, 4)
        ]
    if apart == 2:
        return [(12, pick(4, 6), pick(far_kind(2, 2), OPEN)), (13, 5, pick(far_kind(2, 3), SHUT))]
    if apart == 3:
        return [(14, pick(5, 6), OPEN)]
    if apart == 4:
        return [(13 + level - 1, 2 + level, pick(far_kind(4, level), far_kind(-4, level))) for level in (3, 4)]
    if apart == 5:
        return [(17, pick(6, 5), OPEN)]
    return [(18, pick(6, 4), pick(OPEN, far_kind(-2, 2))), (19, 5, pick(SHUT, far_kind(-2, 3)))]


def wrapped(tile, apart):
    over = (tile + apart) // TILES
    return 1 - over if apart == 7 else over


def greet():
    barrier = pltpu.get_barrier_semaphore()
    me = lax.axis_index("frame")
    row = lax.axis_index("head")
    for step in range(1, FRAMES):
        pl.semaphore_signal(
            barrier, inc=1, device_id={"frame": lax.rem(me + step, FRAMES)}, device_id_type=MESH
        )
    for step in range(1, 4):
        pl.semaphore_signal(
            barrier, inc=1, device_id={"head": lax.rem(row + step, 4)}, device_id_type=MESH
        )


def all_here():
    pl.semaphore_wait(pltpu.get_barrier_semaphore(), FRAMES - 1 + 3)


def pair_rows(first, second):
    lane = lax.broadcasted_iota(jnp.int32, (TOK, TOK), 1)
    both = jnp.where(lane == 0, first, jnp.where(lane == 1, second, 0.0))
    return both.T[:8]


def pair_columns(rows):
    full = jnp.concatenate([rows, jnp.zeros((TOK - 8, TOK), jnp.float32)], axis=0).T
    return full[:, 0:1], full[:, 1:2]


def head_sum(stat, slots, send_sem, recv_sem):
    row = lax.axis_index("head")
    copies = []
    for step in range(1, 4):
        copy = pltpu.make_async_remote_copy(
            src_ref=stat,
            dst_ref=slots.at[step - 1],
            send_sem=send_sem.at[step - 1],
            recv_sem=recv_sem.at[step - 1],
            device_id={"head": lax.rem(row + step, 4)},
            device_id_type=MESH,
        )
        copy.start()
        copies.append(copy)
    return copies


def head_slice(head):
    return pl.ds(head * HD, HD)


def lanes(head):
    return pl.ds(pl.multiple_of(head * HD, HD), HD)


def dot(a, b, contract):
    return lax.dot_general(a, b, (contract, ((), ())), preferred_element_type=jnp.float32)


def frame_rows(frame, width=TOK):
    return pl.ds(pl.multiple_of(frame * width, width), width)


def frame_block(frame):
    return TILE_BLOCKS * (frame // 4) + lax.rem(frame, 4)


def main_kernel(
    offset_ref, q_ref, k_ref, v_ref, g_ref, qgain_ref, kgain_ref,
    qgrad, kgrad, vgrad, total_ref, inner_ref,
    keys, queries, stat, slots, stat2, slots2,
    kv, kt, w, acc, bias, tbuf, gbuf, grads, lows, peaks,
    dq_done, given, other, keep, mixed, dkv_in, dq_in,
    zsend, zrecv, zsend2, zrecv2, vsend, gsend, ksend, qsend, vrecv, grecv, krecv, qrecv, vpass, kpass,
    give_send, give_recv, kvsend, dqsend, kvrecv, dqrecv,
):
    me, is_unit, my_head, block = my_unit()
    core = lax.rem(me, 2)
    partner = me + 1 - 2 * core
    slot_id = 2 * my_head + block // 2
    unit = my_head * NB + block

    def squares(ref):
        sums = jnp.zeros((TOK, HD), jnp.float32)
        for head in range(LOCAL_HEADS):
            part = ref[:, head_slice(head)].astype(jnp.float32)
            sums = sums + part * part
        return jnp.sum(sums, axis=1, keepdims=True)

    greet()
    stat[...] = pair_rows(squares(q_ref), squares(k_ref))
    all_here()
    sums = head_sum(stat, slots, zsend, zrecv)

    def k_at(frame):
        return kv.at[frame_rows(frame_block(frame)), pl.ds(0, HD)]

    def v_at(frame):
        return kv.at[frame_rows(frame_block(frame)), pl.ds(HD, HD)]

    def q_at(frame):
        return w.at[frame // 4, frame_rows(lax.rem(frame, 4), BLK), pl.ds(0, HD)]

    def g_at(frame):
        return w.at[frame // 4, frame_rows(4 + lax.rem(frame, 4), BLK), pl.ds(HD, HD)]

    def remote(src, place, target, send_sem, recv_sem):
        return pltpu.make_async_remote_copy(
            src_ref=src, dst_ref=place(me), send_sem=send_sem, recv_sem=recv_sem.at[me],
            device_id={"frame": target}, device_id_type=MESH,
        )

    def send(src, place, target, send_sem, recv_sem):
        @pl.when(me != target)
        def _():
            remote(src, place, target, send_sem, recv_sem).start()

        @pl.when(me == target)
        def _():
            pltpu.make_async_copy(src, place(me), recv_sem.at[me]).start()

    def key_part(slot, source, place, ssem, rsem):
        return source(slot // 2), place, 2 * lax.rem(3 * slot, 16) + core, ssem.at[slot], rsem

    def query_part(slot, side, source, place, ssem, rsem):
        rows = frame_rows(2 * lax.rem(slot, 2) + side, BLK)
        return source(slot // 2, rows), place, 2 * lax.rem(3 * slot, 16) + side, ssem.at[2 * slot + side], rsem

    def parts_v(slot):
        return (key_part(slot, lambda head: v_ref.at[:, lanes(head)], v_at, vsend, vrecv),)

    def parts_g(slot):
        return tuple(
            query_part(slot, side, lambda head, rows: g_ref.at[rows, lanes(head)], g_at, gsend, grecv)
            for side in range(2)
        )

    def parts_k(slot):
        return (key_part(slot, lambda head: keys.at[head], k_at, ksend, krecv),)

    def parts_q(slot):
        return tuple(
            query_part(slot, side, lambda head, rows: queries.at[head, rows], q_at, qsend, qrecv)
            for side in range(2)
        )

    turn = me // 4 + me // 16

    def send_all(*kinds):
        @pl.loop(0, 2 * LOCAL_HEADS)
        def _(step):
            for kind in kinds:
                for part in kind(lax.rem(step + turn, 2 * LOCAL_HEADS)):
                    send(*part)

    send_all(parts_v, parts_g)

    for copy in sums:
        copy.wait()
    total = stat[...] + slots[0] + slots[1] + slots[2]
    total_ref[...] = total
    qsum, ksum = pair_columns(total)
    qrms = lax.rsqrt(qsum / FEAT + EPSILON)
    krms = lax.rsqrt(ksum / FEAT + EPSILON)
    for head in range(LOCAL_HEADS):
        part = k_ref[:, head_slice(head)].astype(jnp.float32)
        keys[head] = (part * krms * kgain_ref[head_slice(head)].reshape(1, HD)).astype(jnp.bfloat16)
        part = q_ref[:, head_slice(head)].astype(jnp.float32)
        queries[head] = (part * qrms * qgain_ref[head_slice(head)].reshape(1, HD)).astype(jnp.bfloat16)

    send_all(parts_q)
    send_all(parts_k)

    def forward(place, step, send_sem, recv_sem):
        frame = 2 * step + core
        return pltpu.make_async_remote_copy(
            src_ref=place(frame), dst_ref=place(frame), send_sem=send_sem.at[step],
            recv_sem=recv_sem.at[frame], device_id={"frame": partner}, device_id_type=MESH,
        )

    def arrived(place, frame, sem):
        pltpu.make_async_copy(place(frame), place(frame), sem.at[frame]).wait()

    def give(pair):
        return pltpu.make_async_remote_copy(
            src_ref=given.at[pair], dst_ref=other.at[pair], send_sem=give_send.at[pair],
            recv_sem=give_recv.at[pair], device_id={"frame": partner}, device_id_type=MESH,
        )

    def send_dq(frame):
        return pltpu.make_async_remote_copy(
            src_ref=dq_done.at[frame], dst_ref=dq_in.at[unit], send_sem=dqsend.at[frame],
            recv_sem=dqrecv.at[unit], device_id={"frame": frame}, device_id_type=MESH,
        )

    def send_dkv(pair):
        return pltpu.make_async_remote_copy(
            src_ref=mixed.at[pair], dst_ref=dkv_in.at[slot_id], send_sem=kvsend.at[pair],
            recv_sem=kvrecv.at[slot_id], device_id={"frame": 2 * pair + core}, device_id_type=MESH,
        )

    @pl.when(is_unit)
    def _():
        @pl.loop(0, FRAMES // 2)
        def _(step):
            pair = lax.rem(me // 2 + step, FRAMES // 2)
            arrived(v_at, 2 * pair + core, vrecv)
            forward(v_at, pair, vpass, vrecv).start()

        row_frame = lax.broadcasted_iota(jnp.int32, (TOK, TOK), 0) // BLK
        lane_frame = lax.broadcasted_iota(jnp.int32, (TOK, TOK), 1) // BLK
        zero = jnp.zeros((TOK, TOK), jnp.float32)
        hit1 = jnp.where(((row_frame - block - offset_ref[0]) & 3) < 2, 0.0, NEG)
        hit2 = jnp.where(((row_frame - block - offset_ref[1]) & 3) < 1, 0.0, NEG)

        @pl.loop(0, 12)
        def _(kind):
            d = jnp.abs(kind - 4 - lane_frame)
            bias[kind] = jnp.where(d < 2, 0.0, jnp.where(d < 4, hit1, hit2))

        bias[OPEN] = zero
        bias[SHUT] = zero + NEG
        for apart, level in KIND_FAR:
            d = jnp.abs(4 * apart + row_frame - lane_frame)
            bias[far_kind(apart, level)] = jnp.where((d >= 2**level) & (d < 2 ** (level + 1)), 0.0, NEG)

        @pl.loop(0, TILES)
        def _(tile):
            w[tile, 0:TOK, HD:] = jnp.zeros((TOK, HD), jnp.bfloat16)
            w[tile, TOK:, 0:HD] = jnp.zeros((TOK, HD), jnp.bfloat16)
            peaks[tile] = jnp.full((8, TOK), NEG, jnp.float32)

        @pl.loop(0, FRAMES)
        def _(frame):
            arrived(g_at, frame, grecv)
            arrived(q_at, frame, qrecv)

        is_chosen = []
        for level in (2, 3, 4):
            pick = (block + offset_ref[level - 1]) & 3
            is_chosen.append(
                [(1 - jnp.minimum((pick - which) & 3, 1)).astype(jnp.float32) for which in range(NB)]
            )

        def at_step(step, body):
            place = lax.rem(slot_id - step + 20, 10)

            @pl.when(lax.rem(place, 5) != 4)
            def _():
                body(place - place // 5)

        def pass_keys(tile):
            for part in range(2):
                arrived(k_at, 4 * tile + 2 * part + core, krecv)
                forward(k_at, 2 * tile + part, kpass, krecv).start()

        def score(tile):
            for part in range(2):
                frame = 4 * tile + 2 * part + 1 - core
                arrived(v_at, frame, vrecv)
                arrived(k_at, frame, krecv)
            base = TILE_BLOCKS * tile
            for part in range(4):
                blocks = [kv[frame_rows(NB * (base + part) + which, BLK), :] for which in range(NB)]
                for index, weights in enumerate(is_chosen):
                    picked = blocks[0] * weights[0].astype(jnp.bfloat16)
                    for which in range(1, NB):
                        picked = picked + blocks[which] * weights[which].astype(jnp.bfloat16)
                    kv[frame_rows(NB * (base + 4 + index) + part, BLK), :] = picked
            for part in range(TILE_BLOCKS):
                kt[base + part] = kv[frame_rows(base + part), 0:HD].T
            for apart in range(TILES):
                asker = lax.rem(tile + TILES - apart, TILES)
                found = blocks_between(apart, wrapped(asker, apart))
                rows = jnp.concatenate([kv[frame_rows(base + blk), :] for _, blk, _ in found], axis=0)
                both = dot(rows, w[asker], ((1,), (1,)))
                peak = peaks[asker]
                for index, (slot, _, kind) in enumerate(found):
                    part = both[index * TOK : (index + 1) * TOK]
                    t = part[:, 0:TOK] * SCALE2 + bias[kind]
                    tbuf[asker, slot] = t
                    gbuf[asker, slot] = part[:, TOK:]
                    peak = jnp.maximum(peak, jnp.max(t.reshape(16, 8, TOK), axis=0))
                peaks[asker] = peak

        at_step(0, pass_keys)

        @pl.loop(0, 9)
        def _(step):
            at_step(step + 1, pass_keys)
            at_step(step, score)

        at_step(9, score)

        @pl.loop(0, TILES)
        def _(tile):
            peak = jnp.max(peaks[tile], axis=0, keepdims=True)
            total = jnp.zeros((8, TOK), jnp.float32)
            weighted = jnp.zeros((8, TOK), jnp.float32)
            for slot in range(MOST_BLOCKS):
                weight = jnp.exp2(tbuf[tile, slot] - peak)
                tbuf[tile, slot] = weight
                total = total + jnp.sum(weight.reshape(16, 8, TOK), axis=0)
                weighted = weighted + jnp.sum((weight * gbuf[tile, slot]).reshape(16, 8, TOK), axis=0)
            total = jnp.sum(total, axis=0, keepdims=True)
            inverse = 1.0 / total
            delta = jnp.sum(weighted, axis=0, keepdims=True) * inverse
            for slot in range(MOST_BLOCKS):
                probs = tbuf[tile, slot] * inverse
                grad = probs * (gbuf[tile, slot] - delta)
                high = grad.astype(jnp.bfloat16)
                grads[tile, slot, :, 0:TOK] = high
                grads[tile, slot, :, TOK:] = probs.astype(jnp.bfloat16)
                lows[tile, slot] = (grad - high.astype(jnp.float32)).astype(jnp.bfloat16)

        def key_grads(tile):
            for index in range(3):
                acc[4 + index] = jnp.zeros((TOK, 2 * HD), jnp.float32)
            for apart in range(TILES):
                asker = lax.rem(tile + TILES - apart, TILES)
                found = blocks_between(apart, wrapped(asker, apart))
                left = jnp.concatenate([grads[asker, slot] for slot, _, _ in found], axis=0)
                both = dot(left, w[asker], ((1,), (0,)))
                for index, (_, blk, _) in enumerate(found):
                    piece = both[index * TOK : (index + 1) * TOK]
                    if apart == 0:
                        acc[blk] = piece
                    else:
                        acc[blk] += piece
            for part in range(4):
                rows = pl.ds(part * BLK, BLK)
                for which in range(NB):
                    piece = acc[part, which * BLK : (which + 1) * BLK]
                    for index, weights in enumerate(is_chosen):
                        piece = piece + acc[4 + index, rows] * weights[which]
                    acc[part, which * BLK : (which + 1) * BLK] = piece
            for part in range(2):
                pair = 2 * tile + part
                given[pair] = acc[2 * part + 1 - core].astype(jnp.bfloat16)
                give(pair).start()
                keep[pair] = acc[2 * part + core]

        def query_grads(tile):
            total = jnp.zeros((HD, 2 * TOK), jnp.float32)
            for apart in range(TILES):
                base = TILE_BLOCKS * lax.rem(tile + apart, TILES)
                found = blocks_between(apart, wrapped(tile, apart))
                keyt = jnp.concatenate([kt[base + blk] for _, blk, _ in found], axis=1)
                right = jnp.concatenate(
                    [
                        jnp.concatenate([grads[tile, slot, :, 0:TOK], lows[tile, slot]], axis=1)
                        for slot, _, _ in found
                    ],
                    axis=0,
                )
                total = total + dot(keyt, right, ((1,), (0,)))
            dq = (total[:, 0:TOK] + total[:, TOK:]).T.astype(jnp.bfloat16)
            for part in range(4):
                frame = 4 * tile + part
                dq_done[frame] = dq[part * BLK : (part + 1) * BLK]

                @pl.when(frame != me)
                def _():
                    send_dq(frame).start()

                @pl.when(frame == me)
                def _():
                    pltpu.make_async_copy(dq_done.at[frame], dq_in.at[unit], dqrecv.at[unit]).start()

        def mix(tile):
            for part in range(2):
                pair = 2 * tile + part
                give(pair).wait_recv()
                mixed[pair] = (keep[pair] + other[pair].astype(jnp.float32)).astype(jnp.bfloat16)

                @pl.when(2 * pair + core != me)
                def _():
                    send_dkv(pair).start()

                @pl.when(2 * pair + core == me)
                def _():
                    pltpu.make_async_copy(mixed.at[pair], dkv_in.at[slot_id], kvrecv.at[slot_id]).start()

        def turned(step):
            return lax.rem(step + slot_id, TILES)

        key_grads(turned(0))

        @pl.loop(1, TILES)
        def _(step):
            key_grads(turned(step))
            mix(turned(step - 1))
            query_grads(turned(step - 1))

        mix(turned(TILES - 1))
        query_grads(turned(TILES - 1))

    qinner = jnp.zeros((TOK, HD), jnp.float32)
    kinner = jnp.zeros((TOK, HD), jnp.float32)
    for h in range(LOCAL_HEADS):
        for b in range(NB):
            u = h * NB + b
            pltpu.make_async_copy(dq_in.at[u], dq_in.at[u], dqrecv.at[u]).wait()
        dq = dq_in[pl.ds(h * NB, NB)].astype(jnp.float32).reshape(TOK, HD)
        gained = qgain_ref[head_slice(h)].reshape(1, HD) * (dq * SCALE)
        qgrad[:, head_slice(h)] = gained
        qinner = qinner + gained * q_ref[:, head_slice(h)].astype(jnp.float32)
    for h in range(LOCAL_HEADS):
        for u in (2 * h, 2 * h + 1):
            pltpu.make_async_copy(dkv_in.at[u], dkv_in.at[u], kvrecv.at[u]).wait()
        both = dkv_in[2 * h].astype(jnp.float32) + dkv_in[2 * h + 1].astype(jnp.float32)
        vgrad[:, head_slice(h)] = both[:, HD:].astype(jnp.bfloat16)
        gained = kgain_ref[head_slice(h)].reshape(1, HD) * (both[:, 0:HD] * SCALE)
        kgrad[:, head_slice(h)] = gained
        kinner = kinner + gained * k_ref[:, head_slice(h)].astype(jnp.float32)
    stat2[...] = pair_rows(
        jnp.sum(qinner, axis=1, keepdims=True), jnp.sum(kinner, axis=1, keepdims=True)
    )
    for copy in head_sum(stat2, slots2, zsend2, zrecv2):
        copy.wait()
    inner_ref[...] = stat2[...] + slots2[0] + slots2[1] + slots2[2]

    @pl.loop(0, 2 * LOCAL_HEADS)
    def _(slot):
        for parts in (parts_v(slot), parts_g(slot), parts_k(slot), parts_q(slot)):
            for src, place, target, ssem, rsem in parts:
                @pl.when(me != target)
                def _():
                    remote(src, place, target, ssem, rsem).wait_send()

    @pl.when(is_unit)
    def _():
        @pl.loop(0, FRAMES)
        def _(frame):
            @pl.when(frame != me)
            def _():
                send_dq(frame).wait_send()

        @pl.loop(0, FRAMES // 2)
        def _(pair):
            forward(v_at, pair, vpass, vrecv).wait_send()
            forward(k_at, pair, kpass, krecv).wait_send()
            give(pair).wait_send()

            @pl.when(2 * pair + core != me)
            def _():
                send_dkv(pair).wait_send()


def finish_kernel(q_ref, k_ref, qgrad, kgrad, vgrad, total_ref, inner_ref, dq_out, dk_out, dv_out):
    qsum, ksum = pair_columns(total_ref[...])
    qdot, kdot = pair_columns(inner_ref[...])
    for raw, grad, square, inner, out in (
        (q_ref, qgrad, qsum, qdot, dq_out),
        (k_ref, kgrad, ksum, kdot, dk_out),
    ):
        rms = lax.rsqrt(square / FEAT + EPSILON)
        factor = rms * rms * rms / FEAT * inner
        for head in range(LOCAL_HEADS):
            at = head_slice(head)
            out[:, at] = (rms * grad[:, at] - factor * raw[:, at].astype(jnp.float32)).astype(jnp.bfloat16)
    dv_out[...] = vgrad[...]


def local(query_raw, key_raw, values, query_gain, key_gain, out_grad, window_offset):
    bf16, f32 = jnp.bfloat16, jnp.float32
    vmem = pl.BlockSpec(memory_space=pltpu.VMEM)
    smem = pl.BlockSpec(memory_space=pltpu.SMEM)
    dma = pltpu.SemaphoreType.DMA
    shape = jax.ShapeDtypeStruct
    half = FRAMES // 2
    qgrad, kgrad, vgrad, total, inner = pl.pallas_call(
        main_kernel,
        name="band_grads",
        out_shape=(
            shape((TOK, LOCAL), f32),
            shape((TOK, LOCAL), f32),
            shape((TOK, LOCAL), bf16),
            shape((8, TOK), f32),
            shape((8, TOK), f32),
        ),
        in_specs=[smem] + [vmem] * 6,
        out_specs=[vmem] * 5,
        scratch_shapes=[
            pltpu.VMEM((LOCAL_HEADS, TOK, HD), bf16),
            pltpu.VMEM((LOCAL_HEADS, TOK, HD), bf16),
            pltpu.VMEM((8, TOK), f32),
            pltpu.VMEM((3, 8, TOK), f32),
            pltpu.VMEM((8, TOK), f32),
            pltpu.VMEM((3, 8, TOK), f32),
            pltpu.VMEM((56 * TOK, 2 * HD), bf16),
            pltpu.VMEM((56, HD, TOK), bf16),
            pltpu.VMEM((TILES, 2 * TOK, 2 * HD), bf16),
            pltpu.VMEM((TILE_BLOCKS, TOK, 2 * HD), f32),
            pltpu.VMEM((KINDS, TOK, TOK), f32),
            pltpu.VMEM((TILES, MOST_BLOCKS, TOK, TOK), f32),
            pltpu.VMEM((TILES, MOST_BLOCKS, TOK, TOK), f32),
            pltpu.VMEM((TILES, MOST_BLOCKS, TOK, 2 * TOK), bf16),
            pltpu.VMEM((TILES, MOST_BLOCKS, TOK, TOK), bf16),
            pltpu.VMEM((TILES, 8, TOK), f32),
            pltpu.VMEM((FRAMES, BLK, HD), bf16),
            pltpu.VMEM((half, TOK, 2 * HD), bf16),
            pltpu.VMEM((half, TOK, 2 * HD), bf16),
            pltpu.VMEM((half, TOK, 2 * HD), f32),
            pltpu.VMEM((half, TOK, 2 * HD), bf16),
            pltpu.VMEM((UNITS // 2, TOK, 2 * HD), bf16),
            pltpu.VMEM((UNITS, BLK, HD), bf16),
            dma((3,)), dma((3,)), dma((3,)), dma((3,)),
            dma((UNITS // 2,)), dma((UNITS,)), dma((UNITS // 2,)), dma((UNITS,)),
            dma((FRAMES,)), dma((FRAMES,)), dma((FRAMES,)), dma((FRAMES,)),
            dma((half,)), dma((half,)), dma((half,)), dma((half,)),
            dma((half,)), dma((FRAMES,)), dma((UNITS // 2,)), dma((UNITS,)),
        ],
        compiler_params=pltpu.CompilerParams(
            collective_id=0, has_side_effects=True, vmem_limit_bytes=VMEM_LIMIT
        ),
    )(window_offset, query_raw, key_raw, values, out_grad, query_gain, key_gain)
    return pl.pallas_call(
        finish_kernel,
        name="norm_grads",
        out_shape=(shape((TOK, LOCAL), bf16),) * 3,
        in_specs=[vmem] * 7,
        out_specs=[vmem] * 3,
    )(query_raw, key_raw, qgrad, kgrad, vgrad, total, inner)


def solution(mesh):
    placed = (
        P("frame", "head"),
        P("frame", "head"),
        P("frame", "head"),
        P("head"),
        P("head"),
        P("frame", "head"),
        P(),
    )
    return jax.shard_map(
        local,
        mesh=mesh,
        in_specs=placed,
        out_specs=(P("frame", "head"), P("frame", "head"), P("frame", "head")),
        check_vma=False,
    )
```

```python
import functools
import math

import jax
import jax.numpy as jnp
from jax import lax
from jax.experimental import pallas as pl
from jax.experimental.pallas import tpu as pltpu
from jax.sharding import PartitionSpec as P

HEADS = 20
HD = 128
NB = 4
TOK = 128
BLK = 32
FRAMES = 32
FEAT = HEADS * HD
LOCAL_HEADS = 5
LOCAL = LOCAL_HEADS * HD
TILES = 8
EPSILON = 1e-06
NEG = -1e30
SCALE = HD ** (-0.5)
SCALE2 = SCALE * math.log2(math.e)
MESH = pl.DeviceIdType.MESH
VMEM_LIMIT = 60 * 1024 * 1024

UNITS = LOCAL_HEADS * NB


def my_unit():
    me = lax.axis_index("frame")
    slot = lax.rem(11 * (me // 2), 16)
    return me, slot < 2 * LOCAL_HEADS, slot // 2, 2 * lax.rem(slot, 2) + lax.rem(me, 2)


KIND_FAR = [(-4, 3), (-4, 4), (-2, 2), (-2, 3), (2, 2), (2, 3), (4, 3), (4, 4), (-1, 2), (1, 2), (-1, 1), (1, 1)]
OPEN = 6
SHUT = OPEN + 1 + len(KIND_FAR)
KINDS = SHUT + 1
MOST_BLOCKS = 18
TILE_BLOCKS = 8
EARLY_VALUES = 10


def far_kind(apart, level):
    return OPEN + 1 + KIND_FAR.index((apart, level))


def blocks_between(apart, over):
    def pick(plain, wrapped):
        return plain + over * (wrapped - plain)

    if apart == 0:
        return [(part, part, 1 + part) for part in range(4)]
    if apart == 1:
        return [
            (4, pick(0, 6), pick(5, OPEN)),
            (5, 4, pick(far_kind(1, 2), SHUT)),
            (6, 7, pick(far_kind(1, 1), SHUT)),
        ]
    if apart == 7:
        return [
            (7, pick(3, 6), pick(0, OPEN)),
            (8, 4, pick(far_kind(-1, 2), SHUT)),
            (9, 7, pick(far_kind(-1, 1), SHUT)),
        ]
    if apart == 2:
        return [(10, pick(4, 6), pick(far_kind(2, 2), OPEN)), (11, 5, pick(far_kind(2, 3), SHUT))]
    if apart == 3:
        return [(12, pick(5, 6), OPEN)]
    if apart == 4:
        return [(10 + level, 2 + level, pick(far_kind(4, level), far_kind(-4, level))) for level in (3, 4)]
    if apart == 5:
        return [(15, pick(6, 5), OPEN)]
    return [(16, pick(6, 4), pick(OPEN, far_kind(-2, 2))), (17, 5, pick(SHUT, far_kind(-2, 3)))]


def wrapped(tile, apart):
    over = (tile + apart) // TILES
    return 1 - over if apart == 7 else over


def greet():
    barrier = pltpu.get_barrier_semaphore()
    me = lax.axis_index("frame")
    row = lax.axis_index("head")
    for step in range(1, FRAMES):
        pl.semaphore_signal(
            barrier, inc=1, device_id={"frame": lax.rem(me + step, FRAMES)}, device_id_type=MESH
        )
    for step in range(1, 4):
        pl.semaphore_signal(
            barrier, inc=1, device_id={"head": lax.rem(row + step, 4)}, device_id_type=MESH
        )


def all_here():
    pl.semaphore_wait(pltpu.get_barrier_semaphore(), FRAMES - 1 + 3)


def pair_rows(first, second):
    lane = lax.broadcasted_iota(jnp.int32, (TOK, TOK), 1)
    both = jnp.where(lane == 0, first, jnp.where(lane == 1, second, 0.0))
    return both.T[:8]


def pair_columns(rows):
    full = jnp.concatenate([rows, jnp.zeros((TOK - 8, TOK), jnp.float32)], axis=0).T
    return full[:, 0:1], full[:, 1:2]


def head_sum(stat, slots, send_sem, recv_sem):
    row = lax.axis_index("head")
    copies = []
    for step in range(1, 4):
        copy = pltpu.make_async_remote_copy(
            src_ref=stat,
            dst_ref=slots.at[step - 1],
            send_sem=send_sem.at[step - 1],
            recv_sem=recv_sem.at[step - 1],
            device_id={"head": lax.rem(row + step, 4)},
            device_id_type=MESH,
        )
        copy.start()
        copies.append(copy)
    return copies


def head_slice(head):
    return pl.ds(head * HD, HD)


def lanes(head):
    return pl.ds(pl.multiple_of(head * HD, HD), HD)


def dot(a, b, contract):
    return lax.dot_general(a, b, (contract, ((), ())), preferred_element_type=jnp.float32)


def frame_rows(frame, width=TOK):
    return pl.ds(pl.multiple_of(frame * width, width), width)


def frame_block(frame):
    return TILE_BLOCKS * (frame // 4) + lax.rem(frame, 4)


def main_kernel(
    offset_ref, q_ref, k_ref, v_ref, g_ref, qgain_ref, kgain_ref,
    qgrad, kgrad, vgrad, total_ref, inner_ref,
    keys, queries, stat, slots, stat2, slots2,
    kv, kt, w, acc, bias, tbuf, gbuf, grads, lows, peaks, totals, weighteds,
    dq_done, given, other, keep, mixed, dkv_in, dq_in,
    zsend, zrecv, zsend2, zrecv2, vsend, gsend, ksend, qsend, vrecv, grecv, krecv, qrecv, vpass, kpass,
    give_send, give_recv, kvsend, dqsend, kvrecv, dqrecv,
):
    me, is_unit, my_head, block = my_unit()
    core = lax.rem(me, 2)
    partner = me + 1 - 2 * core
    slot_id = 2 * my_head + block // 2
    unit = my_head * NB + block

    def squares(ref):
        sums = jnp.zeros((TOK, HD), jnp.float32)
        for head in range(LOCAL_HEADS):
            part = ref[:, head_slice(head)].astype(jnp.float32)
            sums = sums + part * part
        return jnp.sum(sums, axis=1, keepdims=True)

    greet()
    stat[...] = pair_rows(squares(q_ref), squares(k_ref))
    all_here()
    sums = head_sum(stat, slots, zsend, zrecv)

    def k_at(frame):
        return kv.at[frame_rows(frame_block(frame)), pl.ds(0, HD)]

    def v_at(frame):
        return kv.at[frame_rows(frame_block(frame)), pl.ds(HD, HD)]

    def q_at(frame):
        return w.at[frame // 4, frame_rows(lax.rem(frame, 4), BLK), pl.ds(0, HD)]

    def g_at(frame):
        return w.at[frame // 4, frame_rows(4 + lax.rem(frame, 4), BLK), pl.ds(HD, HD)]

    def remote(src, place, target, send_sem, recv_sem):
        return pltpu.make_async_remote_copy(
            src_ref=src, dst_ref=place(me), send_sem=send_sem, recv_sem=recv_sem.at[me],
            device_id={"frame": target}, device_id_type=MESH,
        )

    def send(src, place, target, send_sem, recv_sem):
        @pl.when(me != target)
        def _():
            remote(src, place, target, send_sem, recv_sem).start()

        @pl.when(me == target)
        def _():
            pltpu.make_async_copy(src, place(me), recv_sem.at[me]).start()

    def key_part(slot, source, place, ssem, rsem):
        return source(slot // 2), place, 2 * lax.rem(3 * slot, 16) + core, ssem.at[slot], rsem

    def query_part(slot, side, source, place, ssem, rsem):
        rows = frame_rows(2 * lax.rem(slot, 2) + side, BLK)
        return source(slot // 2, rows), place, 2 * lax.rem(3 * slot, 16) + side, ssem.at[2 * slot + side], rsem

    def parts_v(slot):
        return (key_part(slot, lambda head: v_ref.at[:, lanes(head)], v_at, vsend, vrecv),)

    def parts_g(slot):
        return tuple(
            query_part(slot, side, lambda head, rows: g_ref.at[rows, lanes(head)], g_at, gsend, grecv)
            for side in range(2)
        )

    def parts_k(slot):
        return (key_part(slot, lambda head: keys.at[head], k_at, ksend, krecv),)

    def parts_q(slot):
        return tuple(
            query_part(slot, side, lambda head, rows: queries.at[head, rows], q_at, qsend, qrecv)
            for side in range(2)
        )

    turn = me // 4 + me // 16

    def send_steps(first, last, *kinds):
        @pl.loop(first, last)
        def _(step):
            for kind in kinds:
                for part in kind(lax.rem(step + turn, 2 * LOCAL_HEADS)):
                    send(*part)

    send_steps(0, 2 * LOCAL_HEADS, parts_g)
    send_steps(0, EARLY_VALUES, parts_v)

    for copy in sums:
        copy.wait()
    total = stat[...] + slots[0] + slots[1] + slots[2]
    total_ref[...] = total
    qsum, ksum = pair_columns(total)
    qrms = lax.rsqrt(qsum / FEAT + EPSILON)
    krms = lax.rsqrt(ksum / FEAT + EPSILON)
    for head in range(LOCAL_HEADS):
        part = k_ref[:, head_slice(head)].astype(jnp.float32)
        keys[head] = (part * krms * kgain_ref[head_slice(head)].reshape(1, HD)).astype(jnp.bfloat16)
        part = q_ref[:, head_slice(head)].astype(jnp.float32)
        queries[head] = (part * qrms * qgain_ref[head_slice(head)].reshape(1, HD)).astype(jnp.bfloat16)

    send_steps(0, 2 * LOCAL_HEADS, parts_k)
    send_steps(0, 2 * LOCAL_HEADS, parts_q)

    def forward(place, step, send_sem, recv_sem):
        frame = 2 * step + core
        return pltpu.make_async_remote_copy(
            src_ref=place(frame), dst_ref=place(frame), send_sem=send_sem.at[step],
            recv_sem=recv_sem.at[frame], device_id={"frame": partner}, device_id_type=MESH,
        )

    def arrived(place, frame, sem):
        pltpu.make_async_copy(place(frame), place(frame), sem.at[frame]).wait()

    def give(pair):
        return pltpu.make_async_remote_copy(
            src_ref=given.at[pair], dst_ref=other.at[pair], send_sem=give_send.at[pair],
            recv_sem=give_recv.at[pair], device_id={"frame": partner}, device_id_type=MESH,
        )

    def send_dq(frame):
        return pltpu.make_async_remote_copy(
            src_ref=dq_done.at[frame], dst_ref=dq_in.at[unit], send_sem=dqsend.at[frame],
            recv_sem=dqrecv.at[unit], device_id={"frame": frame}, device_id_type=MESH,
        )

    def send_dkv(pair):
        return pltpu.make_async_remote_copy(
            src_ref=mixed.at[pair], dst_ref=dkv_in.at[slot_id], send_sem=kvsend.at[pair],
            recv_sem=kvrecv.at[slot_id], device_id={"frame": 2 * pair + core}, device_id_type=MESH,
        )

    @pl.when(is_unit)
    def _():
        row_frame = lax.broadcasted_iota(jnp.int32, (TOK, TOK), 0) // BLK
        lane_frame = lax.broadcasted_iota(jnp.int32, (TOK, TOK), 1) // BLK
        zero = jnp.zeros((TOK, TOK), jnp.float32)
        hit1 = jnp.where(((row_frame - block - offset_ref[0]) & 3) < 2, 0.0, NEG)
        hit2 = jnp.where(((row_frame - block - offset_ref[1]) & 3) < 1, 0.0, NEG)

        @pl.loop(0, OPEN)
        def _(kind):
            d = jnp.abs(kind - 1 - lane_frame)
            bias[kind] = jnp.where(d < 2, 0.0, jnp.where(d < 4, hit1, hit2))

        bias[OPEN] = zero
        bias[SHUT] = zero + NEG
        for apart, level in KIND_FAR:
            frame = row_frame // 2 + 1 if level == 1 else row_frame
            d = jnp.abs(4 * apart + frame - lane_frame)
            meets = (d >= 2**level) & (d < 2 ** (level + 1))
            if level == 2 and abs(apart) == 1:
                meets = meets & (row_frame != (0 if apart == 1 else 3))
            bias[far_kind(apart, level)] = jnp.where(meets, 0.0, NEG)

        @pl.loop(0, TILES)
        def _(tile):
            w[tile, 0:TOK, HD:] = jnp.zeros((TOK, HD), jnp.bfloat16)
            w[tile, TOK:, 0:HD] = jnp.zeros((TOK, HD), jnp.bfloat16)

        def at_step(step, body):
            place = lax.rem(slot_id - step + 20, 10)

            @pl.when(lax.rem(place, 5) != 4)
            def _():
                body(place - place // 5)

        def pass_values(tile):
            for part in range(2):
                arrived(v_at, 4 * tile + 2 * part + core, vrecv)
                forward(v_at, 2 * tile + part, vpass, vrecv).start()

        @pl.loop(0, 10)
        def _(step):
            at_step(step, pass_values)

        def chosen(level, after):
            pick = (block + offset_ref[level - 1] + after) & 3
            return [(1 - jnp.minimum((pick - which) & 3, 1)).astype(jnp.float32) for which in range(NB)]

        moves = [(4 + index, part, part, chosen(2 + index, 0)) for index in range(3) for part in range(4)]
        moves += [(7, 2 * part + after, 1 + part, chosen(1, after)) for part in range(2) for after in range(2)]

        def pass_keys(tile):
            for part in range(2):
                arrived(k_at, 4 * tile + 2 * part + core, krecv)
                forward(k_at, 2 * tile + part, kpass, krecv).start()

        def score(tile):
            for part in range(2):
                frame = 4 * tile + 2 * part + 1 - core
                arrived(v_at, frame, vrecv)
                arrived(k_at, frame, krecv)
            base = TILE_BLOCKS * tile
            for to, place, frame, weights in moves:
                picked = kv[frame_rows(NB * (base + frame), BLK), :] * weights[0].astype(jnp.bfloat16)
                for which in range(1, NB):
                    rows = frame_rows(NB * (base + frame) + which, BLK)
                    picked = picked + kv[rows, :] * weights[which].astype(jnp.bfloat16)
                kv[frame_rows(NB * (base + to) + place, BLK), :] = picked
            for part in range(TILE_BLOCKS):
                kt[base + part] = kv[frame_rows(base + part), 0:HD].T
            for apart in range(TILES):
                asker = lax.rem(tile + TILES - apart, TILES)
                found = blocks_between(apart, wrapped(asker, apart))
                rows = jnp.concatenate([kv[frame_rows(base + blk), :] for _, blk, _ in found], axis=0)
                both = dot(rows, w[asker], ((1,), (1,)))
                for index, (slot, _, kind) in enumerate(found):
                    part = both[index * TOK : (index + 1) * TOK]
                    t = (part[:, 0:TOK] * SCALE2 + bias[kind]).reshape(16, 8, TOK)
                    grad = part[:, TOK:].reshape(16, 8, TOK)
                    peak = jnp.max(t, axis=0)
                    weight = jnp.exp2(t - peak)
                    tbuf[asker, slot] = weight.reshape(TOK, TOK)
                    gbuf[asker, slot] = part[:, TOK:]
                    peaks[asker, slot] = peak
                    totals[asker, slot] = jnp.sum(weight, axis=0)
                    weighteds[asker, slot] = jnp.sum(weight * grad, axis=0)

        @pl.loop(0, 10)
        def _(step):
            at_step(step, pass_keys)

        @pl.loop(0, FRAMES)
        def _(frame):
            arrived(g_at, frame, grecv)
            arrived(q_at, frame, qrecv)

        @pl.loop(0, 10)
        def _(step):
            at_step(step, score)

        @pl.loop(0, TILES)
        def _(tile):
            peak = jnp.max(jnp.max(peaks[tile], axis=0), axis=0, keepdims=True)
            factor = jnp.exp2(peaks[tile] - peak)
            total = jnp.sum(jnp.sum(totals[tile] * factor, axis=0), axis=0, keepdims=True)
            weighted = jnp.sum(jnp.sum(weighteds[tile] * factor, axis=0), axis=0, keepdims=True)
            inverse = 1.0 / total
            delta = weighted * inverse
            factor = factor * inverse
            for slot in range(MOST_BLOCKS):
                probs = (tbuf[tile, slot].reshape(16, 8, TOK) * factor[slot]).reshape(TOK, TOK)
                grad = probs * (gbuf[tile, slot] - delta)
                high = grad.astype(jnp.bfloat16)
                grads[tile, slot, :, 0:TOK] = high
                grads[tile, slot, :, TOK:] = probs.astype(jnp.bfloat16)
                lows[tile, slot] = (grad - high.astype(jnp.float32)).astype(jnp.bfloat16)

        def key_grads(tile):
            for index in range(4, TILE_BLOCKS):
                acc[index] = jnp.zeros((TOK, 2 * HD), jnp.float32)
            for apart in range(TILES):
                asker = lax.rem(tile + TILES - apart, TILES)
                found = blocks_between(apart, wrapped(asker, apart))
                left = jnp.concatenate([grads[asker, slot] for slot, _, _ in found], axis=0)
                both = dot(left, w[asker], ((1,), (0,)))
                for index, (_, blk, _) in enumerate(found):
                    piece = both[index * TOK : (index + 1) * TOK]
                    if apart == 0:
                        acc[blk] = piece
                    else:
                        acc[blk] += piece
            for frame in range(4):
                for which in range(NB):
                    piece = acc[frame, which * BLK : (which + 1) * BLK]
                    for source, place, target, weights in moves:
                        if target == frame:
                            piece = piece + acc[source, place * BLK : (place + 1) * BLK] * weights[which]
                    acc[frame, which * BLK : (which + 1) * BLK] = piece
            for part in range(2):
                pair = 2 * tile + part
                given[pair] = acc[2 * part + 1 - core].astype(jnp.bfloat16)
                give(pair).start()
                keep[pair] = acc[2 * part + core]

        def query_grads(tile):
            total = jnp.zeros((HD, 2 * TOK), jnp.float32)
            for apart in range(TILES):
                base = TILE_BLOCKS * lax.rem(tile + apart, TILES)
                found = blocks_between(apart, wrapped(tile, apart))
                keyt = jnp.concatenate([kt[base + blk] for _, blk, _ in found], axis=1)
                right = jnp.concatenate(
                    [
                        jnp.concatenate([grads[tile, slot, :, 0:TOK], lows[tile, slot]], axis=1)
                        for slot, _, _ in found
                    ],
                    axis=0,
                )
                total = total + dot(keyt, right, ((1,), (0,)))
            dq = (total[:, 0:TOK] + total[:, TOK:]).T.astype(jnp.bfloat16)
            for part in range(4):
                frame = 4 * tile + part
                dq_done[frame] = dq[part * BLK : (part + 1) * BLK]

                @pl.when(frame != me)
                def _():
                    send_dq(frame).start()

                @pl.when(frame == me)
                def _():
                    pltpu.make_async_copy(dq_done.at[frame], dq_in.at[unit], dqrecv.at[unit]).start()

        def mix(tile):
            for part in range(2):
                pair = 2 * tile + part
                give(pair).wait_recv()
                mixed[pair] = (keep[pair] + other[pair].astype(jnp.float32)).astype(jnp.bfloat16)

                @pl.when(2 * pair + core != me)
                def _():
                    send_dkv(pair).start()

                @pl.when(2 * pair + core == me)
                def _():
                    pltpu.make_async_copy(mixed.at[pair], dkv_in.at[slot_id], kvrecv.at[slot_id]).start()

        def turned(step):
            x = lax.rem(me // 8 + step + 1, 4)
            return 2 * x + lax.rem(step // 4 + slot_id, 2)

        key_grads(turned(0))

        @pl.loop(1, TILES)
        def _(step):
            key_grads(turned(step))
            mix(turned(step - 1))
            query_grads(turned(step - 1))

        mix(turned(TILES - 1))
        query_grads(turned(TILES - 1))

    qinner = jnp.zeros((TOK, HD), jnp.float32)
    kinner = jnp.zeros((TOK, HD), jnp.float32)
    for h in range(LOCAL_HEADS):
        for b in range(NB):
            u = h * NB + b
            pltpu.make_async_copy(dq_in.at[u], dq_in.at[u], dqrecv.at[u]).wait()
        dq = dq_in[pl.ds(h * NB, NB)].astype(jnp.float32).reshape(TOK, HD)
        gained = qgain_ref[head_slice(h)].reshape(1, HD) * (dq * SCALE)
        qgrad[:, head_slice(h)] = gained
        qinner = qinner + gained * q_ref[:, head_slice(h)].astype(jnp.float32)
    for h in range(LOCAL_HEADS):
        for u in (2 * h, 2 * h + 1):
            pltpu.make_async_copy(dkv_in.at[u], dkv_in.at[u], kvrecv.at[u]).wait()
        both = dkv_in[2 * h].astype(jnp.float32) + dkv_in[2 * h + 1].astype(jnp.float32)
        vgrad[:, head_slice(h)] = both[:, HD:].astype(jnp.bfloat16)
        gained = kgain_ref[head_slice(h)].reshape(1, HD) * (both[:, 0:HD] * SCALE)
        kgrad[:, head_slice(h)] = gained
        kinner = kinner + gained * k_ref[:, head_slice(h)].astype(jnp.float32)
    stat2[...] = pair_rows(
        jnp.sum(qinner, axis=1, keepdims=True), jnp.sum(kinner, axis=1, keepdims=True)
    )
    for copy in head_sum(stat2, slots2, zsend2, zrecv2):
        copy.wait()
    inner_ref[...] = stat2[...] + slots2[0] + slots2[1] + slots2[2]

    @pl.loop(0, 2 * LOCAL_HEADS)
    def _(slot):
        for parts in (parts_v(slot), parts_g(slot), parts_k(slot), parts_q(slot)):
            for src, place, target, ssem, rsem in parts:
                @pl.when(me != target)
                def _():
                    remote(src, place, target, ssem, rsem).wait_send()

    @pl.when(is_unit)
    def _():
        @pl.loop(0, FRAMES)
        def _(frame):
            @pl.when(frame != me)
            def _():
                send_dq(frame).wait_send()

        @pl.loop(0, FRAMES // 2)
        def _(pair):
            forward(v_at, pair, vpass, vrecv).wait_send()
            forward(k_at, pair, kpass, krecv).wait_send()
            give(pair).wait_send()

            @pl.when(2 * pair + core != me)
            def _():
                send_dkv(pair).wait_send()


def finish_kernel(q_ref, k_ref, qgrad, kgrad, vgrad, total_ref, inner_ref, dq_out, dk_out, dv_out):
    qsum, ksum = pair_columns(total_ref[...])
    qdot, kdot = pair_columns(inner_ref[...])
    for raw, grad, square, inner, out in (
        (q_ref, qgrad, qsum, qdot, dq_out),
        (k_ref, kgrad, ksum, kdot, dk_out),
    ):
        rms = lax.rsqrt(square / FEAT + EPSILON)
        factor = rms * rms * rms / FEAT * inner
        for head in range(LOCAL_HEADS):
            at = head_slice(head)
            out[:, at] = (rms * grad[:, at] - factor * raw[:, at].astype(jnp.float32)).astype(jnp.bfloat16)
    dv_out[...] = vgrad[...]


def local(query_raw, key_raw, values, query_gain, key_gain, out_grad, window_offset):
    bf16, f32 = jnp.bfloat16, jnp.float32
    vmem = pl.BlockSpec(memory_space=pltpu.VMEM)
    smem = pl.BlockSpec(memory_space=pltpu.SMEM)
    dma = pltpu.SemaphoreType.DMA
    shape = jax.ShapeDtypeStruct
    half = FRAMES // 2
    qgrad, kgrad, vgrad, total, inner = pl.pallas_call(
        main_kernel,
        name="band_grads",
        out_shape=(
            shape((TOK, LOCAL), f32),
            shape((TOK, LOCAL), f32),
            shape((TOK, LOCAL), bf16),
            shape((8, TOK), f32),
            shape((8, TOK), f32),
        ),
        in_specs=[smem] + [vmem] * 6,
        out_specs=[vmem] * 5,
        scratch_shapes=[
            pltpu.VMEM((LOCAL_HEADS, TOK, HD), bf16),
            pltpu.VMEM((LOCAL_HEADS, TOK, HD), bf16),
            pltpu.VMEM((8, TOK), f32),
            pltpu.VMEM((3, 8, TOK), f32),
            pltpu.VMEM((8, TOK), f32),
            pltpu.VMEM((3, 8, TOK), f32),
            pltpu.VMEM((TILES * TILE_BLOCKS * TOK, 2 * HD), bf16),
            pltpu.VMEM((TILES * TILE_BLOCKS, HD, TOK), bf16),
            pltpu.VMEM((TILES, 2 * TOK, 2 * HD), bf16),
            pltpu.VMEM((TILE_BLOCKS, TOK, 2 * HD), f32),
            pltpu.VMEM((KINDS, TOK, TOK), f32),
            pltpu.VMEM((TILES, MOST_BLOCKS, TOK, TOK), f32),
            pltpu.VMEM((TILES, MOST_BLOCKS, TOK, TOK), f32),
            pltpu.VMEM((TILES, MOST_BLOCKS, TOK, 2 * TOK), bf16),
            pltpu.VMEM((TILES, MOST_BLOCKS, TOK, TOK), bf16),
            pltpu.VMEM((TILES, MOST_BLOCKS, 8, TOK), f32),
            pltpu.VMEM((TILES, MOST_BLOCKS, 8, TOK), f32),
            pltpu.VMEM((TILES, MOST_BLOCKS, 8, TOK), f32),
            pltpu.VMEM((FRAMES, BLK, HD), bf16),
            pltpu.VMEM((half, TOK, 2 * HD), bf16),
            pltpu.VMEM((half, TOK, 2 * HD), bf16),
            pltpu.VMEM((half, TOK, 2 * HD), f32),
            pltpu.VMEM((half, TOK, 2 * HD), bf16),
            pltpu.VMEM((UNITS // 2, TOK, 2 * HD), bf16),
            pltpu.VMEM((UNITS, BLK, HD), bf16),
            dma((3,)), dma((3,)), dma((3,)), dma((3,)),
            dma((UNITS // 2,)), dma((UNITS,)), dma((UNITS // 2,)), dma((UNITS,)),
            dma((FRAMES,)), dma((FRAMES,)), dma((FRAMES,)), dma((FRAMES,)),
            dma((half,)), dma((half,)), dma((half,)), dma((half,)),
            dma((half,)), dma((FRAMES,)), dma((UNITS // 2,)), dma((UNITS,)),
        ],
        compiler_params=pltpu.CompilerParams(
            collective_id=0, has_side_effects=True, vmem_limit_bytes=VMEM_LIMIT
        ),
    )(window_offset, query_raw, key_raw, values, out_grad, query_gain, key_gain)
    return pl.pallas_call(
        finish_kernel,
        name="norm_grads",
        out_shape=(shape((TOK, LOCAL), bf16),) * 3,
        in_specs=[vmem] * 7,
        out_specs=[vmem] * 3,
    )(query_raw, key_raw, qgrad, kgrad, vgrad, total, inner)


def solution(mesh):
    placed = (
        P("frame", "head"),
        P("frame", "head"),
        P("frame", "head"),
        P("head"),
        P("head"),
        P("frame", "head"),
        P(),
    )
    return jax.shard_map(
        local,
        mesh=mesh,
        in_specs=placed,
        out_specs=(P("frame", "head"), P("frame", "head"), P("frame", "head")),
        check_vma=False,
    )
```

```python
import functools
import math

import jax
import jax.numpy as jnp
from jax import lax
from jax.experimental import pallas as pl
from jax.experimental.pallas import tpu as pltpu
from jax.sharding import PartitionSpec as P

HEADS = 20
HD = 128
NB = 4
TOK = 128
BLK = 32
FRAMES = 32
FEAT = HEADS * HD
LOCAL_HEADS = 5
LOCAL = LOCAL_HEADS * HD
TILES = 8
EPSILON = 1e-06
NEG = -1e30
SCALE = HD ** (-0.5)
SCALE2 = SCALE * math.log2(math.e)
MESH = pl.DeviceIdType.MESH
VMEM_LIMIT = 60 * 1024 * 1024

UNITS = LOCAL_HEADS * NB


def my_unit():
    me = lax.axis_index("frame")
    slot = lax.rem(11 * (me // 2), 16)
    return me, slot < 2 * LOCAL_HEADS, slot // 2, 2 * lax.rem(slot, 2) + lax.rem(me, 2)


KIND_FAR = [(-4, 3), (-4, 4), (-2, 2), (-2, 3), (2, 2), (2, 3), (4, 3), (4, 4), (-1, 2), (1, 2), (-1, 1), (1, 1)]
OPEN = 6
SHUT = OPEN + 1 + len(KIND_FAR)
KINDS = SHUT + 1
MOST_BLOCKS = 18
TILE_BLOCKS = 8
EARLY_VALUES = 10


def far_kind(apart, level):
    return OPEN + 1 + KIND_FAR.index((apart, level))


def blocks_between(apart, over):
    def pick(plain, wrapped):
        return plain + over * (wrapped - plain)

    if apart == 0:
        return [(part, part, 1 + part) for part in range(4)]
    if apart == 1:
        return [
            (4, pick(0, 6), pick(5, OPEN)),
            (5, 4, pick(far_kind(1, 2), SHUT)),
            (6, 7, pick(far_kind(1, 1), SHUT)),
        ]
    if apart == 7:
        return [
            (7, pick(3, 6), pick(0, OPEN)),
            (8, 4, pick(far_kind(-1, 2), SHUT)),
            (9, 7, pick(far_kind(-1, 1), SHUT)),
        ]
    if apart == 2:
        return [(10, pick(4, 6), pick(far_kind(2, 2), OPEN)), (11, 5, pick(far_kind(2, 3), SHUT))]
    if apart == 3:
        return [(12, pick(5, 6), OPEN)]
    if apart == 4:
        return [(10 + level, 2 + level, pick(far_kind(4, level), far_kind(-4, level))) for level in (3, 4)]
    if apart == 5:
        return [(15, pick(6, 5), OPEN)]
    return [(16, pick(6, 4), pick(OPEN, far_kind(-2, 2))), (17, 5, pick(SHUT, far_kind(-2, 3)))]


def wrapped(tile, apart):
    over = (tile + apart) // TILES
    return 1 - over if apart == 7 else over


def greet():
    barrier = pltpu.get_barrier_semaphore()
    me = lax.axis_index("frame")
    row = lax.axis_index("head")
    for step in range(1, FRAMES):
        pl.semaphore_signal(
            barrier, inc=1, device_id={"frame": lax.rem(me + step, FRAMES)}, device_id_type=MESH
        )
    for step in range(1, 4):
        pl.semaphore_signal(
            barrier, inc=1, device_id={"head": lax.rem(row + step, 4)}, device_id_type=MESH
        )


def all_here():
    pl.semaphore_wait(pltpu.get_barrier_semaphore(), FRAMES - 1 + 3)


def pair_rows(first, second):
    lane = lax.broadcasted_iota(jnp.int32, (TOK, TOK), 1)
    both = jnp.where(lane == 0, first, jnp.where(lane == 1, second, 0.0))
    return both.T[:8]


def pair_columns(rows):
    full = jnp.concatenate([rows, jnp.zeros((TOK - 8, TOK), jnp.float32)], axis=0).T
    return full[:, 0:1], full[:, 1:2]


def head_sum(stat, slots, send_sem, recv_sem):
    row = lax.axis_index("head")
    copies = []
    for step in range(1, 4):
        copy = pltpu.make_async_remote_copy(
            src_ref=stat,
            dst_ref=slots.at[step - 1],
            send_sem=send_sem.at[step - 1],
            recv_sem=recv_sem.at[step - 1],
            device_id={"head": lax.rem(row + step, 4)},
            device_id_type=MESH,
        )
        copy.start()
        copies.append(copy)
    return copies


def head_slice(head):
    return pl.ds(head * HD, HD)


def lanes(head):
    return pl.ds(pl.multiple_of(head * HD, HD), HD)


def dot(a, b, contract):
    return lax.dot_general(a, b, (contract, ((), ())), preferred_element_type=jnp.float32)


def frame_rows(frame, width=TOK):
    return pl.ds(pl.multiple_of(frame * width, width), width)


def frame_block(frame):
    return TILE_BLOCKS * (frame // 4) + lax.rem(frame, 4)


def main_kernel(
    offset_ref, q_ref, k_ref, v_ref, g_ref, qgain_ref, kgain_ref,
    qgrad, kgrad, vgrad, total_ref, inner_ref,
    keys, queries, stat, slots, stat2, slots2,
    kv, kt, w, acc, bias, tbuf, gbuf, grads, peaks, totals, weighteds,
    dq_done, given, other, keep, mixed, dkv_in, dq_in,
    zsend, zrecv, zsend2, zrecv2, home_send, vrecv, krecv, qrecv, pass_send, pass_recv,
    give_send, give_recv, kvsend, dqsend, kvrecv, dqrecv,
):
    me, is_unit, my_head, block = my_unit()
    core = lax.rem(me, 2)
    partner = me + 1 - 2 * core
    slot_id = 2 * my_head + block // 2
    unit = my_head * NB + block

    def squares(ref):
        sums = jnp.zeros((TOK, HD), jnp.float32)
        for head in range(LOCAL_HEADS):
            part = ref[:, head_slice(head)].astype(jnp.float32)
            sums = sums + part * part
        return jnp.sum(sums, axis=1, keepdims=True)

    greet()
    stat[...] = pair_rows(squares(q_ref), squares(k_ref))
    all_here()
    sums = head_sum(stat, slots, zsend, zrecv)

    def k_at(frame):
        return kv.at[frame_rows(frame_block(frame)), pl.ds(0, HD)]

    def v_at(frame):
        return kv.at[frame_rows(frame_block(frame)), pl.ds(HD, HD)]

    def q_at(frame):
        return w.at[frame // 4, frame_rows(lax.rem(frame, 4), BLK), pl.ds(0, HD)]

    def g_at(frame):
        return w.at[frame // 4, frame_rows(4 + lax.rem(frame, 4), BLK), pl.ds(HD, HD)]

    def remote(src, place, target, recv_sem):
        return pltpu.make_async_remote_copy(
            src_ref=src, dst_ref=place(me), send_sem=home_send, recv_sem=recv_sem,
            device_id={"frame": target}, device_id_type=MESH,
        )

    def send(src, place, target, recv_sem):
        @pl.when(me != target)
        def _():
            remote(src, place, target, recv_sem).start()

        @pl.when(me == target)
        def _():
            pltpu.make_async_copy(src, place(me), recv_sem).start()

    def key_part(slot, source, place, rsem):
        return source(slot // 2), place, 2 * lax.rem(3 * slot, 16) + core, rsem.at[me // 2]

    def query_part(slot, side, source, place):
        rows = frame_rows(2 * lax.rem(slot, 2) + side, BLK)
        return source(slot // 2, rows), place, 2 * lax.rem(3 * slot, 16) + side, qrecv

    def parts_v(slot):
        return (key_part(slot, lambda head: v_ref.at[:, lanes(head)], v_at, vrecv),)

    def parts_g(slot):
        return tuple(
            query_part(slot, side, lambda head, rows: g_ref.at[rows, lanes(head)], g_at)
            for side in range(2)
        )

    def parts_k(slot):
        return (key_part(slot, lambda head: keys.at[head], k_at, krecv),)

    def parts_q(slot):
        return tuple(
            query_part(slot, side, lambda head, rows: queries.at[head, rows], q_at)
            for side in range(2)
        )

    turn = me // 4 + me // 16

    def send_steps(first, last, *kinds):
        @pl.loop(first, last)
        def _(step):
            for kind in kinds:
                for part in kind(lax.rem(step + turn, 2 * LOCAL_HEADS)):
                    send(*part)

    send_steps(0, 2 * LOCAL_HEADS, parts_g)
    send_steps(0, EARLY_VALUES, parts_v)

    for copy in sums:
        copy.wait()
    total = stat[...] + slots[0] + slots[1] + slots[2]
    total_ref[...] = total
    qsum, ksum = pair_columns(total)
    qrms = lax.rsqrt(qsum / FEAT + EPSILON)
    krms = lax.rsqrt(ksum / FEAT + EPSILON)
    for head in range(LOCAL_HEADS):
        part = k_ref[:, head_slice(head)].astype(jnp.float32)
        keys[head] = (part * krms * kgain_ref[head_slice(head)].reshape(1, HD)).astype(jnp.bfloat16)
        part = q_ref[:, head_slice(head)].astype(jnp.float32)
        queries[head] = (part * qrms * qgain_ref[head_slice(head)].reshape(1, HD)).astype(jnp.bfloat16)

    send_steps(0, 2 * LOCAL_HEADS, parts_k)
    send_steps(0, 2 * LOCAL_HEADS, parts_q)

    def forward(place, frame):
        return pltpu.make_async_remote_copy(
            src_ref=place(frame), dst_ref=place(frame), send_sem=pass_send, recv_sem=pass_recv,
            device_id={"frame": partner}, device_id_type=MESH,
        )

    def await_bytes(ref, sem):
        pltpu.make_async_copy(ref, ref, sem).wait()

    def give(pair):
        return pltpu.make_async_remote_copy(
            src_ref=given.at[pair], dst_ref=other.at[pair], send_sem=give_send,
            recv_sem=give_recv.at[pair], device_id={"frame": partner}, device_id_type=MESH,
        )

    def send_dq(frame):
        return pltpu.make_async_remote_copy(
            src_ref=dq_done.at[frame], dst_ref=dq_in.at[unit], send_sem=dqsend,
            recv_sem=dqrecv.at[my_head], device_id={"frame": frame}, device_id_type=MESH,
        )

    def send_dkv(pair):
        return pltpu.make_async_remote_copy(
            src_ref=mixed.at[pair], dst_ref=dkv_in.at[slot_id], send_sem=kvsend,
            recv_sem=kvrecv.at[my_head], device_id={"frame": 2 * pair + core}, device_id_type=MESH,
        )

    @pl.when(is_unit)
    def _():
        row_frame = lax.broadcasted_iota(jnp.int32, (TOK, TOK), 0) // BLK
        lane_frame = lax.broadcasted_iota(jnp.int32, (TOK, TOK), 1) // BLK
        zero = jnp.zeros((TOK, TOK), jnp.float32)
        hit1 = jnp.where(((row_frame - block - offset_ref[0]) & 3) < 2, 0.0, NEG)
        hit2 = jnp.where(((row_frame - block - offset_ref[1]) & 3) < 1, 0.0, NEG)

        @pl.loop(0, OPEN)
        def _(kind):
            d = jnp.abs(kind - 1 - lane_frame)
            bias[kind] = jnp.where(d < 2, 0.0, jnp.where(d < 4, hit1, hit2))

        bias[OPEN] = zero
        bias[SHUT] = zero + NEG
        for apart, level in KIND_FAR:
            frame = row_frame // 2 + 1 if level == 1 else row_frame
            d = jnp.abs(4 * apart + frame - lane_frame)
            meets = (d >= 2**level) & (d < 2 ** (level + 1))
            if level == 2 and abs(apart) == 1:
                meets = meets & (row_frame != (0 if apart == 1 else 3))
            bias[far_kind(apart, level)] = jnp.where(meets, 0.0, NEG)

        @pl.loop(0, TILES)
        def _(tile):
            w[tile, 0:TOK, HD:] = jnp.zeros((TOK, HD), jnp.bfloat16)
            w[tile, TOK:, 0:HD] = jnp.zeros((TOK, HD), jnp.bfloat16)

        def at_step(step, body):
            place = lax.rem(slot_id - step + 20, 10)

            @pl.when(lax.rem(place, 5) != 4)
            def _():
                body(place - place // 5)

        def passing(place, sem):
            def body(tile):
                for part in range(2):
                    frame = 4 * tile + 2 * part + core
                    await_bytes(place(frame), sem.at[frame // 2])
                    forward(place, frame).start()

            return body

        @pl.loop(0, 10)
        def _(step):
            at_step(step, passing(v_at, vrecv))

        def chosen(level, after):
            pick = (block + offset_ref[level - 1] + after) & 3
            return [(1 - jnp.minimum((pick - which) & 3, 1)).astype(jnp.float32) for which in range(NB)]

        moves = [(4 + index, part, part, chosen(2 + index, 0)) for index in range(3) for part in range(4)]
        moves += [(7, 2 * part + after, 1 + part, chosen(1, after)) for part in range(2) for after in range(2)]

        def score(tile):
            base = TILE_BLOCKS * tile
            for to, place, frame, weights in moves:
                picked = kv[frame_rows(NB * (base + frame), BLK), :] * weights[0].astype(jnp.bfloat16)
                for which in range(1, NB):
                    rows = frame_rows(NB * (base + frame) + which, BLK)
                    picked = picked + kv[rows, :] * weights[which].astype(jnp.bfloat16)
                kv[frame_rows(NB * (base + to) + place, BLK), :] = picked
            for part in range(TILE_BLOCKS):
                kt[base + part] = kv[frame_rows(base + part), 0:HD].T
            for apart in range(TILES):
                asker = lax.rem(tile + TILES - apart, TILES)
                found = blocks_between(apart, wrapped(asker, apart))
                rows = jnp.concatenate([kv[frame_rows(base + blk), :] for _, blk, _ in found], axis=0)
                both = dot(rows, w[asker], ((1,), (1,)))
                for index, (slot, _, kind) in enumerate(found):
                    part = both[index * TOK : (index + 1) * TOK]
                    t = (part[:, 0:TOK] * SCALE2 + bias[kind]).reshape(16, 8, TOK)
                    grad = part[:, TOK:].reshape(16, 8, TOK)
                    peak = jnp.max(t, axis=0)
                    weight = jnp.exp2(t - peak)
                    tbuf[asker, slot] = weight.reshape(TOK, TOK)
                    gbuf[asker, slot] = part[:, TOK:]
                    peaks[asker, slot] = peak
                    totals[asker, slot] = jnp.sum(weight, axis=0)
                    weighteds[asker, slot] = jnp.sum(weight * grad, axis=0)

        @pl.loop(0, 10)
        def _(step):
            at_step(step, passing(k_at, krecv))

        await_bytes(w.at[pl.ds(0, TILES // 2)], qrecv)
        await_bytes(kv.at[pl.ds(0, FRAMES * TOK // 2)], pass_recv)

        @pl.loop(0, 10)
        def _(step):
            at_step(step, score)

        def turned(step):
            x = lax.rem(me // 8 + step + 1, 4)
            return 2 * x + lax.rem(step // 4 + slot_id, 2)

        @pl.loop(0, TILES)
        def _(step):
            tile = turned(step)
            peak = jnp.max(jnp.max(peaks[tile], axis=0), axis=0, keepdims=True)
            factor = jnp.exp2(peaks[tile] - peak)
            total = jnp.sum(jnp.sum(totals[tile] * factor, axis=0), axis=0, keepdims=True)
            weighted = jnp.sum(jnp.sum(weighteds[tile] * factor, axis=0), axis=0, keepdims=True)
            inverse = 1.0 / total
            delta = weighted * inverse
            factor = factor * inverse
            total = jnp.zeros((HD, 2 * TOK), jnp.float32)
            for apart in range(TILES):
                base = TILE_BLOCKS * lax.rem(tile + apart, TILES)
                found = blocks_between(apart, wrapped(tile, apart))
                right = []
                for slot, _, _ in found:
                    probs = (tbuf[tile, slot].reshape(16, 8, TOK) * factor[slot]).reshape(TOK, TOK)
                    grad = probs * (gbuf[tile, slot] - delta)
                    high = grad.astype(jnp.bfloat16)
                    grads[tile, slot, :, 0:TOK] = high
                    grads[tile, slot, :, TOK:] = probs.astype(jnp.bfloat16)
                    low = (grad - high.astype(jnp.float32)).astype(jnp.bfloat16)
                    right.append(jnp.concatenate([high, low], axis=1))
                keyt = jnp.concatenate([kt[base + blk] for _, blk, _ in found], axis=1)
                total = total + dot(keyt, jnp.concatenate(right, axis=0), ((1,), (0,)))
            dq = (total[:, 0:TOK] + total[:, TOK:]).T.astype(jnp.bfloat16)
            for part in range(4):
                dq_done[4 * tile + part] = dq[part * BLK : (part + 1) * BLK]
            for part in range(4):
                frame = 4 * tile + part

                @pl.when(frame != me)
                def _():
                    send_dq(frame).start()

                @pl.when(frame == me)
                def _():
                    pltpu.make_async_copy(dq_done.at[frame], dq_in.at[unit], dqrecv.at[my_head]).start()

        def key_grads(tile):
            for index in range(4, TILE_BLOCKS):
                acc[index] = jnp.zeros((TOK, 2 * HD), jnp.float32)
            for apart in range(TILES):
                asker = lax.rem(tile + TILES - apart, TILES)
                found = blocks_between(apart, wrapped(asker, apart))
                left = jnp.concatenate([grads[asker, slot] for slot, _, _ in found], axis=0)
                both = dot(left, w[asker], ((1,), (0,)))
                for index, (_, blk, _) in enumerate(found):
                    piece = both[index * TOK : (index + 1) * TOK]
                    if apart == 0:
                        acc[blk] = piece
                    else:
                        acc[blk] += piece
            for frame in range(4):
                for which in range(NB):
                    piece = acc[frame, which * BLK : (which + 1) * BLK]
                    for source, place, target, weights in moves:
                        if target == frame:
                            piece = piece + acc[source, place * BLK : (place + 1) * BLK] * weights[which]
                    acc[frame, which * BLK : (which + 1) * BLK] = piece
            for part in range(2):
                pair = 2 * tile + part
                given[pair] = acc[2 * part + 1 - core].astype(jnp.bfloat16)
                give(pair).start()
                keep[pair] = acc[2 * part + core]

        def mix(tile):
            for part in range(2):
                pair = 2 * tile + part
                give(pair).wait_recv()
                mixed[pair] = (keep[pair] + other[pair].astype(jnp.float32)).astype(jnp.bfloat16)

                @pl.when(2 * pair + core != me)
                def _():
                    send_dkv(pair).start()

                @pl.when(2 * pair + core == me)
                def _():
                    pltpu.make_async_copy(mixed.at[pair], dkv_in.at[slot_id], kvrecv.at[my_head]).start()

        key_grads(turned(0))

        @pl.loop(1, TILES)
        def _(step):
            key_grads(turned(step))
            mix(turned(step - 1))

        mix(turned(TILES - 1))

    qinner = jnp.zeros((TOK, HD), jnp.float32)
    kinner = jnp.zeros((TOK, HD), jnp.float32)
    for h in range(LOCAL_HEADS):
        await_bytes(dq_in.at[pl.ds(h * NB, NB)], dqrecv.at[h])
        dq = dq_in[pl.ds(h * NB, NB)].astype(jnp.float32).reshape(TOK, HD)
        gained = qgain_ref[head_slice(h)].reshape(1, HD) * (dq * SCALE)
        qgrad[:, head_slice(h)] = gained
        qinner = qinner + gained * q_ref[:, head_slice(h)].astype(jnp.float32)
    for h in range(LOCAL_HEADS):
        await_bytes(dkv_in.at[pl.ds(2 * h, 2)], kvrecv.at[h])
        both = dkv_in[2 * h].astype(jnp.float32) + dkv_in[2 * h + 1].astype(jnp.float32)
        vgrad[:, head_slice(h)] = both[:, HD:].astype(jnp.bfloat16)
        gained = kgain_ref[head_slice(h)].reshape(1, HD) * (both[:, 0:HD] * SCALE)
        kgrad[:, head_slice(h)] = gained
        kinner = kinner + gained * k_ref[:, head_slice(h)].astype(jnp.float32)
    stat2[...] = pair_rows(
        jnp.sum(qinner, axis=1, keepdims=True), jnp.sum(kinner, axis=1, keepdims=True)
    )
    for copy in head_sum(stat2, slots2, zsend2, zrecv2):
        copy.wait()
    inner_ref[...] = stat2[...] + slots2[0] + slots2[1] + slots2[2]

    sent = 2 * (2 * LOCAL_HEADS) * TOK + 2 * UNITS * BLK
    kept = 2 * TOK + 2 * BLK

    @pl.when(jnp.logical_not(is_unit))
    def _():
        await_bytes(kv.at[pl.ds(0, sent // 2)], home_send)

    @pl.when(is_unit)
    def _():
        await_bytes(kv.at[pl.ds(0, (sent - kept) // 2)], home_send)
        await_bytes(kv.at[pl.ds(0, FRAMES * TOK // 2)], pass_send)
        await_bytes(dq_done.at[pl.ds(0, FRAMES - 1)], dqsend)
        await_bytes(given, give_send)
        await_bytes(mixed.at[pl.ds(0, FRAMES // 2 - 1)], kvsend)


def finish_kernel(q_ref, k_ref, qgrad, kgrad, vgrad, total_ref, inner_ref, dq_out, dk_out, dv_out):
    qsum, ksum = pair_columns(total_ref[...])
    qdot, kdot = pair_columns(inner_ref[...])
    for raw, grad, square, inner, out in (
        (q_ref, qgrad, qsum, qdot, dq_out),
        (k_ref, kgrad, ksum, kdot, dk_out),
    ):
        rms = lax.rsqrt(square / FEAT + EPSILON)
        factor = rms * rms * rms / FEAT * inner
        for head in range(LOCAL_HEADS):
            at = head_slice(head)
            out[:, at] = (rms * grad[:, at] - factor * raw[:, at].astype(jnp.float32)).astype(jnp.bfloat16)
    dv_out[...] = vgrad[...]


def local(query_raw, key_raw, values, query_gain, key_gain, out_grad, window_offset):
    bf16, f32 = jnp.bfloat16, jnp.float32
    vmem = pl.BlockSpec(memory_space=pltpu.VMEM)
    smem = pl.BlockSpec(memory_space=pltpu.SMEM)
    dma = pltpu.SemaphoreType.DMA
    shape = jax.ShapeDtypeStruct
    half = FRAMES // 2
    qgrad, kgrad, vgrad, total, inner = pl.pallas_call(
        main_kernel,
        name="band_grads",
        out_shape=(
            shape((TOK, LOCAL), f32),
            shape((TOK, LOCAL), f32),
            shape((TOK, LOCAL), bf16),
            shape((8, TOK), f32),
            shape((8, TOK), f32),
        ),
        in_specs=[smem] + [vmem] * 6,
        out_specs=[vmem] * 5,
        scratch_shapes=[
            pltpu.VMEM((LOCAL_HEADS, TOK, HD), bf16),
            pltpu.VMEM((LOCAL_HEADS, TOK, HD), bf16),
            pltpu.VMEM((8, TOK), f32),
            pltpu.VMEM((3, 8, TOK), f32),
            pltpu.VMEM((8, TOK), f32),
            pltpu.VMEM((3, 8, TOK), f32),
            pltpu.VMEM((TILES * TILE_BLOCKS * TOK, 2 * HD), bf16),
            pltpu.VMEM((TILES * TILE_BLOCKS, HD, TOK), bf16),
            pltpu.VMEM((TILES, 2 * TOK, 2 * HD), bf16),
            pltpu.VMEM((TILE_BLOCKS, TOK, 2 * HD), f32),
            pltpu.VMEM((KINDS, TOK, TOK), f32),
            pltpu.VMEM((TILES, MOST_BLOCKS, TOK, TOK), f32),
            pltpu.VMEM((TILES, MOST_BLOCKS, TOK, TOK), f32),
            pltpu.VMEM((TILES, MOST_BLOCKS, TOK, 2 * TOK), bf16),
            pltpu.VMEM((TILES, MOST_BLOCKS, 8, TOK), f32),
            pltpu.VMEM((TILES, MOST_BLOCKS, 8, TOK), f32),
            pltpu.VMEM((TILES, MOST_BLOCKS, 8, TOK), f32),
            pltpu.VMEM((FRAMES, BLK, HD), bf16),
            pltpu.VMEM((half, TOK, 2 * HD), bf16),
            pltpu.VMEM((half, TOK, 2 * HD), bf16),
            pltpu.VMEM((half, TOK, 2 * HD), f32),
            pltpu.VMEM((half, TOK, 2 * HD), bf16),
            pltpu.VMEM((UNITS // 2, TOK, 2 * HD), bf16),
            pltpu.VMEM((UNITS, BLK, HD), bf16),
            dma((3,)), dma((3,)), dma((3,)), dma((3,)),
            dma, dma((half,)), dma((half,)), dma, dma, dma,
            dma, dma((half,)),
            dma, dma, dma((LOCAL_HEADS,)), dma((LOCAL_HEADS,)),
        ],
        compiler_params=pltpu.CompilerParams(
            collective_id=0, has_side_effects=True, vmem_limit_bytes=VMEM_LIMIT
        ),
    )(window_offset, query_raw, key_raw, values, out_grad, query_gain, key_gain)
    return pl.pallas_call(
        finish_kernel,
        name="norm_grads",
        out_shape=(shape((TOK, LOCAL), bf16),) * 3,
        in_specs=[vmem] * 7,
        out_specs=[vmem] * 3,
    )(query_raw, key_raw, qgrad, kgrad, vgrad, total, inner)


def solution(mesh):
    placed = (
        P("frame", "head"),
        P("frame", "head"),
        P("frame", "head"),
        P("head"),
        P("head"),
        P("frame", "head"),
        P(),
    )
    return jax.shard_map(
        local,
        mesh=mesh,
        in_specs=placed,
        out_specs=(P("frame", "head"), P("frame", "head"), P("frame", "head")),
        check_vma=False,
    )
```

```python
import functools
import math

import jax
import jax.numpy as jnp
from jax import lax
from jax.experimental import pallas as pl
from jax.experimental.pallas import tpu as pltpu
from jax.sharding import PartitionSpec as P

HEADS = 20
HD = 128
NB = 4
TOK = 128
BLK = 32
FRAMES = 32
FEAT = HEADS * HD
LOCAL_HEADS = 5
LOCAL = LOCAL_HEADS * HD
TILES = 8
EPSILON = 1e-06
NEG = -1e30
SCALE = HD ** (-0.5)
SCALE2 = SCALE * math.log2(math.e)
MESH = pl.DeviceIdType.MESH
VMEM_LIMIT = 60 * 1024 * 1024

UNITS = LOCAL_HEADS * NB


def my_unit():
    me = lax.axis_index("frame")
    slot = lax.rem(11 * (me // 2), 16)
    return me, slot < 2 * LOCAL_HEADS, slot // 2, 2 * lax.rem(slot, 2) + lax.rem(me, 2)


KIND_FAR = [(-4, 3), (-4, 4), (-2, 2), (-2, 3), (2, 2), (2, 3), (4, 3), (4, 4), (-1, 2), (1, 2), (-1, 1), (1, 1)]
OPEN = 6
SHUT = OPEN + 1 + len(KIND_FAR)
KINDS = SHUT + 1
MOST_BLOCKS = 18
TILE_BLOCKS = 8
EARLY_VALUES = 10


def far_kind(apart, level):
    return OPEN + 1 + KIND_FAR.index((apart, level))


def blocks_between(apart, over):
    def pick(plain, wrapped):
        return plain + over * (wrapped - plain)

    if apart == 0:
        return [(part, part, 1 + part) for part in range(4)]
    if apart == 1:
        return [
            (4, pick(0, 6), pick(5, OPEN)),
            (5, 4, pick(far_kind(1, 2), SHUT)),
            (6, 7, pick(far_kind(1, 1), SHUT)),
        ]
    if apart == 7:
        return [
            (7, pick(3, 6), pick(0, OPEN)),
            (8, 4, pick(far_kind(-1, 2), SHUT)),
            (9, 7, pick(far_kind(-1, 1), SHUT)),
        ]
    if apart == 2:
        return [(10, pick(4, 6), pick(far_kind(2, 2), OPEN)), (11, 5, pick(far_kind(2, 3), SHUT))]
    if apart == 3:
        return [(12, pick(5, 6), OPEN)]
    if apart == 4:
        return [(10 + level, 2 + level, pick(far_kind(4, level), far_kind(-4, level))) for level in (3, 4)]
    if apart == 5:
        return [(15, pick(6, 5), OPEN)]
    return [(16, pick(6, 4), pick(OPEN, far_kind(-2, 2))), (17, 5, pick(SHUT, far_kind(-2, 3)))]


def wrapped(tile, apart):
    over = (tile + apart) // TILES
    return 1 - over if apart == 7 else over


def greet():
    barrier = pltpu.get_barrier_semaphore()
    me = lax.axis_index("frame")
    row = lax.axis_index("head")
    for step in range(1, FRAMES):
        pl.semaphore_signal(
            barrier, inc=1, device_id={"frame": lax.rem(me + step, FRAMES)}, device_id_type=MESH
        )
    for step in range(1, 4):
        pl.semaphore_signal(
            barrier, inc=1, device_id={"head": lax.rem(row + step, 4)}, device_id_type=MESH
        )


def all_here():
    pl.semaphore_wait(pltpu.get_barrier_semaphore(), FRAMES - 1 + 3)


def pair_rows(first, second):
    lane = lax.broadcasted_iota(jnp.int32, (TOK, TOK), 1)
    both = jnp.where(lane == 0, first, jnp.where(lane == 1, second, 0.0))
    return both.T[:8]


def pair_columns(rows):
    full = jnp.concatenate([rows, jnp.zeros((TOK - 8, TOK), jnp.float32)], axis=0).T
    return full[:, 0:1], full[:, 1:2]


def head_sum(stat, slots, send_sem, recv_sem):
    row = lax.axis_index("head")
    copies = []
    for step in range(1, 4):
        copy = pltpu.make_async_remote_copy(
            src_ref=stat,
            dst_ref=slots.at[step - 1],
            send_sem=send_sem.at[step - 1],
            recv_sem=recv_sem.at[step - 1],
            device_id={"head": lax.rem(row + step, 4)},
            device_id_type=MESH,
        )
        copy.start()
        copies.append(copy)
    return copies


def head_slice(head):
    return pl.ds(head * HD, HD)


def lanes(head):
    return pl.ds(pl.multiple_of(head * HD, HD), HD)


def dot(a, b, contract):
    return lax.dot_general(a, b, (contract, ((), ())), preferred_element_type=jnp.float32)


def frame_rows(frame, width=TOK):
    return pl.ds(pl.multiple_of(frame * width, width), width)


def frame_block(frame):
    return TILE_BLOCKS * (frame // 4) + lax.rem(frame, 4)


def main_kernel(
    offset_ref, q_hbm, k_hbm, v_hbm, g_hbm, qgain_ref, kgain_ref,
    qgrad, kgrad, vgrad, total_ref, inner_ref,
    q_ref, k_ref, v_ref, g_ref, load_sem, keys, queries, stat, slots, stat2, slots2,
    kv, kt, picks, w, acc, bias, tbuf, gbuf, grads, peaks, totals, weighteds,
    dq_done, given, other, keep, mixed, dkv_in, dq_in,
    zsend, zrecv, zsend2, zrecv2, home_send, vrecv, krecv, qrecv, pass_send, pass_recv,
    give_send, give_recv, kvsend, dqsend, kvrecv, dqrecv,
):
    me, is_unit, my_head, block = my_unit()
    core = lax.rem(me, 2)
    partner = me + 1 - 2 * core
    slot_id = 2 * my_head + block // 2
    unit = my_head * NB + block

    def squares(ref):
        sums = jnp.zeros((TOK, HD), jnp.float32)
        for head in range(LOCAL_HEADS):
            part = ref[:, head_slice(head)].astype(jnp.float32)
            sums = sums + part * part
        return jnp.sum(sums, axis=1, keepdims=True)

    loads = [
        pltpu.make_async_copy(src, dst, load_sem.at[index])
        for index, (src, dst) in enumerate(((q_hbm, q_ref), (k_hbm, k_ref), (v_hbm, v_ref), (g_hbm, g_ref)))
    ]
    for load in loads:
        load.start()
    greet()
    for load in loads:
        load.wait()
    stat[...] = pair_rows(squares(q_ref), squares(k_ref))
    all_here()
    sums = head_sum(stat, slots, zsend, zrecv)

    def k_at(frame):
        return kv.at[frame_rows(frame_block(frame)), pl.ds(0, HD)]

    def v_at(frame):
        return kv.at[frame_rows(frame_block(frame)), pl.ds(HD, HD)]

    def q_at(frame):
        return w.at[frame // 4, frame_rows(lax.rem(frame, 4), BLK), pl.ds(0, HD)]

    def g_at(frame):
        return w.at[frame // 4, frame_rows(4 + lax.rem(frame, 4), BLK), pl.ds(HD, HD)]

    def remote(src, place, target, recv_sem):
        return pltpu.make_async_remote_copy(
            src_ref=src, dst_ref=place(me), send_sem=home_send, recv_sem=recv_sem,
            device_id={"frame": target}, device_id_type=MESH,
        )

    def send(src, place, target, recv_sem):
        @pl.when(me != target)
        def _():
            remote(src, place, target, recv_sem).start()

        @pl.when(me == target)
        def _():
            pltpu.make_async_copy(src, place(me), recv_sem).start()

    def key_part(slot, source, place, rsem):
        return source(slot // 2), place, 2 * lax.rem(3 * slot, 16) + core, rsem.at[me // 2]

    def query_part(slot, side, source, place):
        rows = frame_rows(2 * lax.rem(slot, 2) + side, BLK)
        return source(slot // 2, rows), place, 2 * lax.rem(3 * slot, 16) + side, qrecv

    def parts_v(slot):
        return (key_part(slot, lambda head: v_ref.at[:, lanes(head)], v_at, vrecv),)

    def parts_g(slot):
        return tuple(
            query_part(slot, side, lambda head, rows: g_ref.at[rows, lanes(head)], g_at)
            for side in range(2)
        )

    def parts_k(slot):
        return (key_part(slot, lambda head: keys.at[head], k_at, krecv),)

    def parts_q(slot):
        return tuple(
            query_part(slot, side, lambda head, rows: queries.at[head, rows], q_at)
            for side in range(2)
        )

    turn = me // 4 + me // 16

    def send_steps(first, last, *kinds):
        @pl.loop(first, last)
        def _(step):
            for kind in kinds:
                for part in kind(lax.rem(step + turn, 2 * LOCAL_HEADS)):
                    send(*part)

    send_steps(0, 2 * LOCAL_HEADS, parts_g)
    send_steps(0, EARLY_VALUES, parts_v)

    for copy in sums:
        copy.wait()
    total = stat[...] + slots[0] + slots[1] + slots[2]
    total_ref[...] = total
    qsum, ksum = pair_columns(total)
    qrms = lax.rsqrt(qsum / FEAT + EPSILON)
    krms = lax.rsqrt(ksum / FEAT + EPSILON)
    for head in range(LOCAL_HEADS):
        part = k_ref[:, head_slice(head)].astype(jnp.float32)
        keys[head] = (part * krms * kgain_ref[head_slice(head)].reshape(1, HD)).astype(jnp.bfloat16)
        part = q_ref[:, head_slice(head)].astype(jnp.float32)
        queries[head] = (part * qrms * qgain_ref[head_slice(head)].reshape(1, HD)).astype(jnp.bfloat16)

    send_steps(0, 2 * LOCAL_HEADS, parts_k)
    send_steps(0, 2 * LOCAL_HEADS, parts_q)

    def forward(place, frame):
        return pltpu.make_async_remote_copy(
            src_ref=place(frame), dst_ref=place(frame), send_sem=pass_send, recv_sem=pass_recv,
            device_id={"frame": partner}, device_id_type=MESH,
        )

    def await_bytes(ref, sem):
        pltpu.make_async_copy(ref, ref, sem).wait()

    def give(pair):
        return pltpu.make_async_remote_copy(
            src_ref=given.at[pair], dst_ref=other.at[pair], send_sem=give_send,
            recv_sem=give_recv.at[pair], device_id={"frame": partner}, device_id_type=MESH,
        )

    def send_dq(frame):
        return pltpu.make_async_remote_copy(
            src_ref=dq_done.at[frame], dst_ref=dq_in.at[unit], send_sem=dqsend,
            recv_sem=dqrecv.at[my_head], device_id={"frame": frame}, device_id_type=MESH,
        )

    def send_dkv(pair):
        return pltpu.make_async_remote_copy(
            src_ref=mixed.at[pair], dst_ref=dkv_in.at[slot_id], send_sem=kvsend,
            recv_sem=kvrecv.at[my_head], device_id={"frame": 2 * pair + core}, device_id_type=MESH,
        )

    @pl.when(is_unit)
    def _():
        row_frame = lax.broadcasted_iota(jnp.int32, (TOK, TOK), 0) // BLK
        lane_frame = lax.broadcasted_iota(jnp.int32, (TOK, TOK), 1) // BLK
        zero = jnp.zeros((TOK, TOK), jnp.float32)
        hit1 = jnp.where(((row_frame - block - offset_ref[0]) & 3) < 2, 0.0, NEG)
        hit2 = jnp.where(((row_frame - block - offset_ref[1]) & 3) < 1, 0.0, NEG)

        @pl.loop(0, OPEN)
        def _(kind):
            d = jnp.abs(kind - 1 - lane_frame)
            bias[kind] = jnp.where(d < 2, 0.0, jnp.where(d < 4, hit1, hit2))

        bias[OPEN] = zero
        bias[SHUT] = zero + NEG
        for apart, level in KIND_FAR:
            frame = row_frame // 2 + 1 if level == 1 else row_frame
            d = jnp.abs(4 * apart + frame - lane_frame)
            meets = (d >= 2**level) & (d < 2 ** (level + 1))
            if level == 2 and abs(apart) == 1:
                meets = meets & (row_frame != (0 if apart == 1 else 3))
            bias[far_kind(apart, level)] = jnp.where(meets, 0.0, NEG)

        @pl.loop(0, TILES)
        def _(tile):
            w[tile, 0:TOK, HD:] = jnp.zeros((TOK, HD), jnp.bfloat16)
            w[tile, TOK:, 0:HD] = jnp.zeros((TOK, HD), jnp.bfloat16)

        def at_step(step, body):
            place = lax.rem(slot_id - step + 20, 10)

            @pl.when(lax.rem(place, 5) != 4)
            def _():
                body(place - place // 5)

        def passing(place, sem):
            def body(tile):
                for part in range(2):
                    frame = 4 * tile + 2 * part + core
                    await_bytes(place(frame), sem.at[frame // 2])
                    forward(place, frame).start()

            return body

        @pl.loop(0, 10)
        def _(step):
            at_step(step, passing(v_at, vrecv))

        def chosen(level, after):
            pick = (block + offset_ref[level - 1] + after) & 3
            return [(1 - jnp.minimum((pick - which) & 3, 1)).astype(jnp.float32) for which in range(NB)]

        moves = [(4 + index, part, part, chosen(2 + index, 0)) for index in range(3) for part in range(4)]
        moves += [(7, 2 * part + after, 1 + part, chosen(1, after)) for part in range(2) for after in range(2)]

        def score(tile):
            base = TILE_BLOCKS * tile
            for part in range(4):
                kt[base + part] = kv[frame_rows(base + part), 0:HD].T
            for to, place, frame, weights in moves:
                picked = kv[frame_rows(NB * (base + frame), BLK), :] * weights[0].astype(jnp.bfloat16)
                for which in range(1, NB):
                    rows = frame_rows(NB * (base + frame) + which, BLK)
                    picked = picked + kv[rows, :] * weights[which].astype(jnp.bfloat16)
                picks[to - 4, place * BLK : (place + 1) * BLK] = picked
            picks[4] = kv[frame_rows(base), :]
            picks[5] = kv[frame_rows(base + 3), :]
            for part in range(4, TILE_BLOCKS):
                kt[base + part] = picks[part - 4, :, 0:HD].T

            def operand(apart, over, index, blk):
                if apart == 0:
                    return kv[frame_rows(base + blk), :]
                if apart in (1, 7) and index == 0:
                    end = 4 if apart == 1 else 5
                    return picks[end + over * (2 - end)]
                return picks[blk - 4]

            for apart in range(TILES):
                asker = lax.rem(tile + TILES - apart, TILES)
                over = wrapped(asker, apart)
                found = blocks_between(apart, over)
                rows = jnp.concatenate(
                    [operand(apart, over, index, blk) for index, (_, blk, _) in enumerate(found)], axis=0
                )
                both = dot(rows, w[asker], ((1,), (1,)))
                for index, (slot, _, kind) in enumerate(found):
                    part = both[index * TOK : (index + 1) * TOK]
                    t = (part[:, 0:TOK] * SCALE2 + bias[kind]).reshape(16, 8, TOK)
                    grad = part[:, TOK:].reshape(16, 8, TOK)
                    peak = jnp.max(t, axis=0)
                    weight = jnp.exp2(t - peak)
                    tbuf[asker, slot] = weight.reshape(TOK, TOK)
                    gbuf[asker, slot] = part[:, TOK:]
                    peaks[asker, slot] = peak
                    totals[asker, slot] = jnp.sum(weight, axis=0)
                    weighteds[asker, slot] = jnp.sum(weight * grad, axis=0)

        @pl.loop(0, 10)
        def _(step):
            at_step(step, passing(k_at, krecv))

        await_bytes(w.at[pl.ds(0, TILES // 2)], qrecv)
        await_bytes(kv.at[pl.ds(0, FRAMES * TOK // 2)], pass_recv)

        @pl.loop(0, 10)
        def _(step):
            at_step(step, score)

        def turned(step):
            x = lax.rem(me // 8 + step + 1, 4)
            return 2 * x + lax.rem(step // 4 + slot_id, 2)

        @pl.loop(0, TILES)
        def _(step):
            tile = turned(step)
            peak = jnp.max(jnp.max(peaks[tile], axis=0), axis=0, keepdims=True)
            factor = jnp.exp2(peaks[tile] - peak)
            total = jnp.sum(jnp.sum(totals[tile] * factor, axis=0), axis=0, keepdims=True)
            weighted = jnp.sum(jnp.sum(weighteds[tile] * factor, axis=0), axis=0, keepdims=True)
            inverse = 1.0 / total
            delta = weighted * inverse
            factor = factor * inverse
            total = jnp.zeros((HD, 2 * TOK), jnp.float32)
            for apart in range(TILES):
                base = TILE_BLOCKS * lax.rem(tile + apart, TILES)
                found = blocks_between(apart, wrapped(tile, apart))
                right = []
                for slot, _, _ in found:
                    probs = (tbuf[tile, slot].reshape(16, 8, TOK) * factor[slot]).reshape(TOK, TOK)
                    grad = probs * (gbuf[tile, slot] - delta)
                    high = grad.astype(jnp.bfloat16)
                    grads[tile, slot, :, 0:TOK] = high
                    grads[tile, slot, :, TOK:] = probs.astype(jnp.bfloat16)
                    low = (grad - high.astype(jnp.float32)).astype(jnp.bfloat16)
                    right.append(jnp.concatenate([high, low], axis=1))
                keyt = jnp.concatenate([kt[base + blk] for _, blk, _ in found], axis=1)
                total = total + dot(keyt, jnp.concatenate(right, axis=0), ((1,), (0,)))
            dq = (total[:, 0:TOK] + total[:, TOK:]).T.astype(jnp.bfloat16)
            for part in range(4):
                dq_done[4 * tile + part] = dq[part * BLK : (part + 1) * BLK]
            for part in range(4):
                frame = 4 * tile + part

                @pl.when(frame != me)
                def _():
                    send_dq(frame).start()

                @pl.when(frame == me)
                def _():
                    pltpu.make_async_copy(dq_done.at[frame], dq_in.at[unit], dqrecv.at[my_head]).start()

        def key_grads(tile):
            for index in range(4, TILE_BLOCKS):
                acc[index] = jnp.zeros((TOK, 2 * HD), jnp.float32)
            for apart in range(TILES):
                asker = lax.rem(tile + TILES - apart, TILES)
                found = blocks_between(apart, wrapped(asker, apart))
                left = jnp.concatenate([grads[asker, slot] for slot, _, _ in found], axis=0)
                both = dot(left, w[asker], ((1,), (0,)))
                for index, (_, blk, _) in enumerate(found):
                    piece = both[index * TOK : (index + 1) * TOK]
                    if apart == 0:
                        acc[blk] = piece
                    else:
                        acc[blk] += piece
            for frame in range(4):
                for which in range(NB):
                    piece = acc[frame, which * BLK : (which + 1) * BLK]
                    for source, place, target, weights in moves:
                        if target == frame:
                            piece = piece + acc[source, place * BLK : (place + 1) * BLK] * weights[which]
                    acc[frame, which * BLK : (which + 1) * BLK] = piece
            for part in range(2):
                pair = 2 * tile + part
                given[pair] = acc[2 * part + 1 - core].astype(jnp.bfloat16)
                give(pair).start()
                keep[pair] = acc[2 * part + core]

        def mix(tile):
            for part in range(2):
                pair = 2 * tile + part
                give(pair).wait_recv()
                mixed[pair] = (keep[pair] + other[pair].astype(jnp.float32)).astype(jnp.bfloat16)

                @pl.when(2 * pair + core != me)
                def _():
                    send_dkv(pair).start()

                @pl.when(2 * pair + core == me)
                def _():
                    pltpu.make_async_copy(mixed.at[pair], dkv_in.at[slot_id], kvrecv.at[my_head]).start()

        key_grads(turned(0))

        @pl.loop(1, TILES)
        def _(step):
            key_grads(turned(step))
            mix(turned(step - 1))

        mix(turned(TILES - 1))

    qinner = jnp.zeros((TOK, HD), jnp.float32)
    kinner = jnp.zeros((TOK, HD), jnp.float32)
    for h in range(LOCAL_HEADS):
        await_bytes(dq_in.at[pl.ds(h * NB, NB)], dqrecv.at[h])
        dq = dq_in[pl.ds(h * NB, NB)].astype(jnp.float32).reshape(TOK, HD)
        gained = qgain_ref[head_slice(h)].reshape(1, HD) * (dq * SCALE)
        qgrad[:, head_slice(h)] = gained
        qinner = qinner + gained * q_ref[:, head_slice(h)].astype(jnp.float32)
    for h in range(LOCAL_HEADS):
        await_bytes(dkv_in.at[pl.ds(2 * h, 2)], kvrecv.at[h])
        both = dkv_in[2 * h].astype(jnp.float32) + dkv_in[2 * h + 1].astype(jnp.float32)
        vgrad[:, head_slice(h)] = both[:, HD:].astype(jnp.bfloat16)
        gained = kgain_ref[head_slice(h)].reshape(1, HD) * (both[:, 0:HD] * SCALE)
        kgrad[:, head_slice(h)] = gained
        kinner = kinner + gained * k_ref[:, head_slice(h)].astype(jnp.float32)
    stat2[...] = pair_rows(
        jnp.sum(qinner, axis=1, keepdims=True), jnp.sum(kinner, axis=1, keepdims=True)
    )
    for copy in head_sum(stat2, slots2, zsend2, zrecv2):
        copy.wait()
    inner_ref[...] = stat2[...] + slots2[0] + slots2[1] + slots2[2]

    sent = 2 * (2 * LOCAL_HEADS) * TOK + 2 * UNITS * BLK
    kept = 2 * TOK + 2 * BLK

    @pl.when(jnp.logical_not(is_unit))
    def _():
        await_bytes(kv.at[pl.ds(0, sent // 2)], home_send)

    @pl.when(is_unit)
    def _():
        await_bytes(kv.at[pl.ds(0, (sent - kept) // 2)], home_send)
        await_bytes(kv.at[pl.ds(0, FRAMES * TOK // 2)], pass_send)
        await_bytes(dq_done.at[pl.ds(0, FRAMES - 1)], dqsend)
        await_bytes(given, give_send)
        await_bytes(mixed.at[pl.ds(0, FRAMES // 2 - 1)], kvsend)


def finish_kernel(q_ref, k_ref, qgrad, kgrad, vgrad, total_ref, inner_ref, dq_out, dk_out, dv_out):
    qsum, ksum = pair_columns(total_ref[...])
    qdot, kdot = pair_columns(inner_ref[...])
    for raw, grad, square, inner, out in (
        (q_ref, qgrad, qsum, qdot, dq_out),
        (k_ref, kgrad, ksum, kdot, dk_out),
    ):
        rms = lax.rsqrt(square / FEAT + EPSILON)
        factor = rms * rms * rms / FEAT * inner
        for head in range(LOCAL_HEADS):
            at = head_slice(head)
            out[:, at] = (rms * grad[:, at] - factor * raw[:, at].astype(jnp.float32)).astype(jnp.bfloat16)
    dv_out[...] = vgrad[...]


def local(query_raw, key_raw, values, query_gain, key_gain, out_grad, window_offset):
    bf16, f32 = jnp.bfloat16, jnp.float32
    vmem = pl.BlockSpec(memory_space=pltpu.VMEM)
    smem = pl.BlockSpec(memory_space=pltpu.SMEM)
    dma = pltpu.SemaphoreType.DMA
    shape = jax.ShapeDtypeStruct
    half = FRAMES // 2
    qgrad, kgrad, vgrad, total, inner = pl.pallas_call(
        main_kernel,
        name="band_grads",
        out_shape=(
            shape((TOK, LOCAL), f32),
            shape((TOK, LOCAL), f32),
            shape((TOK, LOCAL), bf16),
            shape((8, TOK), f32),
            shape((8, TOK), f32),
        ),
        in_specs=[smem] + [pl.BlockSpec(memory_space=pl.ANY)] * 4 + [vmem] * 2,
        out_specs=[vmem] * 5,
        scratch_shapes=[
            pltpu.VMEM((TOK, LOCAL), bf16),
            pltpu.VMEM((TOK, LOCAL), bf16),
            pltpu.VMEM((TOK, LOCAL), bf16),
            pltpu.VMEM((TOK, LOCAL), bf16),
            dma((4,)),
            pltpu.VMEM((LOCAL_HEADS, TOK, HD), bf16),
            pltpu.VMEM((LOCAL_HEADS, TOK, HD), bf16),
            pltpu.VMEM((8, TOK), f32),
            pltpu.VMEM((3, 8, TOK), f32),
            pltpu.VMEM((8, TOK), f32),
            pltpu.VMEM((3, 8, TOK), f32),
            pltpu.VMEM((TILES * TILE_BLOCKS * TOK, 2 * HD), bf16),
            pltpu.VMEM((TILES * TILE_BLOCKS, HD, TOK), bf16),
            pltpu.VMEM((6, TOK, 2 * HD), bf16),
            pltpu.VMEM((TILES, 2 * TOK, 2 * HD), bf16),
            pltpu.VMEM((TILE_BLOCKS, TOK, 2 * HD), f32),
            pltpu.VMEM((KINDS, TOK, TOK), f32),
            pltpu.VMEM((TILES, MOST_BLOCKS, TOK, TOK), f32),
            pltpu.VMEM((TILES, MOST_BLOCKS, TOK, TOK), f32),
            pltpu.VMEM((TILES, MOST_BLOCKS, TOK, 2 * TOK), bf16),
            pltpu.VMEM((TILES, MOST_BLOCKS, 8, TOK), f32),
            pltpu.VMEM((TILES, MOST_BLOCKS, 8, TOK), f32),
            pltpu.VMEM((TILES, MOST_BLOCKS, 8, TOK), f32),
            pltpu.VMEM((FRAMES, BLK, HD), bf16),
            pltpu.VMEM((half, TOK, 2 * HD), bf16),
            pltpu.VMEM((half, TOK, 2 * HD), bf16),
            pltpu.VMEM((half, TOK, 2 * HD), f32),
            pltpu.VMEM((half, TOK, 2 * HD), bf16),
            pltpu.VMEM((UNITS // 2, TOK, 2 * HD), bf16),
            pltpu.VMEM((UNITS, BLK, HD), bf16),
            dma((3,)), dma((3,)), dma((3,)), dma((3,)),
            dma, dma((half,)), dma((half,)), dma, dma, dma,
            dma, dma((half,)),
            dma, dma, dma((LOCAL_HEADS,)), dma((LOCAL_HEADS,)),
        ],
        compiler_params=pltpu.CompilerParams(
            collective_id=0, has_side_effects=True, vmem_limit_bytes=VMEM_LIMIT
        ),
    )(window_offset, query_raw, key_raw, values, out_grad, query_gain, key_gain)
    return pl.pallas_call(
        finish_kernel,
        name="norm_grads",
        out_shape=(shape((TOK, LOCAL), bf16),) * 3,
        in_specs=[vmem] * 7,
        out_specs=[vmem] * 3,
    )(query_raw, key_raw, qgrad, kgrad, vgrad, total, inner)


def solution(mesh):
    placed = (
        P("frame", "head"),
        P("frame", "head"),
        P("frame", "head"),
        P("head"),
        P("head"),
        P("frame", "head"),
        P(),
    )
    return jax.shard_map(
        local,
        mesh=mesh,
        in_specs=placed,
        out_specs=(P("frame", "head"), P("frame", "head"), P("frame", "head")),
        check_vma=False,
    )
```

```python
import functools
import math

import jax
import jax.numpy as jnp
from jax import lax
from jax.experimental import pallas as pl
from jax.experimental.pallas import tpu as pltpu
from jax.sharding import PartitionSpec as P

HEADS = 20
HD = 128
NB = 4
TOK = 128
BLK = 32
FRAMES = 32
FEAT = HEADS * HD
LOCAL_HEADS = 5
LOCAL = LOCAL_HEADS * HD
TILES = 8
EPSILON = 1e-06
NEG = -1e30
SCALE = HD ** (-0.5)
SCALE2 = SCALE * math.log2(math.e)
MESH = pl.DeviceIdType.MESH
VMEM_LIMIT = 60 * 1024 * 1024

UNITS = LOCAL_HEADS * NB


def my_unit():
    me = lax.axis_index("frame")
    slot = me // 2
    return me, slot < 2 * LOCAL_HEADS, slot // 2, 2 * lax.rem(slot, 2) + lax.rem(me, 2)


KIND_FAR = [(-4, 3), (-4, 4), (-2, 2), (-2, 3), (2, 2), (2, 3), (4, 3), (4, 4), (-1, 2), (1, 2), (-1, 1), (1, 1)]
OPEN = 6
SHUT = OPEN + 1 + len(KIND_FAR)
KINDS = SHUT + 1
MOST_BLOCKS = 18
TILE_BLOCKS = 8
EARLY_VALUES = 10


def far_kind(apart, level):
    return OPEN + 1 + KIND_FAR.index((apart, level))


def blocks_between(apart, over):
    def pick(plain, wrapped):
        return plain + over * (wrapped - plain)

    if apart == 0:
        return [(part, part, 1 + part) for part in range(4)]
    if apart == 1:
        return [
            (4, pick(0, 6), pick(5, OPEN)),
            (5, 4, pick(far_kind(1, 2), SHUT)),
            (6, 7, pick(far_kind(1, 1), SHUT)),
        ]
    if apart == 7:
        return [
            (7, pick(3, 6), pick(0, OPEN)),
            (8, 4, pick(far_kind(-1, 2), SHUT)),
            (9, 7, pick(far_kind(-1, 1), SHUT)),
        ]
    if apart == 2:
        return [(10, pick(4, 6), pick(far_kind(2, 2), OPEN)), (11, 5, pick(far_kind(2, 3), SHUT))]
    if apart == 3:
        return [(12, pick(5, 6), OPEN)]
    if apart == 4:
        return [(10 + level, 2 + level, pick(far_kind(4, level), far_kind(-4, level))) for level in (3, 4)]
    if apart == 5:
        return [(15, pick(6, 5), OPEN)]
    return [(16, pick(6, 4), pick(OPEN, far_kind(-2, 2))), (17, 5, pick(SHUT, far_kind(-2, 3)))]


def wrapped(tile, apart):
    over = (tile + apart) // TILES
    return 1 - over if apart == 7 else over


def greet():
    barrier = pltpu.get_barrier_semaphore()
    me = lax.axis_index("frame")
    row = lax.axis_index("head")
    for step in range(1, FRAMES):
        pl.semaphore_signal(
            barrier, inc=1, device_id={"frame": (me + step) & (FRAMES - 1)}, device_id_type=MESH
        )
    for step in range(1, 4):
        pl.semaphore_signal(
            barrier, inc=1, device_id={"head": lax.rem(row + step, 4)}, device_id_type=MESH
        )


def all_here():
    pl.semaphore_wait(pltpu.get_barrier_semaphore(), FRAMES - 1 + 3)


def pair_rows(first, second):
    lane = lax.broadcasted_iota(jnp.int32, (TOK, TOK), 1)
    both = jnp.where(lane == 0, first, jnp.where(lane == 1, second, 0.0))
    return both.T[:8]


def pair_columns(rows):
    full = jnp.concatenate([rows, jnp.zeros((TOK - 8, TOK), jnp.float32)], axis=0).T
    return full[:, 0:1], full[:, 1:2]


def head_sum(stat, slots, send_sem, recv_sem):
    row = lax.axis_index("head")
    copies = []
    for step in range(1, 4):
        copy = pltpu.make_async_remote_copy(
            src_ref=stat,
            dst_ref=slots.at[step - 1],
            send_sem=send_sem.at[step - 1],
            recv_sem=recv_sem.at[step - 1],
            device_id={"head": lax.rem(row + step, 4)},
            device_id_type=MESH,
        )
        copy.start()
        copies.append(copy)
    return copies


def head_slice(head):
    return pl.ds(head * HD, HD)


def lanes(head):
    return pl.ds(pl.multiple_of(head * HD, HD), HD)


def dot(a, b, contract):
    return lax.dot_general(a, b, (contract, ((), ())), preferred_element_type=jnp.float32)


def frame_rows(frame, width=TOK):
    return pl.ds(pl.multiple_of(frame * width, width), width)


def frame_block(frame):
    return TILE_BLOCKS * (frame // 4) + lax.rem(frame, 4)


def main_kernel(
    offset_ref, q_hbm, k_hbm, v_hbm, g_hbm, qgain_ref, kgain_ref,
    qgrad_out, kgrad_out, vgrad_out, total_ref, inner_ref,
    qgrad, kgrad, vgrad, store_sem, q_ref, k_ref, v_ref, g_ref, load_sem, keys, queries, stat, slots, stat2, slots2,
    kv, kt, picks, w, acc, bias, tbuf, gbuf, grads, peaks, totals, weighteds,
    dq_done, given, other, keep, mixed, dkv_in, dq_in,
    zsend, zrecv, zsend2, zrecv2, home_send, vrecv, krecv, qrecv, pass_send, pass_recv,
    give_send, give_recv, kvsend, dqsend, kvrecv, dqrecv,
):
    me, is_unit, my_head, block = my_unit()
    core = lax.rem(me, 2)
    partner = me + 1 - 2 * core
    slot_id = 2 * my_head + block // 2
    unit = my_head * NB + block

    def squares(ref):
        sums = jnp.zeros((TOK, HD), jnp.float32)
        for head in range(LOCAL_HEADS):
            part = ref[:, head_slice(head)].astype(jnp.float32)
            sums = sums + part * part
        return jnp.sum(sums, axis=1, keepdims=True)

    loads = [
        pltpu.make_async_copy(src, dst, load_sem.at[index])
        for index, (src, dst) in enumerate(((q_hbm, q_ref), (k_hbm, k_ref), (v_hbm, v_ref), (g_hbm, g_ref)))
    ]
    for load in loads:
        load.start()
    greet()
    for load in loads:
        load.wait()
    stat[...] = pair_rows(squares(q_ref), squares(k_ref))
    all_here()
    sums = head_sum(stat, slots, zsend, zrecv)

    def k_at(frame):
        return kv.at[frame_rows(frame_block(frame)), pl.ds(0, HD)]

    def v_at(frame):
        return kv.at[frame_rows(frame_block(frame)), pl.ds(HD, HD)]

    def q_at(frame):
        return w.at[frame // 4, frame_rows(lax.rem(frame, 4), BLK), pl.ds(0, HD)]

    def g_at(frame):
        return w.at[frame // 4, frame_rows(4 + lax.rem(frame, 4), BLK), pl.ds(HD, HD)]

    def remote(src, place, target, recv_sem):
        return pltpu.make_async_remote_copy(
            src_ref=src, dst_ref=place(me), send_sem=home_send, recv_sem=recv_sem,
            device_id={"frame": target}, device_id_type=MESH,
        )

    def send(src, place, target, recv_sem):
        @pl.when(me != target)
        def _():
            remote(src, place, target, recv_sem).start()

        @pl.when(me == target)
        def _():
            pltpu.make_async_copy(src, place(me), recv_sem).start()

    def key_part(slot, source, place, rsem):
        return source(slot // 2), place, 2 * slot + core, rsem.at[me // 2]

    def query_part(slot, side, source, place):
        rows = frame_rows(2 * lax.rem(slot, 2) + side, BLK)
        return source(slot // 2, rows), place, 2 * slot + side, qrecv

    def parts_v(slot):
        return (key_part(slot, lambda head: v_ref.at[:, lanes(head)], v_at, vrecv),)

    def parts_g(slot):
        return tuple(
            query_part(slot, side, lambda head, rows: g_ref.at[rows, lanes(head)], g_at)
            for side in range(2)
        )

    def parts_k(slot):
        return (key_part(slot, lambda head: keys.at[head], k_at, krecv),)

    def parts_q(slot):
        return tuple(
            query_part(slot, side, lambda head, rows: queries.at[head, rows], q_at)
            for side in range(2)
        )

    turn = me // 4 + me // 16

    def send_steps(first, last, *kinds):
        @pl.loop(first, last)
        def _(step):
            for kind in kinds:
                for part in kind(lax.rem(step + turn, 2 * LOCAL_HEADS)):
                    send(*part)

    send_steps(0, 2 * LOCAL_HEADS, parts_g)
    send_steps(0, EARLY_VALUES, parts_v)

    for copy in sums:
        copy.wait()
    total = stat[...] + slots[0] + slots[1] + slots[2]
    total_ref[...] = total
    qsum, ksum = pair_columns(total)
    qrms = lax.rsqrt(qsum / FEAT + EPSILON)
    krms = lax.rsqrt(ksum / FEAT + EPSILON)
    for head in range(LOCAL_HEADS):
        part = k_ref[:, head_slice(head)].astype(jnp.float32)
        keys[head] = (part * krms * kgain_ref[head_slice(head)].reshape(1, HD)).astype(jnp.bfloat16)
        part = q_ref[:, head_slice(head)].astype(jnp.float32)
        queries[head] = (part * qrms * qgain_ref[head_slice(head)].reshape(1, HD)).astype(jnp.bfloat16)

    send_steps(0, 2 * LOCAL_HEADS, parts_k)
    send_steps(0, 2 * LOCAL_HEADS, parts_q)

    def forward(place, frame):
        return pltpu.make_async_remote_copy(
            src_ref=place(frame), dst_ref=place(frame), send_sem=pass_send, recv_sem=pass_recv,
            device_id={"frame": partner}, device_id_type=MESH,
        )

    def await_bytes(ref, sem):
        pltpu.make_async_copy(ref, ref, sem).wait()

    def give(pair):
        return pltpu.make_async_remote_copy(
            src_ref=given.at[pair], dst_ref=other.at[pair], send_sem=give_send,
            recv_sem=give_recv.at[pair], device_id={"frame": partner}, device_id_type=MESH,
        )

    def send_dq(frame):
        return pltpu.make_async_remote_copy(
            src_ref=dq_done.at[frame], dst_ref=dq_in.at[unit], send_sem=dqsend,
            recv_sem=dqrecv.at[my_head], device_id={"frame": frame}, device_id_type=MESH,
        )

    def send_dkv(pair):
        return pltpu.make_async_remote_copy(
            src_ref=mixed.at[pair], dst_ref=dkv_in.at[slot_id], send_sem=kvsend,
            recv_sem=kvrecv.at[my_head], device_id={"frame": 2 * pair + core}, device_id_type=MESH,
        )

    @pl.when(is_unit)
    def _():
        row_frame = lax.broadcasted_iota(jnp.int32, (TOK, TOK), 0) // BLK
        lane_frame = lax.broadcasted_iota(jnp.int32, (TOK, TOK), 1) // BLK
        zero = jnp.zeros((TOK, TOK), jnp.float32)
        hit1 = jnp.where(((row_frame - block - offset_ref[0]) & 3) < 2, 0.0, NEG)
        hit2 = jnp.where(((row_frame - block - offset_ref[1]) & 3) < 1, 0.0, NEG)

        @pl.loop(0, OPEN)
        def _(kind):
            d = jnp.abs(kind - 1 - lane_frame)
            bias[kind] = jnp.where(d < 2, 0.0, jnp.where(d < 4, hit1, hit2))

        bias[OPEN] = zero
        bias[SHUT] = zero + NEG
        for apart, level in KIND_FAR:
            frame = row_frame // 2 + 1 if level == 1 else row_frame
            d = jnp.abs(4 * apart + frame - lane_frame)
            meets = (d >= 2**level) & (d < 2 ** (level + 1))
            if level == 2 and abs(apart) == 1:
                meets = meets & (row_frame != (0 if apart == 1 else 3))
            bias[far_kind(apart, level)] = jnp.where(meets, 0.0, NEG)

        @pl.loop(0, TILES)
        def _(tile):
            w[tile, 0:TOK, HD:] = jnp.zeros((TOK, HD), jnp.bfloat16)
            w[tile, TOK:, 0:HD] = jnp.zeros((TOK, HD), jnp.bfloat16)

        def at_step(step, body):
            place = lax.rem(slot_id - step + 20, 10)

            @pl.when(lax.rem(place, 5) != 4)
            def _():
                body(place - place // 5)

        def passing(place, sem):
            def body(tile):
                for part in range(2):
                    frame = 4 * tile + 2 * part + core
                    await_bytes(place(frame), sem.at[frame // 2])
                    forward(place, frame).start()

            return body

        @pl.loop(0, 10)
        def _(step):
            at_step(step, passing(v_at, vrecv))

        def chosen(level, after):
            pick = (block + offset_ref[level - 1] + after) & 3
            return [(1 - jnp.minimum((pick - which) & 3, 1)).astype(jnp.float32) for which in range(NB)]

        moves = [(4 + index, part, part, chosen(2 + index, 0)) for index in range(3) for part in range(4)]
        moves += [(7, 2 * part + after, 1 + part, chosen(1, after)) for part in range(2) for after in range(2)]

        def score(tile):
            base = TILE_BLOCKS * tile
            for part in range(4):
                kt[base + part] = kv[frame_rows(base + part), 0:HD].T
            for to, place, frame, weights in moves:
                picked = kv[frame_rows(NB * (base + frame), BLK), :] * weights[0].astype(jnp.bfloat16)
                for which in range(1, NB):
                    rows = frame_rows(NB * (base + frame) + which, BLK)
                    picked = picked + kv[rows, :] * weights[which].astype(jnp.bfloat16)
                picks[to - 4, place * BLK : (place + 1) * BLK] = picked
            picks[4] = kv[frame_rows(base), :]
            picks[5] = kv[frame_rows(base + 3), :]
            for part in range(4, TILE_BLOCKS):
                kt[base + part] = picks[part - 4, :, 0:HD].T

            def operand(apart, over, index, blk):
                if apart == 0:
                    return kv[frame_rows(base + blk), :]
                if apart in (1, 7) and index == 0:
                    end = 4 if apart == 1 else 5
                    return picks[end + over * (2 - end)]
                return picks[blk - 4]

            for apart in range(TILES):
                asker = lax.rem(tile + TILES - apart, TILES)
                over = wrapped(asker, apart)
                found = blocks_between(apart, over)
                rows = jnp.concatenate(
                    [operand(apart, over, index, blk) for index, (_, blk, _) in enumerate(found)], axis=0
                )
                both = dot(rows, w[asker], ((1,), (1,)))
                for index, (slot, _, kind) in enumerate(found):
                    part = both[index * TOK : (index + 1) * TOK]
                    t = (part[:, 0:TOK] * SCALE2 + bias[kind]).reshape(16, 8, TOK)
                    grad = part[:, TOK:].reshape(16, 8, TOK)
                    peak = jnp.max(t, axis=0)
                    weight = jnp.exp2(t - peak)
                    tbuf[asker, slot] = weight.reshape(TOK, TOK)
                    gbuf[asker, slot] = part[:, TOK:]
                    peaks[asker, slot] = peak
                    totals[asker, slot] = jnp.sum(weight, axis=0)
                    weighteds[asker, slot] = jnp.sum(weight * grad, axis=0)

        @pl.loop(0, 10)
        def _(step):
            at_step(step, passing(k_at, krecv))

        await_bytes(w.at[pl.ds(0, TILES // 2)], qrecv)
        await_bytes(kv.at[pl.ds(0, FRAMES * TOK // 2)], pass_recv)

        @pl.loop(0, 10)
        def _(step):
            at_step(step, score)

        def turned(step):
            x = lax.rem(me // 8 + step + 1, 4)
            return 2 * x + lax.rem(step // 4 + slot_id, 2)

        @pl.loop(0, TILES)
        def _(step):
            tile = turned(step)
            peak = jnp.max(jnp.max(peaks[tile], axis=0), axis=0, keepdims=True)
            factor = jnp.exp2(peaks[tile] - peak)
            total = jnp.sum(jnp.sum(totals[tile] * factor, axis=0), axis=0, keepdims=True)
            weighted = jnp.sum(jnp.sum(weighteds[tile] * factor, axis=0), axis=0, keepdims=True)
            inverse = 1.0 / total
            delta = weighted * inverse
            factor = factor * inverse
            total = jnp.zeros((HD, 2 * TOK), jnp.float32)
            for apart in range(TILES):
                base = TILE_BLOCKS * lax.rem(tile + apart, TILES)
                found = blocks_between(apart, wrapped(tile, apart))
                right = []
                for slot, _, _ in found:
                    probs = (tbuf[tile, slot].reshape(16, 8, TOK) * factor[slot]).reshape(TOK, TOK)
                    grad = probs * (gbuf[tile, slot] - delta)
                    high = grad.astype(jnp.bfloat16)
                    grads[tile, slot, :, 0:TOK] = high
                    grads[tile, slot, :, TOK:] = probs.astype(jnp.bfloat16)
                    low = (grad - high.astype(jnp.float32)).astype(jnp.bfloat16)
                    right.append(jnp.concatenate([high, low], axis=1))
                keyt = jnp.concatenate([kt[base + blk] for _, blk, _ in found], axis=1)
                total = total + dot(keyt, jnp.concatenate(right, axis=0), ((1,), (0,)))
            dq = (total[:, 0:TOK] + total[:, TOK:]).T.astype(jnp.bfloat16)
            for part in range(4):
                dq_done[4 * tile + part] = dq[part * BLK : (part + 1) * BLK]
            for part in range(4):
                frame = 4 * tile + part

                @pl.when(frame != me)
                def _():
                    send_dq(frame).start()

                @pl.when(frame == me)
                def _():
                    pltpu.make_async_copy(dq_done.at[frame], dq_in.at[unit], dqrecv.at[my_head]).start()

        def key_grads(tile):
            for index in range(4, TILE_BLOCKS):
                acc[index] = jnp.zeros((TOK, 2 * HD), jnp.float32)
            for apart in range(TILES):
                asker = lax.rem(tile + TILES - apart, TILES)
                found = blocks_between(apart, wrapped(asker, apart))
                left = jnp.concatenate([grads[asker, slot] for slot, _, _ in found], axis=0)
                both = dot(left, w[asker], ((1,), (0,)))
                for index, (_, blk, _) in enumerate(found):
                    piece = both[index * TOK : (index + 1) * TOK]
                    if apart == 0:
                        acc[blk] = piece
                    else:
                        acc[blk] += piece
            for frame in range(4):
                for which in range(NB):
                    piece = acc[frame, which * BLK : (which + 1) * BLK]
                    for source, place, target, weights in moves:
                        if target == frame:
                            piece = piece + acc[source, place * BLK : (place + 1) * BLK] * weights[which]
                    acc[frame, which * BLK : (which + 1) * BLK] = piece
            for part in range(2):
                pair = 2 * tile + part
                given[pair] = acc[2 * part + 1 - core].astype(jnp.bfloat16)
                give(pair).start()
                keep[pair] = acc[2 * part + core]

        def mix(tile):
            for part in range(2):
                pair = 2 * tile + part
                give(pair).wait_recv()
                mixed[pair] = (keep[pair] + other[pair].astype(jnp.float32)).astype(jnp.bfloat16)

                @pl.when(2 * pair + core != me)
                def _():
                    send_dkv(pair).start()

                @pl.when(2 * pair + core == me)
                def _():
                    pltpu.make_async_copy(mixed.at[pair], dkv_in.at[slot_id], kvrecv.at[my_head]).start()

        key_grads(turned(0))

        @pl.loop(1, TILES)
        def _(step):
            key_grads(turned(step))
            mix(turned(step - 1))

        mix(turned(TILES - 1))

    qinner = jnp.zeros((TOK, HD), jnp.float32)
    kinner = jnp.zeros((TOK, HD), jnp.float32)
    for h in range(LOCAL_HEADS):
        await_bytes(dq_in.at[pl.ds(h * NB, NB)], dqrecv.at[h])
        dq = dq_in[pl.ds(h * NB, NB)].astype(jnp.float32).reshape(TOK, HD)
        gained = qgain_ref[head_slice(h)].reshape(1, HD) * (dq * SCALE)
        qgrad[:, head_slice(h)] = gained
        qinner = qinner + gained * q_ref[:, head_slice(h)].astype(jnp.float32)
    for h in range(LOCAL_HEADS):
        await_bytes(dkv_in.at[pl.ds(2 * h, 2)], kvrecv.at[h])
        both = dkv_in[2 * h].astype(jnp.float32) + dkv_in[2 * h + 1].astype(jnp.float32)
        vgrad[:, head_slice(h)] = both[:, HD:].astype(jnp.bfloat16)
        gained = kgain_ref[head_slice(h)].reshape(1, HD) * (both[:, 0:HD] * SCALE)
        kgrad[:, head_slice(h)] = gained
        kinner = kinner + gained * k_ref[:, head_slice(h)].astype(jnp.float32)
    stores = [
        pltpu.make_async_copy(src, dst, store_sem.at[index])
        for index, (src, dst) in enumerate(((qgrad, qgrad_out), (kgrad, kgrad_out), (vgrad, vgrad_out)))
    ]
    stat2[...] = pair_rows(
        jnp.sum(qinner, axis=1, keepdims=True), jnp.sum(kinner, axis=1, keepdims=True)
    )
    sums = head_sum(stat2, slots2, zsend2, zrecv2)
    for store in stores:
        store.start()
    for copy in sums:
        copy.wait()
    inner_ref[...] = stat2[...] + slots2[0] + slots2[1] + slots2[2]

    for store in stores:
        store.wait()

    sent = 2 * (2 * LOCAL_HEADS) * TOK + 2 * UNITS * BLK
    kept = 2 * TOK + 2 * BLK

    @pl.when(jnp.logical_not(is_unit))
    def _():
        await_bytes(kv.at[pl.ds(0, sent // 2)], home_send)

    @pl.when(is_unit)
    def _():
        await_bytes(kv.at[pl.ds(0, (sent - kept) // 2)], home_send)
        await_bytes(kv.at[pl.ds(0, FRAMES * TOK // 2)], pass_send)
        await_bytes(dq_done.at[pl.ds(0, FRAMES - 1)], dqsend)
        await_bytes(given, give_send)
        await_bytes(mixed.at[pl.ds(0, FRAMES // 2 - 1)], kvsend)


def finish_kernel(q_ref, k_ref, qgrad, kgrad, vgrad, total_ref, inner_ref, dq_out, dk_out, dv_out):
    qsum, ksum = pair_columns(total_ref[...])
    qdot, kdot = pair_columns(inner_ref[...])
    for raw, grad, square, inner, out in (
        (q_ref, qgrad, qsum, qdot, dq_out),
        (k_ref, kgrad, ksum, kdot, dk_out),
    ):
        rms = lax.rsqrt(square / FEAT + EPSILON)
        factor = rms * rms * rms / FEAT * inner
        for head in range(LOCAL_HEADS):
            at = head_slice(head)
            out[:, at] = (rms * grad[:, at] - factor * raw[:, at].astype(jnp.float32)).astype(jnp.bfloat16)
    dv_out[...] = vgrad[...]


def local(query_raw, key_raw, values, query_gain, key_gain, out_grad, window_offset):
    bf16, f32 = jnp.bfloat16, jnp.float32
    vmem = pl.BlockSpec(memory_space=pltpu.VMEM)
    smem = pl.BlockSpec(memory_space=pltpu.SMEM)
    dma = pltpu.SemaphoreType.DMA
    shape = jax.ShapeDtypeStruct
    half = FRAMES // 2
    qgrad, kgrad, vgrad, total, inner = pl.pallas_call(
        main_kernel,
        name="band_grads",
        out_shape=(
            shape((TOK, LOCAL), f32),
            shape((TOK, LOCAL), f32),
            shape((TOK, LOCAL), bf16),
            shape((8, TOK), f32),
            shape((8, TOK), f32),
        ),
        in_specs=[smem] + [pl.BlockSpec(memory_space=pl.ANY)] * 4 + [vmem] * 2,
        out_specs=[pl.BlockSpec(memory_space=pl.ANY)] * 3 + [vmem] * 2,
        scratch_shapes=[
            pltpu.VMEM((TOK, LOCAL), f32),
            pltpu.VMEM((TOK, LOCAL), f32),
            pltpu.VMEM((TOK, LOCAL), bf16),
            dma((3,)),
            pltpu.VMEM((TOK, LOCAL), bf16),
            pltpu.VMEM((TOK, LOCAL), bf16),
            pltpu.VMEM((TOK, LOCAL), bf16),
            pltpu.VMEM((TOK, LOCAL), bf16),
            dma((4,)),
            pltpu.VMEM((LOCAL_HEADS, TOK, HD), bf16),
            pltpu.VMEM((LOCAL_HEADS, TOK, HD), bf16),
            pltpu.VMEM((8, TOK), f32),
            pltpu.VMEM((3, 8, TOK), f32),
            pltpu.VMEM((8, TOK), f32),
            pltpu.VMEM((3, 8, TOK), f32),
            pltpu.VMEM((TILES * TILE_BLOCKS * TOK, 2 * HD), bf16),
            pltpu.VMEM((TILES * TILE_BLOCKS, HD, TOK), bf16),
            pltpu.VMEM((6, TOK, 2 * HD), bf16),
            pltpu.VMEM((TILES, 2 * TOK, 2 * HD), bf16),
            pltpu.VMEM((TILE_BLOCKS, TOK, 2 * HD), f32),
            pltpu.VMEM((KINDS, TOK, TOK), f32),
            pltpu.VMEM((TILES, MOST_BLOCKS, TOK, TOK), f32),
            pltpu.VMEM((TILES, MOST_BLOCKS, TOK, TOK), f32),
            pltpu.VMEM((TILES, MOST_BLOCKS, TOK, 2 * TOK), bf16),
            pltpu.VMEM((TILES, MOST_BLOCKS, 8, TOK), f32),
            pltpu.VMEM((TILES, MOST_BLOCKS, 8, TOK), f32),
            pltpu.VMEM((TILES, MOST_BLOCKS, 8, TOK), f32),
            pltpu.VMEM((FRAMES, BLK, HD), bf16),
            pltpu.VMEM((half, TOK, 2 * HD), bf16),
            pltpu.VMEM((half, TOK, 2 * HD), bf16),
            pltpu.VMEM((half, TOK, 2 * HD), f32),
            pltpu.VMEM((half, TOK, 2 * HD), bf16),
            pltpu.VMEM((UNITS // 2, TOK, 2 * HD), bf16),
            pltpu.VMEM((UNITS, BLK, HD), bf16),
            dma((3,)), dma((3,)), dma((3,)), dma((3,)),
            dma, dma((half,)), dma((half,)), dma, dma, dma,
            dma, dma((half,)),
            dma, dma, dma((LOCAL_HEADS,)), dma((LOCAL_HEADS,)),
        ],
        compiler_params=pltpu.CompilerParams(
            collective_id=0, has_side_effects=True, vmem_limit_bytes=VMEM_LIMIT
        ),
    )(window_offset, query_raw, key_raw, values, out_grad, query_gain, key_gain)
    return pl.pallas_call(
        finish_kernel,
        name="norm_grads",
        out_shape=(shape((TOK, LOCAL), bf16),) * 3,
        in_specs=[vmem] * 7,
        out_specs=[vmem] * 3,
    )(query_raw, key_raw, qgrad, kgrad, vgrad, total, inner)


def solution(mesh):
    placed = (
        P("frame", "head"),
        P("frame", "head"),
        P("frame", "head"),
        P("head"),
        P("head"),
        P("frame", "head"),
        P(),
    )
    return jax.shard_map(
        local,
        mesh=mesh,
        in_specs=placed,
        out_specs=(P("frame", "head"), P("frame", "head"), P("frame", "head")),
        check_vma=False,
    )
```

```python
import functools
import math

import jax
import jax.numpy as jnp
from jax import lax
from jax.experimental import pallas as pl
from jax.experimental.pallas import tpu as pltpu
from jax.sharding import PartitionSpec as P

HEADS = 20
HD = 128
NB = 4
TOK = 128
BLK = 32
FRAMES = 32
FEAT = HEADS * HD
LOCAL_HEADS = 5
LOCAL = LOCAL_HEADS * HD
TILES = 8
EPSILON = 1e-06
NEG = -1e30
SCALE = HD ** (-0.5)
SCALE2 = SCALE * math.log2(math.e)
MESH = pl.DeviceIdType.MESH
VMEM_LIMIT = 60 * 1024 * 1024

UNITS = LOCAL_HEADS * NB


def my_unit():
    me = lax.axis_index("frame")
    slot = me // 2
    return me, slot < 2 * LOCAL_HEADS, slot // 2, 2 * lax.rem(slot, 2) + lax.rem(me, 2)


KIND_FAR = [(-4, 3), (-4, 4), (-2, 2), (-2, 3), (2, 2), (2, 3), (4, 3), (4, 4), (-1, 2), (1, 2), (-1, 1), (1, 1)]
OPEN = 6
SHUT = OPEN + 1 + len(KIND_FAR)
KINDS = SHUT + 1
MOST_BLOCKS = 18
TILE_BLOCKS = 8
EARLY_VALUES = 10


def far_kind(apart, level):
    return OPEN + 1 + KIND_FAR.index((apart, level))


def blocks_between(apart, over):
    def pick(plain, wrapped):
        return plain + over * (wrapped - plain)

    if apart == 0:
        return [(part, part, 1 + part) for part in range(4)]
    if apart == 1:
        return [
            (4, pick(0, 6), pick(5, OPEN)),
            (5, 4, pick(far_kind(1, 2), SHUT)),
            (6, 7, pick(far_kind(1, 1), SHUT)),
        ]
    if apart == 7:
        return [
            (7, pick(3, 6), pick(0, OPEN)),
            (8, 4, pick(far_kind(-1, 2), SHUT)),
            (9, 7, pick(far_kind(-1, 1), SHUT)),
        ]
    if apart == 2:
        return [(10, pick(4, 6), pick(far_kind(2, 2), OPEN)), (11, 5, pick(far_kind(2, 3), SHUT))]
    if apart == 3:
        return [(12, pick(5, 6), OPEN)]
    if apart == 4:
        return [(10 + level, 2 + level, pick(far_kind(4, level), far_kind(-4, level))) for level in (3, 4)]
    if apart == 5:
        return [(15, pick(6, 5), OPEN)]
    return [(16, pick(6, 4), pick(OPEN, far_kind(-2, 2))), (17, 5, pick(SHUT, far_kind(-2, 3)))]


def wrapped(tile, apart):
    over = (tile + apart) // TILES
    return 1 - over if apart == 7 else over


def greet():
    barrier = pltpu.get_barrier_semaphore()
    me = lax.axis_index("frame")
    row = lax.axis_index("head")
    for step in range(1, FRAMES):
        pl.semaphore_signal(
            barrier, inc=1, device_id={"frame": (me + step) & (FRAMES - 1)}, device_id_type=MESH
        )
    for step in range(1, 4):
        pl.semaphore_signal(
            barrier, inc=1, device_id={"head": lax.rem(row + step, 4)}, device_id_type=MESH
        )


def all_here():
    pl.semaphore_wait(pltpu.get_barrier_semaphore(), FRAMES - 1 + 3)


def pair_rows(first, second):
    lane = lax.broadcasted_iota(jnp.int32, (TOK, TOK), 1)
    both = jnp.where(lane == 0, first, jnp.where(lane == 1, second, 0.0))
    return both.T[:8]


def pair_columns(rows):
    full = jnp.concatenate([rows, jnp.zeros((TOK - 8, TOK), jnp.float32)], axis=0).T
    return full[:, 0:1], full[:, 1:2]


def head_sum(stat, slots, send_sem, recv_sem):
    row = lax.axis_index("head")
    copies = []
    for step in range(1, 4):
        copy = pltpu.make_async_remote_copy(
            src_ref=stat,
            dst_ref=slots.at[step - 1],
            send_sem=send_sem.at[step - 1],
            recv_sem=recv_sem.at[step - 1],
            device_id={"head": lax.rem(row + step, 4)},
            device_id_type=MESH,
        )
        copy.start()
        copies.append(copy)
    return copies


def head_slice(head):
    return pl.ds(head * HD, HD)


def lanes(head):
    return pl.ds(pl.multiple_of(head * HD, HD), HD)


def dot(a, b, contract):
    return lax.dot_general(a, b, (contract, ((), ())), preferred_element_type=jnp.float32)


def frame_rows(frame, width=TOK):
    return pl.ds(pl.multiple_of(frame * width, width), width)


def frame_block(frame):
    return TILE_BLOCKS * (frame // 4) + lax.rem(frame, 4)


def main_kernel(
    offset_ref, q_hbm, k_hbm, v_hbm, g_hbm, qgain_ref, kgain_ref,
    qgrad_out, kgrad_out, vgrad_out, total_ref, inner_ref,
    qgrad, kgrad, vgrad, store_sem, q_ref, k_ref, v_ref, g_ref, load_sem, keys, queries, stat, slots, stat2, slots2,
    kv, kt, picks, w, acc, bias, tbuf, gbuf, grads, peaks, totals, weighteds,
    dq_done, given, other, keep, mixed, dkv_in, dq_in,
    zsend, zrecv, zsend2, zrecv2, home_send, vrecv, krecv, qrecv, pass_send, pass_recv,
    give_send, give_recv, kvsend, dqsend, kvrecv, dqrecv,
):
    me, is_unit, my_head, block = my_unit()
    core = lax.rem(me, 2)
    partner = me + 1 - 2 * core
    slot_id = 2 * my_head + block // 2
    unit = my_head * NB + block

    def squares(ref):
        sums = jnp.zeros((TOK, HD), jnp.float32)
        for head in range(LOCAL_HEADS):
            part = ref[:, head_slice(head)].astype(jnp.float32)
            sums = sums + part * part
        return jnp.sum(sums, axis=1, keepdims=True)

    loads = [
        pltpu.make_async_copy(src, dst, load_sem.at[index])
        for index, (src, dst) in enumerate(((q_hbm, q_ref), (k_hbm, k_ref), (v_hbm, v_ref), (g_hbm, g_ref)))
    ]
    for load in loads:
        load.start()
    greet()
    for load in loads[:2]:
        load.wait()
    stat[...] = pair_rows(squares(q_ref), squares(k_ref))
    all_here()
    sums = head_sum(stat, slots, zsend, zrecv)
    for load in loads[2:]:
        load.wait()

    def k_at(frame):
        return kv.at[frame_rows(frame_block(frame)), pl.ds(0, HD)]

    def v_at(frame):
        return kv.at[frame_rows(frame_block(frame)), pl.ds(HD, HD)]

    def q_at(frame):
        return w.at[frame // 4, frame_rows(lax.rem(frame, 4), BLK), pl.ds(0, HD)]

    def g_at(frame):
        return w.at[frame // 4, frame_rows(4 + lax.rem(frame, 4), BLK), pl.ds(HD, HD)]

    def remote(src, place, target, recv_sem):
        return pltpu.make_async_remote_copy(
            src_ref=src, dst_ref=place(me), send_sem=home_send, recv_sem=recv_sem,
            device_id={"frame": target}, device_id_type=MESH,
        )

    def send(src, place, target, recv_sem):
        @pl.when(me != target)
        def _():
            remote(src, place, target, recv_sem).start()

        @pl.when(me == target)
        def _():
            pltpu.make_async_copy(src, place(me), recv_sem).start()

    def key_part(slot, source, place, rsem):
        return source(slot // 2), place, 2 * slot + core, rsem.at[me // 2]

    def query_part(slot, side, source, place):
        rows = frame_rows(2 * lax.rem(slot, 2) + side, BLK)
        return source(slot // 2, rows), place, 2 * slot + side, qrecv

    def parts_v(slot):
        return (key_part(slot, lambda head: v_ref.at[:, lanes(head)], v_at, vrecv),)

    def parts_g(slot):
        return tuple(
            query_part(slot, side, lambda head, rows: g_ref.at[rows, lanes(head)], g_at)
            for side in range(2)
        )

    def parts_k(slot):
        return (key_part(slot, lambda head: keys.at[head], k_at, krecv),)

    def parts_q(slot):
        return tuple(
            query_part(slot, side, lambda head, rows: queries.at[head, rows], q_at)
            for side in range(2)
        )

    turn = me // 4 + me // 16

    def send_steps(first, last, *kinds):
        @pl.loop(first, last)
        def _(step):
            for kind in kinds:
                for part in kind(lax.rem(step + turn, 2 * LOCAL_HEADS)):
                    send(*part)

    send_steps(0, 2 * LOCAL_HEADS, parts_g)
    send_steps(0, EARLY_VALUES, parts_v)

    for copy in sums:
        copy.wait()
    total = stat[...] + slots[0] + slots[1] + slots[2]
    total_ref[...] = total
    qsum, ksum = pair_columns(total)
    qrms = lax.rsqrt(qsum / FEAT + EPSILON)
    krms = lax.rsqrt(ksum / FEAT + EPSILON)
    for head in range(LOCAL_HEADS):
        part = k_ref[:, head_slice(head)].astype(jnp.float32)
        keys[head] = (part * krms * kgain_ref[head_slice(head)].reshape(1, HD)).astype(jnp.bfloat16)
        part = q_ref[:, head_slice(head)].astype(jnp.float32)
        queries[head] = (part * qrms * qgain_ref[head_slice(head)].reshape(1, HD)).astype(jnp.bfloat16)

    send_steps(0, 2 * LOCAL_HEADS, parts_k)
    send_steps(0, 2 * LOCAL_HEADS, parts_q)

    def forward(place, frame):
        return pltpu.make_async_remote_copy(
            src_ref=place(frame), dst_ref=place(frame), send_sem=pass_send, recv_sem=pass_recv,
            device_id={"frame": partner}, device_id_type=MESH,
        )

    def await_bytes(ref, sem):
        pltpu.make_async_copy(ref, ref, sem).wait()

    def give(pair):
        return pltpu.make_async_remote_copy(
            src_ref=given.at[pair], dst_ref=other.at[pair], send_sem=give_send,
            recv_sem=give_recv.at[pair], device_id={"frame": partner}, device_id_type=MESH,
        )

    def send_dq(frame):
        return pltpu.make_async_remote_copy(
            src_ref=dq_done.at[frame], dst_ref=dq_in.at[unit], send_sem=dqsend,
            recv_sem=dqrecv.at[my_head], device_id={"frame": frame}, device_id_type=MESH,
        )

    def send_dkv(pair):
        return pltpu.make_async_remote_copy(
            src_ref=mixed.at[pair], dst_ref=dkv_in.at[slot_id], send_sem=kvsend,
            recv_sem=kvrecv.at[my_head], device_id={"frame": 2 * pair + core}, device_id_type=MESH,
        )

    @pl.when(is_unit)
    def _():
        row_frame = lax.broadcasted_iota(jnp.int32, (TOK, TOK), 0) // BLK
        lane_frame = lax.broadcasted_iota(jnp.int32, (TOK, TOK), 1) // BLK
        zero = jnp.zeros((TOK, TOK), jnp.float32)
        hit1 = jnp.where(((row_frame - block - offset_ref[0]) & 3) < 2, 0.0, NEG)
        hit2 = jnp.where(((row_frame - block - offset_ref[1]) & 3) < 1, 0.0, NEG)

        @pl.loop(0, OPEN)
        def _(kind):
            d = jnp.abs(kind - 1 - lane_frame)
            bias[kind] = jnp.where(d < 2, 0.0, jnp.where(d < 4, hit1, hit2))

        bias[OPEN] = zero
        bias[SHUT] = zero + NEG
        for apart, level in KIND_FAR:
            frame = row_frame // 2 + 1 if level == 1 else row_frame
            d = jnp.abs(4 * apart + frame - lane_frame)
            meets = (d >= 2**level) & (d < 2 ** (level + 1))
            if level == 2 and abs(apart) == 1:
                meets = meets & (row_frame != (0 if apart == 1 else 3))
            bias[far_kind(apart, level)] = jnp.where(meets, 0.0, NEG)

        @pl.loop(0, TILES)
        def _(tile):
            w[tile, 0:TOK, HD:] = jnp.zeros((TOK, HD), jnp.bfloat16)
            w[tile, TOK:, 0:HD] = jnp.zeros((TOK, HD), jnp.bfloat16)

        def at_step(step, body):
            place = lax.rem(slot_id - step + 20, 10)

            @pl.when(lax.rem(place, 5) != 4)
            def _():
                body(place - place // 5)

        def passing(place, sem):
            def body(tile):
                for part in range(2):
                    frame = 4 * tile + 2 * part + core
                    await_bytes(place(frame), sem.at[frame // 2])
                    forward(place, frame).start()

            return body

        @pl.loop(0, 10)
        def _(step):
            at_step(step, passing(v_at, vrecv))

        def chosen(level, after):
            pick = (block + offset_ref[level - 1] + after) & 3
            return [(1 - jnp.minimum((pick - which) & 3, 1)).astype(jnp.float32) for which in range(NB)]

        moves = [(4 + index, part, part, chosen(2 + index, 0)) for index in range(3) for part in range(4)]
        moves += [(7, 2 * part + after, 1 + part, chosen(1, after)) for part in range(2) for after in range(2)]

        def score(tile):
            base = TILE_BLOCKS * tile
            for part in range(4):
                kt[base + part] = kv[frame_rows(base + part), 0:HD].T
            for to, place, frame, weights in moves:
                picked = kv[frame_rows(NB * (base + frame), BLK), :] * weights[0].astype(jnp.bfloat16)
                for which in range(1, NB):
                    rows = frame_rows(NB * (base + frame) + which, BLK)
                    picked = picked + kv[rows, :] * weights[which].astype(jnp.bfloat16)
                picks[to - 4, place * BLK : (place + 1) * BLK] = picked
            picks[4] = kv[frame_rows(base), :]
            picks[5] = kv[frame_rows(base + 3), :]
            for part in range(4, TILE_BLOCKS):
                kt[base + part] = picks[part - 4, :, 0:HD].T

            def operand(apart, over, index, blk):
                if apart == 0:
                    return kv[frame_rows(base + blk), :]
                if apart in (1, 7) and index == 0:
                    end = 4 if apart == 1 else 5
                    return picks[end + over * (2 - end)]
                return picks[blk - 4]

            for apart in range(TILES):
                asker = lax.rem(tile + TILES - apart, TILES)
                over = wrapped(asker, apart)
                found = blocks_between(apart, over)
                rows = jnp.concatenate(
                    [operand(apart, over, index, blk) for index, (_, blk, _) in enumerate(found)], axis=0
                )
                both = dot(rows, w[asker], ((1,), (1,)))
                for index, (slot, _, kind) in enumerate(found):
                    part = both[index * TOK : (index + 1) * TOK]
                    t = (part[:, 0:TOK] * SCALE2 + bias[kind]).reshape(16, 8, TOK)
                    grad = part[:, TOK:].reshape(16, 8, TOK)
                    peak = jnp.max(t, axis=0)
                    weight = jnp.exp2(t - peak)
                    tbuf[asker, slot] = weight.reshape(TOK, TOK)
                    gbuf[asker, slot] = part[:, TOK:]
                    peaks[asker, slot] = peak
                    totals[asker, slot] = jnp.sum(weight, axis=0)
                    weighteds[asker, slot] = jnp.sum(weight * grad, axis=0)

        @pl.loop(0, 10)
        def _(step):
            at_step(step, passing(k_at, krecv))

        await_bytes(w.at[pl.ds(0, TILES // 2)], qrecv)
        await_bytes(kv.at[pl.ds(0, FRAMES * TOK // 2)], pass_recv)

        @pl.loop(0, 10)
        def _(step):
            at_step(step, score)

        def turned(step):
            x = lax.rem(me // 8 + step + 1, 4)
            return 2 * x + lax.rem(step // 4 + slot_id, 2)

        @pl.loop(0, TILES)
        def _(step):
            tile = turned(step)
            peak = jnp.max(jnp.max(peaks[tile], axis=0), axis=0, keepdims=True)
            factor = jnp.exp2(peaks[tile] - peak)
            total = jnp.sum(jnp.sum(totals[tile] * factor, axis=0), axis=0, keepdims=True)
            weighted = jnp.sum(jnp.sum(weighteds[tile] * factor, axis=0), axis=0, keepdims=True)
            inverse = 1.0 / total
            delta = weighted * inverse
            factor = factor * inverse
            total = jnp.zeros((HD, 2 * TOK), jnp.float32)
            for apart in range(TILES):
                base = TILE_BLOCKS * lax.rem(tile + apart, TILES)
                found = blocks_between(apart, wrapped(tile, apart))
                right = []
                for slot, _, _ in found:
                    probs = (tbuf[tile, slot].reshape(16, 8, TOK) * factor[slot]).reshape(TOK, TOK)
                    grad = probs * (gbuf[tile, slot] - delta)
                    high = grad.astype(jnp.bfloat16)
                    grads[tile, slot, :, 0:TOK] = high
                    grads[tile, slot, :, TOK:] = probs.astype(jnp.bfloat16)
                    low = (grad - high.astype(jnp.float32)).astype(jnp.bfloat16)
                    right.append(jnp.concatenate([high, low], axis=1))
                keyt = jnp.concatenate([kt[base + blk] for _, blk, _ in found], axis=1)
                total = total + dot(keyt, jnp.concatenate(right, axis=0), ((1,), (0,)))
            dq = (total[:, 0:TOK] + total[:, TOK:]).T.astype(jnp.bfloat16)
            for part in range(4):
                dq_done[4 * tile + part] = dq[part * BLK : (part + 1) * BLK]
            for part in range(4):
                frame = 4 * tile + part

                @pl.when(frame != me)
                def _():
                    send_dq(frame).start()

                @pl.when(frame == me)
                def _():
                    pltpu.make_async_copy(dq_done.at[frame], dq_in.at[unit], dqrecv.at[my_head]).start()

        def key_grads(tile):
            for index in range(4, TILE_BLOCKS):
                acc[index] = jnp.zeros((TOK, 2 * HD), jnp.float32)
            for apart in range(TILES):
                asker = lax.rem(tile + TILES - apart, TILES)
                found = blocks_between(apart, wrapped(asker, apart))
                left = jnp.concatenate([grads[asker, slot] for slot, _, _ in found], axis=0)
                both = dot(left, w[asker], ((1,), (0,)))
                for index, (_, blk, _) in enumerate(found):
                    piece = both[index * TOK : (index + 1) * TOK]
                    if apart == 0:
                        acc[blk] = piece
                    else:
                        acc[blk] += piece
            for frame in range(4):
                for which in range(NB):
                    piece = acc[frame, which * BLK : (which + 1) * BLK]
                    for source, place, target, weights in moves:
                        if target == frame:
                            piece = piece + acc[source, place * BLK : (place + 1) * BLK] * weights[which]
                    acc[frame, which * BLK : (which + 1) * BLK] = piece
            for part in range(2):
                pair = 2 * tile + part
                given[pair] = acc[2 * part + 1 - core].astype(jnp.bfloat16)
                give(pair).start()
                keep[pair] = acc[2 * part + core]

        def mix(tile):
            for part in range(2):
                pair = 2 * tile + part
                give(pair).wait_recv()
                mixed[pair] = (keep[pair] + other[pair].astype(jnp.float32)).astype(jnp.bfloat16)

                @pl.when(2 * pair + core != me)
                def _():
                    send_dkv(pair).start()

                @pl.when(2 * pair + core == me)
                def _():
                    pltpu.make_async_copy(mixed.at[pair], dkv_in.at[slot_id], kvrecv.at[my_head]).start()

        key_grads(turned(0))

        @pl.loop(1, TILES)
        def _(step):
            key_grads(turned(step))
            mix(turned(step - 1))

        mix(turned(TILES - 1))

    qinner = jnp.zeros((TOK, HD), jnp.float32)
    kinner = jnp.zeros((TOK, HD), jnp.float32)
    for h in range(LOCAL_HEADS):
        await_bytes(dq_in.at[pl.ds(h * NB, NB)], dqrecv.at[h])
        dq = dq_in[pl.ds(h * NB, NB)].astype(jnp.float32).reshape(TOK, HD)
        gained = qgain_ref[head_slice(h)].reshape(1, HD) * (dq * SCALE)
        qgrad[:, head_slice(h)] = gained
        qinner = qinner + gained * q_ref[:, head_slice(h)].astype(jnp.float32)
    for h in range(LOCAL_HEADS):
        await_bytes(dkv_in.at[pl.ds(2 * h, 2)], kvrecv.at[h])
        both = dkv_in[2 * h].astype(jnp.float32) + dkv_in[2 * h + 1].astype(jnp.float32)
        vgrad[:, head_slice(h)] = both[:, HD:].astype(jnp.bfloat16)
        gained = kgain_ref[head_slice(h)].reshape(1, HD) * (both[:, 0:HD] * SCALE)
        kgrad[:, head_slice(h)] = gained
        kinner = kinner + gained * k_ref[:, head_slice(h)].astype(jnp.float32)
    stores = [
        pltpu.make_async_copy(src, dst, store_sem.at[index])
        for index, (src, dst) in enumerate(((qgrad, qgrad_out), (kgrad, kgrad_out), (vgrad, vgrad_out)))
    ]
    stat2[...] = pair_rows(
        jnp.sum(qinner, axis=1, keepdims=True), jnp.sum(kinner, axis=1, keepdims=True)
    )
    sums = head_sum(stat2, slots2, zsend2, zrecv2)
    for store in stores:
        store.start()
    for copy in sums:
        copy.wait()
    inner_ref[...] = stat2[...] + slots2[0] + slots2[1] + slots2[2]

    for store in stores:
        store.wait()

    sent = 2 * (2 * LOCAL_HEADS) * TOK + 2 * UNITS * BLK
    kept = 2 * TOK + 2 * BLK

    @pl.when(jnp.logical_not(is_unit))
    def _():
        await_bytes(kv.at[pl.ds(0, sent // 2)], home_send)

    @pl.when(is_unit)
    def _():
        await_bytes(kv.at[pl.ds(0, (sent - kept) // 2)], home_send)
        await_bytes(kv.at[pl.ds(0, FRAMES * TOK // 2)], pass_send)
        await_bytes(dq_done.at[pl.ds(0, FRAMES - 1)], dqsend)
        await_bytes(given, give_send)
        await_bytes(mixed.at[pl.ds(0, FRAMES // 2 - 1)], kvsend)


def finish_kernel(q_ref, k_ref, qgrad, kgrad, vgrad, total_ref, inner_ref, dq_out, dk_out, dv_out):
    qsum, ksum = pair_columns(total_ref[...])
    qdot, kdot = pair_columns(inner_ref[...])
    for raw, grad, square, inner, out in (
        (q_ref, qgrad, qsum, qdot, dq_out),
        (k_ref, kgrad, ksum, kdot, dk_out),
    ):
        rms = lax.rsqrt(square / FEAT + EPSILON)
        factor = rms * rms * rms / FEAT * inner
        for head in range(LOCAL_HEADS):
            at = head_slice(head)
            out[:, at] = (rms * grad[:, at] - factor * raw[:, at].astype(jnp.float32)).astype(jnp.bfloat16)
    dv_out[...] = vgrad[...]


def local(query_raw, key_raw, values, query_gain, key_gain, out_grad, window_offset):
    bf16, f32 = jnp.bfloat16, jnp.float32
    vmem = pl.BlockSpec(memory_space=pltpu.VMEM)
    smem = pl.BlockSpec(memory_space=pltpu.SMEM)
    dma = pltpu.SemaphoreType.DMA
    shape = jax.ShapeDtypeStruct
    half = FRAMES // 2
    qgrad, kgrad, vgrad, total, inner = pl.pallas_call(
        main_kernel,
        name="band_grads",
        out_shape=(
            shape((TOK, LOCAL), f32),
            shape((TOK, LOCAL), f32),
            shape((TOK, LOCAL), bf16),
            shape((8, TOK), f32),
            shape((8, TOK), f32),
        ),
        in_specs=[smem] + [pl.BlockSpec(memory_space=pl.ANY)] * 4 + [vmem] * 2,
        out_specs=[pl.BlockSpec(memory_space=pl.ANY)] * 3 + [vmem] * 2,
        scratch_shapes=[
            pltpu.VMEM((TOK, LOCAL), f32),
            pltpu.VMEM((TOK, LOCAL), f32),
            pltpu.VMEM((TOK, LOCAL), bf16),
            dma((3,)),
            pltpu.VMEM((TOK, LOCAL), bf16),
            pltpu.VMEM((TOK, LOCAL), bf16),
            pltpu.VMEM((TOK, LOCAL), bf16),
            pltpu.VMEM((TOK, LOCAL), bf16),
            dma((4,)),
            pltpu.VMEM((LOCAL_HEADS, TOK, HD), bf16),
            pltpu.VMEM((LOCAL_HEADS, TOK, HD), bf16),
            pltpu.VMEM((8, TOK), f32),
            pltpu.VMEM((3, 8, TOK), f32),
            pltpu.VMEM((8, TOK), f32),
            pltpu.VMEM((3, 8, TOK), f32),
            pltpu.VMEM((TILES * TILE_BLOCKS * TOK, 2 * HD), bf16),
            pltpu.VMEM((TILES * TILE_BLOCKS, HD, TOK), bf16),
            pltpu.VMEM((6, TOK, 2 * HD), bf16),
            pltpu.VMEM((TILES, 2 * TOK, 2 * HD), bf16),
            pltpu.VMEM((TILE_BLOCKS, TOK, 2 * HD), f32),
            pltpu.VMEM((KINDS, TOK, TOK), f32),
            pltpu.VMEM((TILES, MOST_BLOCKS, TOK, TOK), f32),
            pltpu.VMEM((TILES, MOST_BLOCKS, TOK, TOK), f32),
            pltpu.VMEM((TILES, MOST_BLOCKS, TOK, 2 * TOK), bf16),
            pltpu.VMEM((TILES, MOST_BLOCKS, 8, TOK), f32),
            pltpu.VMEM((TILES, MOST_BLOCKS, 8, TOK), f32),
            pltpu.VMEM((TILES, MOST_BLOCKS, 8, TOK), f32),
            pltpu.VMEM((FRAMES, BLK, HD), bf16),
            pltpu.VMEM((half, TOK, 2 * HD), bf16),
            pltpu.VMEM((half, TOK, 2 * HD), bf16),
            pltpu.VMEM((half, TOK, 2 * HD), f32),
            pltpu.VMEM((half, TOK, 2 * HD), bf16),
            pltpu.VMEM((UNITS // 2, TOK, 2 * HD), bf16),
            pltpu.VMEM((UNITS, BLK, HD), bf16),
            dma((3,)), dma((3,)), dma((3,)), dma((3,)),
            dma, dma((half,)), dma((half,)), dma, dma, dma,
            dma, dma((half,)),
            dma, dma, dma((LOCAL_HEADS,)), dma((LOCAL_HEADS,)),
        ],
        compiler_params=pltpu.CompilerParams(
            collective_id=0, has_side_effects=True, vmem_limit_bytes=VMEM_LIMIT
        ),
    )(window_offset, query_raw, key_raw, values, out_grad, query_gain, key_gain)
    return pl.pallas_call(
        finish_kernel,
        name="norm_grads",
        out_shape=(shape((TOK, LOCAL), bf16),) * 3,
        in_specs=[vmem] * 7,
        out_specs=[vmem] * 3,
    )(query_raw, key_raw, qgrad, kgrad, vgrad, total, inner)


def solution(mesh):
    placed = (
        P("frame", "head"),
        P("frame", "head"),
        P("frame", "head"),
        P("head"),
        P("head"),
        P("frame", "head"),
        P(),
    )
    return jax.shard_map(
        local,
        mesh=mesh,
        in_specs=placed,
        out_specs=(P("frame", "head"), P("frame", "head"), P("frame", "head")),
        check_vma=False,
    )
```
